512 devices in a mesh: dp: 64 (over z, y_hi, core), cls: 8 (over x, y_lo).
Axes of the slice: x: 4, y: 8 (y_hi: 4, y_lo: 2; y = y_hi * 2 + y_lo), z: 8, core: 2. Of those that a mesh axis runs over, the one named last changes fastest.
Arguments:
- features: bfloat16 [32768, 12544], P('dp', 'cls'), may hold values from -6 to 6
- fc_weight: bfloat16 [12544, 512], P('cls'), may hold values from -0.0546875 to 0.0546875
- class_weight: bfloat16 [4096, 512], P('cls'), may hold values from -0.29882812 to 0.29882812
- labels: int32 [32768], P('dp'), may hold values from 0 to 4095
Outputs:
- fc_grad: bfloat16 [12544, 512], P('cls')
- class_grad: bfloat16 [4096, 512], P('cls')
The draws below stay inside these ranges and needn't reach their ends.
All inputs are finite; a program needn't handle non-finite values.
Results may differ from the reference program's by a relative error of at most 0.024.
Values may be sent and summed in bfloat16 or wider, within the bound.
No kernel may reach another device: no remote copies, remote signals or barrier semaphores. Data moves between devices by JAX's collectives and lax.ppermute only.
A program may use at most 64 MiB of HBM per device.

```python
import math
import jax
import jax.numpy as jnp
from jax import lax

D = 512
FIN = 12544
FACES = 32768
CLASSES = 4096
N_CLS = 8


def touch_ends(entries, rng, least, high):
    spot = [jax.random.randint(jax.random.fold_in(rng, axis), (), 0, length) for axis, length in enumerate(entries.shape)]
    longest = entries.shape.index(max(entries.shape))
    next_to = spot[:longest] + [(spot[longest] + 1) % entries.shape[longest]] + spot[longest + 1:]
    return entries.at[tuple(spot)].set(least).at[tuple(next_to)].set(high)


def block_levels(rng, dims, cuts, least, high):
    def one(axis_at, shards_of):
        steps = jax.random.uniform(jax.random.fold_in(jax.random.fold_in(rng, 6), axis_at), (shards_of,), jnp.float32, least / len(cuts), high / len(cuts))
        return jnp.repeat(jnp.exp(steps), dims[axis_at] // shards_of).reshape((-1,) + (1,) * (len(dims) - axis_at - 1))

    gain = one(*cuts[0])
    for cut in cuts[1:]:
        gain = gain * one(*cut)
    return gain


def normal_values(key, extent, scale, limit, cuts=(), held_as=jnp.bfloat16):
    drawn = jax.random.normal(key, extent, jnp.float32) * scale
    if len(cuts) > 0:
        drawn = block_levels(key, extent, cuts, -0.22, 0.18) * drawn
    return jnp.clip(drawn, min=-limit, max=limit).astype(held_as)


def setup_inputs(seed: int = 0) -> dict:
    arg_keys = jax.random.split(jax.random.key(seed), 5)
    features = normal_values(arg_keys[0], (FACES, FIN), 1.0, 6.0, ((0, 64), (1, 8)))
    fc_weight = normal_values(arg_keys[1], (FIN, D), FIN ** -0.5, 0.0546875, ((0, 8),))
    class_weight = normal_values(arg_keys[2], (CLASSES, D), 0.05, 0.29882812, ((0, 8),))
    labels = touch_ends(jax.random.randint(arg_keys[3], (FACES,), 0, CLASSES), jax.random.fold_in(arg_keys[3], 1), 0, CLASSES - 1).astype(jnp.int32)
    return dict(features=features, fc_weight=fc_weight, class_weight=class_weight, labels=labels)


SCALE = 64.0
MARGIN = 0.5
SOFTEN = 0.01
EPSILON = 1e-06

def margin_terms(cosine, is_target):
    sine = jnp.sqrt(1.0 + SOFTEN - cosine * cosine)
    shifted = cosine * math.cos(MARGIN) - sine * math.sin(MARGIN)
    powers = jnp.exp(SCALE * jnp.where(is_target, shifted, cosine))
    slopes = SCALE * jnp.where(is_target, math.cos(MARGIN) + math.sin(MARGIN) * cosine / sine, 1.0)
    return (powers, slopes)

def softmax_grad(powers, totals, slopes, is_target, loss_weight):
    onehot = is_target.astype(jnp.float32)
    return ((powers / totals[:, None] - onehot) * loss_weight * slopes).astype(jnp.bfloat16)

def rounded_term(left, right):
    term = jnp.dot(left, right, preferred_element_type=jnp.float32).astype(jnp.bfloat16)
    term = lax.optimization_barrier(term)
    return term.astype(jnp.float32)

def reference(features, fc_weight, class_weight, labels):
    face_count = features.shape[0]
    block_width = features.shape[1] // N_CLS
    raw_embed = jnp.zeros((face_count, fc_weight.shape[1]), jnp.float32)
    for block in range(N_CLS):
        low = block * block_width
        raw_embed = raw_embed + rounded_term(features[:, low:low + block_width], fc_weight[low:low + block_width])
    embed_norm = jnp.sqrt(lax.optimization_barrier(jnp.sum(raw_embed * raw_embed, axis=1, keepdims=True)) + EPSILON)
    unit_f = raw_embed / embed_norm
    unit_embed = unit_f.astype(jnp.bfloat16)
    class_f = class_weight.astype(jnp.float32)
    class_norm = jnp.sqrt(lax.optimization_barrier(jnp.sum(class_f * class_f, axis=1, keepdims=True)) + EPSILON)
    class_unit_f = class_f / class_norm
    class_unit = class_unit_f.astype(jnp.bfloat16)
    cosine = lax.dot_general(unit_embed, class_unit, (((1,), (1,)), ((), ())), preferred_element_type=jnp.float32)
    columns = lax.broadcasted_iota(jnp.int32, cosine.shape, 1)
    is_target = columns == labels[:, None]
    powers, slopes = margin_terms(cosine, is_target)
    totals = lax.optimization_barrier(jnp.sum(powers, axis=1))
    loss_weight = 1.0 / math.sqrt(face_count)
    cos_grad = softmax_grad(powers, totals, slopes, is_target, loss_weight)
    class_block = class_weight.shape[0] // N_CLS
    unit_grad = jnp.zeros((face_count, class_weight.shape[1]), jnp.float32)
    for block in range(N_CLS):
        low = block * class_block
        unit_grad = unit_grad + rounded_term(cos_grad[:, low:low + class_block], class_unit[low:low + class_block])
    class_part = lax.dot_general(cos_grad, unit_embed, (((0,), (0,)), ((), ())), preferred_element_type=jnp.float32)
    raw_grad = ((unit_grad - unit_f * lax.optimization_barrier(jnp.sum(unit_f * unit_grad, axis=1, keepdims=True))) / embed_norm).astype(jnp.bfloat16)
    fc_grad = lax.dot_general(features, raw_grad, (((0,), (0,)), ((), ())), preferred_element_type=jnp.float32)
    class_grad = (class_part - class_unit_f * lax.optimization_barrier(jnp.sum(class_unit_f * class_part, axis=1, keepdims=True))) / class_norm
    return (fc_grad.astype(jnp.bfloat16), class_grad.astype(jnp.bfloat16))
```

```python
import math

import jax
import jax.numpy as jnp
from jax import lax
from jax.sharding import Mesh
from jax.sharding import PartitionSpec as P

SCALE = 64.0
MARGIN = 0.5
SOFTEN = 0.01
EPSILON = 1e-06

CLS = ("x", "yl")
CHIPS = ("z", "yh")
LANES = 128


def exchange(blocks, axes):
    return lax.all_to_all(blocks, axes, 0, 0, tiled=True)


def repeat_rows(block, count):
    return jnp.broadcast_to(block[None], (count,) + block.shape).reshape(
        (count * block.shape[0],) + block.shape[1:]
    )


def split_f32(value):
    high = lax.reduce_precision(value, 8, 7)
    rest = value - high
    mid = lax.reduce_precision(rest, 8, 7)
    low = rest - mid
    return [part.astype(jnp.bfloat16) for part in (high, mid, low)]


def packed(matrix, *columns):
    parts = [matrix]
    for column in columns:
        parts.extend(split_f32(column))
    parts.append(jnp.zeros((matrix.shape[0], LANES - 3 * len(columns)), jnp.bfloat16))
    return jnp.concatenate(parts, axis=1)


def unpacked(extra, which):
    low = 3 * which
    return jnp.sum(extra[:, low : low + 3].astype(jnp.float32), axis=1, keepdims=True)


def shards(features, fc_weight, class_weight, labels):
    faces = features.shape[0]
    classes, width = class_weight.shape
    n_cls = lax.axis_size(CLS)
    n_chips = lax.axis_size(CHIPS)
    loss_weight = 1.0 / math.sqrt(faces * n_chips * lax.axis_size("core"))
    position = lax.axis_index(CLS)

    class_f = class_weight.astype(jnp.float32)
    class_norm = jnp.sqrt(jnp.sum(class_f * class_f, axis=1, keepdims=True) + EPSILON)
    class_unit_f = class_f / class_norm
    class_unit = class_unit_f.astype(jnp.bfloat16)
    columns = position * classes + lax.broadcasted_iota(jnp.int32, (faces, classes), 1)
    is_target = columns == labels[:, None]

    raw_part = jnp.dot(features, fc_weight, preferred_element_type=jnp.float32)
    target_part = jnp.dot(
        is_target.astype(jnp.bfloat16), class_unit, preferred_element_type=jnp.float32
    )
    sent = jnp.concatenate([raw_part, target_part], axis=1).astype(jnp.bfloat16)
    got = exchange(sent, CLS).reshape(n_cls, faces // n_cls, 2 * width)
    got = jnp.sum(got.astype(jnp.float32), axis=0)
    raw_embed, target_unit = got[:, :width], got[:, width:]
    embed_norm = jnp.sqrt(jnp.sum(raw_embed * raw_embed, axis=1, keepdims=True) + EPSILON)
    unit_f = raw_embed / embed_norm
    unit = unit_f.astype(jnp.bfloat16)

    units = exchange(repeat_rows(unit, n_cls), CLS)
    cosine = lax.dot_general(
        units, class_unit, (((1,), (1,)), ((), ())), preferred_element_type=jnp.float32
    )
    others = jnp.where(is_target, 0.0, jnp.exp(SCALE * cosine))
    rest_part = jnp.sum(others, axis=1, keepdims=True)
    pull_part = jnp.dot(
        others.astype(jnp.bfloat16), class_unit, preferred_element_type=jnp.float32
    ).astype(jnp.bfloat16)
    got = exchange(packed(pull_part, rest_part), CLS).reshape(
        n_cls, faces // n_cls, width + LANES
    )
    got = jnp.sum(got.astype(jnp.float32), axis=0)
    pull, rest = got[:, :width], unpacked(got[:, width:], 0)

    cos_t = jnp.sum(
        unit.astype(jnp.float32) * target_unit, axis=1, keepdims=True
    )
    sine_t = jnp.sqrt(1.0 + SOFTEN - cos_t * cos_t)
    power_t = jnp.exp(SCALE * (cos_t * math.cos(MARGIN) - sine_t * math.sin(MARGIN)))
    slope_t = SCALE * (math.cos(MARGIN) + math.sin(MARGIN) * cos_t / sine_t)
    inverse = loss_weight / (rest + power_t)
    pull_scale = SCALE * inverse
    target_scale = rest * inverse * slope_t
    unit_grad = pull * pull_scale - target_unit * target_scale
    raw_grad = (
        (unit_grad - unit_f * jnp.sum(unit_f * unit_grad, axis=1, keepdims=True)) / embed_norm
    ).astype(jnp.bfloat16)

    got = exchange(repeat_rows(packed(raw_grad, pull_scale, target_scale), n_cls), CLS)
    raw_grads = got[:, :width]
    pull_scales, target_scales = unpacked(got[:, width:], 0), unpacked(got[:, width:], 1)
    cos_grad = jnp.where(is_target, -target_scales, others * pull_scales).astype(jnp.bfloat16)
    class_part = lax.dot_general(
        cos_grad, units, (((0,), (0,)), ((), ())), preferred_element_type=jnp.float32
    )
    class_part = (
        class_part - class_unit_f * jnp.sum(class_unit_f * class_part, axis=1, keepdims=True)
    ) / class_norm
    fc_part = lax.dot_general(
        features, raw_grads, (((0,), (0,)), ((), ())), preferred_element_type=jnp.float32
    )

    fc_rows = fc_part.shape[0]
    rows = fc_rows + classes
    groups = width // LANES
    piece = -(-rows * groups // (2 * n_chips * 8)) * 8
    half = piece * n_chips
    parts = jnp.concatenate([fc_part, class_part], axis=0)
    parts = parts.reshape(rows, groups, LANES).transpose(1, 0, 2).reshape(rows * groups, LANES)
    parts = jnp.pad(parts, ((0, 2 * half - rows * groups), (0, 0)))
    core = lax.axis_index("core")
    swap = [(0, 1), (1, 0)]
    mine = lax.dynamic_slice_in_dim(parts, core * half, half)
    theirs = lax.dynamic_slice_in_dim(parts, (1 - core) * half, half).astype(jnp.bfloat16)
    theirs = lax.ppermute(theirs, "core", swap)
    mine = (mine + theirs.astype(jnp.float32)).astype(jnp.bfloat16)
    got = exchange(mine, CHIPS).reshape(n_chips, piece, LANES)
    done = jnp.sum(got.astype(jnp.float32), axis=0).astype(jnp.bfloat16)
    mine = exchange(repeat_rows(done, n_chips), CHIPS)
    theirs = lax.ppermute(mine, "core", swap)
    first = jnp.where(core == 0, mine, theirs)
    second = jnp.where(core == 0, theirs, mine)
    whole = jnp.concatenate([first, second], axis=0)[: rows * groups]
    whole = whole.reshape(groups, rows, LANES).transpose(1, 0, 2).reshape(rows, width)
    return whole[:fc_rows], whole[fc_rows:]


def solution(mesh):
    fine = Mesh(mesh.devices.reshape(8, 4, 2, 4, 2), ("z", "yh", "core", "x", "yl"))
    dp = ("z", "yh", "core")
    placed = (P(dp, CLS), P(CLS, None), P(CLS, None), P(dp))
    return jax.shard_map(
        shards,
        mesh=fine,
        in_specs=placed,
        out_specs=(P(CLS, None), P(CLS, None)),
        check_vma=False,
    )
```

```python
import functools
import math

import jax
import jax.numpy as jnp
from jax import lax
from jax.experimental import pallas as pl
from jax.experimental.pallas import tpu as pltpu
from jax.sharding import Mesh
from jax.sharding import PartitionSpec as P

SCALE = 64.0
MARGIN = 0.5
SOFTEN = 0.01
EPSILON = 1e-06

CLS = ("x", "yl")
CHIPS = ("z", "yh")
LANES = 128
VMEM = pl.BlockSpec(memory_space=pltpu.VMEM)
SMEM = pl.BlockSpec(memory_space=pltpu.SMEM)


def exchange(blocks, axes):
    return lax.all_to_all(blocks, axes, 0, 0, tiled=True)


def across(left, right):
    return lax.dot_general(
        left, right, (((0,), (0,)), ((), ())), preferred_element_type=jnp.float32
    )


def row_norm(values):
    return jnp.sqrt(jnp.sum(values * values, axis=1, keepdims=True) + EPSILON)


def packed_columns(*columns):
    rows = columns[0].shape[0]
    lane = lax.broadcasted_iota(jnp.int32, (rows, LANES), 1)
    block = jnp.zeros((rows, LANES), jnp.float32)
    for at, column in enumerate(columns):
        rest = column
        for part in range(3):
            term = rest.astype(jnp.bfloat16).astype(jnp.float32)
            block = jnp.where(lane == 3 * at + part, term, block)
            rest = rest - term
    return block.astype(jnp.bfloat16)


def unpacked_column(block, at):
    lane = lax.broadcasted_iota(jnp.int32, block.shape, 1)
    inside = (lane >= 3 * at) & (lane < 3 * at + 3)
    return jnp.sum(jnp.where(inside, block, 0.0), axis=1, keepdims=True)


def embed_kernel(first_ref, features_ref, fc_ref, class_ref, labels_ref, sent_ref, unit_ref):
    width = fc_ref.shape[1]

    @pl.when(pl.program_id(0) == 0)
    def _():
        class_f = class_ref[...].astype(jnp.float32)
        unit_ref[...] = (class_f / row_norm(class_f)).astype(jnp.bfloat16)

    raw_part = jnp.dot(features_ref[...], fc_ref[...], preferred_element_type=jnp.float32)
    sent_ref[:, :width] = raw_part.astype(jnp.bfloat16)
    classes = unit_ref.shape[0]
    columns = first_ref[0] + lax.broadcasted_iota(
        jnp.int32, (features_ref.shape[0], classes), 1
    )
    chosen = jnp.where(columns == labels_ref[...], 1.0, 0.0).astype(jnp.bfloat16)
    target_part = jnp.dot(chosen, unit_ref[...], preferred_element_type=jnp.float32)
    sent_ref[:, width:] = target_part.astype(jnp.bfloat16)


def embed(first, features, fc_weight, class_weight, labels):
    faces, inputs = features.shape
    classes, width = class_weight.shape
    step = 128
    return pl.pallas_call(
        embed_kernel,
        grid=(faces // step,),
        in_specs=[
            SMEM,
            pl.BlockSpec((step, inputs), lambda i: (i, 0)),
            pl.BlockSpec((inputs, width), lambda i: (0, 0)),
            pl.BlockSpec((classes, width), lambda i: (0, 0)),
            pl.BlockSpec((step, 1), lambda i: (i, 0)),
        ],
        out_specs=[
            pl.BlockSpec((step, 2 * width), lambda i: (i, 0)),
            pl.BlockSpec((classes, width), lambda i: (0, 0)),
        ],
        out_shape=[
            jax.ShapeDtypeStruct((faces, 2 * width), jnp.bfloat16),
            jax.ShapeDtypeStruct((classes, width), jnp.bfloat16),
        ],
        name="embed",
    )(first, features, fc_weight, class_weight, labels)


def cosine_kernel(first_ref, units_ref, class_ref, labels_ref, pull_ref, others_ref):
    faces, width = units_ref.shape
    classes = class_ref.shape[0]
    step = 128
    for at in range(0, faces, step):
        here = slice(at, at + step)
        cosine = lax.dot_general(
            units_ref[here, :],
            class_ref[...],
            (((1,), (1,)), ((), ())),
            preferred_element_type=jnp.float32,
        )
        columns = first_ref[0] + lax.broadcasted_iota(jnp.int32, (step, classes), 1)
        is_target = columns == labels_ref[here, :]
        powers = jnp.exp(SCALE * cosine)
        others = jnp.where(is_target, 0.0, powers)
        others_ref[here, :] = jnp.where(is_target, -1.0, powers)
        pull = jnp.dot(
            others.astype(jnp.bfloat16), class_ref[...], preferred_element_type=jnp.float32
        )
        pull_ref[here, :width] = pull.astype(jnp.bfloat16)
        pull_ref[here, width:] = packed_columns(jnp.sum(others, axis=1, keepdims=True))


def cosines(first, units, class_unit, labels):
    faces, width = units.shape
    classes = class_unit.shape[0]
    return pl.pallas_call(
        cosine_kernel,
        in_specs=[SMEM, VMEM, VMEM, VMEM],
        out_specs=[VMEM, VMEM],
        out_shape=[
            jax.ShapeDtypeStruct((faces, width + LANES), jnp.bfloat16),
            jax.ShapeDtypeStruct((faces, classes), jnp.float32),
        ],
        name="cosines",
    )(first, units, class_unit, labels)


def raw_grad_kernel(loss_weight, pulls_ref, raw_ref, target_ref, sent_ref):
    width = raw_ref.shape[1]
    pulls = jnp.sum(pulls_ref[...].astype(jnp.float32), axis=0)
    pull, rest = pulls[:, :width], unpacked_column(pulls[:, width:], 0)
    raw_embed, target = raw_ref[...], target_ref[...]
    embed_norm = row_norm(raw_embed)
    unit_f = raw_embed / embed_norm
    unit = unit_f.astype(jnp.bfloat16).astype(jnp.float32)
    cos_t = jnp.sum(unit * target, axis=1, keepdims=True)
    sine_t = jnp.sqrt(1.0 + SOFTEN - cos_t * cos_t)
    power_t = jnp.exp(SCALE * (cos_t * math.cos(MARGIN) - sine_t * math.sin(MARGIN)))
    slope_t = SCALE * (math.cos(MARGIN) + math.sin(MARGIN) * cos_t / sine_t)
    inverse = loss_weight / (rest + power_t)
    pull_scale = SCALE * inverse
    target_scale = rest * inverse * slope_t
    unit_grad = pull * pull_scale - target * target_scale
    raw_grad = (
        unit_grad - unit_f * jnp.sum(unit_f * unit_grad, axis=1, keepdims=True)
    ) / embed_norm
    raw_grad = raw_grad.astype(jnp.bfloat16)
    scales = packed_columns(pull_scale, target_scale)
    for copy in range(sent_ref.shape[0]):
        sent_ref[copy, :, :width] = raw_grad
        sent_ref[copy, :, width:] = scales


def raw_grads(loss_weight, pulls, raw_embed, target_unit):
    return pl.pallas_call(
        functools.partial(raw_grad_kernel, loss_weight),
        in_specs=[VMEM, VMEM, VMEM],
        out_specs=VMEM,
        out_shape=jax.ShapeDtypeStruct(pulls.shape, jnp.bfloat16),
        name="raw_grads",
    )(pulls, raw_embed, target_unit)


def parts_kernel(
    half_ref, features_ref, grads_ref, units_ref, others_ref, class_ref, out_ref
):
    chips = out_ref.shape[0]
    classes, width = class_ref.shape
    groups = width // LANES
    inputs = features_ref.shape[1]
    rows = inputs // (2 * chips * 8) * 8
    main = 2 * chips * rows
    half = half_ref[0]
    grads = grads_ref[:, :width]
    some = chips // 2
    for at in range(0, chips, some):
        first = pl.multiple_of(half * (chips * rows) + at * rows, LANES)
        part = across(features_ref[:, pl.ds(first, some * rows)], grads)
        part = part.astype(out_ref.dtype).reshape(some, rows, width)
        for group in range(groups):
            out_ref[at : at + some, group * rows : (group + 1) * rows, :] = part[
                :, :, group * LANES : (group + 1) * LANES
            ]

    over = across(features_ref[:, main:], grads)
    each = over.shape[0] // 2
    over = jnp.where(half == 0, over[:each], over[each:]).astype(out_ref.dtype)
    base = groups * rows
    used = each // 8 * groups
    for tile in range(used):
        row, group = tile // groups * 8, tile % groups * LANES
        out_ref[tile, base + groups * 8 :, :] = over[row : row + 8, group : group + LANES]
    out_ref[used:, base + groups * 8 :, :] = jnp.zeros(
        (chips - used, 8, LANES), out_ref.dtype
    )

    scales = grads_ref[:, width:].astype(jnp.float32)
    pull_scale, target_scale = unpacked_column(scales, 0), unpacked_column(scales, 1)
    count = classes // 2
    first = pl.multiple_of(half * count, LANES)
    others = others_ref[:, pl.ds(first, count)]
    cos_grad = jnp.where(others < 0.0, -target_scale, others * pull_scale)
    part = across(cos_grad.astype(jnp.bfloat16), units_ref[...])
    class_f = class_ref[pl.ds(first, count), :].astype(jnp.float32)
    class_norm = row_norm(class_f)
    class_unit = class_f / class_norm
    part = (part - class_unit * jnp.sum(class_unit * part, axis=1, keepdims=True)) / class_norm
    part = part.astype(out_ref.dtype).reshape(chips, 8, width)
    for group in range(groups):
        out_ref[:, base + group * 8 : base + (group + 1) * 8, :] = part[
            :, :, group * LANES : (group + 1) * LANES
        ]


def parts(half, dtype, chips, features, grads, units, others, class_weight):
    groups = class_weight.shape[1] // LANES
    rows = features.shape[1] // (2 * chips * 8) * 8
    height = groups * rows + groups * 8 + 8
    return pl.pallas_call(
        parts_kernel,
        in_specs=[SMEM, VMEM, VMEM, VMEM, VMEM, VMEM],
        out_specs=VMEM,
        out_shape=jax.ShapeDtypeStruct((chips, height, LANES), dtype),
        name="parts",
    )(half, features, grads, units, others, class_weight)


def assemble_kernel(core_ref, mine_ref, theirs_ref, fc_ref, class_ref):
    chips = mine_ref.shape[0]
    inputs, width = fc_ref.shape
    groups = width // LANES
    rows = inputs // (2 * chips * 8) * 8
    main = 2 * chips * rows
    each = (inputs - main) // 2
    base = groups * rows
    count = class_ref.shape[0] // 2
    for source, half in ((mine_ref, core_ref[0]), (theirs_ref, 1 - core_ref[0])):
        for group in range(groups):
            lanes = slice(group * LANES, (group + 1) * LANES)
            block = source[:, group * rows : (group + 1) * rows, :].astype(jnp.float32)
            fc_ref[pl.ds(pl.multiple_of(half * (chips * rows), LANES), chips * rows), lanes] = (
                block.reshape(chips * rows, LANES).astype(jnp.bfloat16)
            )
            block = source[:, base + group * 8 : base + (group + 1) * 8, :].astype(jnp.float32)
            class_ref[pl.ds(pl.multiple_of(half * count, LANES), count), lanes] = (
                block.reshape(count, LANES).astype(jnp.bfloat16)
            )
            strips = each // 8
            block = jnp.concatenate(
                [source[strip * groups + group, base + groups * 8 :, :] for strip in range(strips)],
                axis=0,
            )
            fc_ref[pl.ds(pl.multiple_of(main + half * each, each), each), lanes] = block


def assemble(core, mine, theirs, inputs, classes, width):
    return pl.pallas_call(
        assemble_kernel,
        in_specs=[SMEM, VMEM, VMEM],
        out_specs=[VMEM, VMEM],
        out_shape=[
            jax.ShapeDtypeStruct((inputs, width), jnp.bfloat16),
            jax.ShapeDtypeStruct((classes, width), jnp.bfloat16),
        ],
        name="assemble",
    )(core, mine, theirs)


def shards(features, fc_weight, class_weight, labels):
    faces, inputs = features.shape
    classes, width = class_weight.shape
    n_cls = lax.axis_size(CLS)
    chips = lax.axis_size(CHIPS)
    loss_weight = 1.0 / math.sqrt(faces * chips * lax.axis_size("core"))
    first = (lax.axis_index(CLS) * classes).reshape(1)
    core = lax.axis_index("core").reshape(1)
    labels = labels.reshape(faces, 1)

    sent, class_unit = embed(first, features, fc_weight, class_weight, labels)
    got = exchange(sent, CLS).reshape(n_cls, faces // n_cls, 2 * width)
    got = jnp.sum(got.astype(jnp.float32), axis=0)
    raw_embed, target_unit = got[:, :width], got[:, width:]
    unit = (raw_embed / row_norm(raw_embed)).astype(jnp.bfloat16)
    units = exchange(jnp.broadcast_to(unit, (n_cls,) + unit.shape), CLS)
    units = units.reshape(faces, width)

    pull, others = cosines(first, units, class_unit, labels)
    got = exchange(pull, CLS).reshape(n_cls, faces // n_cls, width + LANES)
    sent = raw_grads(loss_weight, got, raw_embed, target_unit)
    grads = exchange(sent, CLS).reshape(faces, width + LANES)

    swap = [(0, 1), (1, 0)]
    operands = (features, grads, units, others, class_weight)
    theirs = lax.ppermute(parts(1 - core, jnp.bfloat16, chips, *operands), "core", swap)
    mine = parts(core, jnp.float32, chips, *operands)
    mine = (mine + theirs.astype(jnp.float32)).astype(jnp.bfloat16)
    done = jnp.sum(exchange(mine, CHIPS).astype(jnp.float32), axis=0).astype(jnp.bfloat16)
    mine = exchange(jnp.broadcast_to(done, (chips,) + done.shape), CHIPS)
    theirs = lax.ppermute(mine, "core", swap)
    return tuple(assemble(core, mine, theirs, inputs, classes, width))


def solution(mesh):
    fine = Mesh(mesh.devices.reshape(8, 4, 2, 4, 2), ("z", "yh", "core", "x", "yl"))
    dp = ("z", "yh", "core")
    placed = (P(dp, CLS), P(CLS, None), P(CLS, None), P(dp))
    return jax.shard_map(
        shards,
        mesh=fine,
        in_specs=placed,
        out_specs=(P(CLS, None), P(CLS, None)),
        check_vma=False,
    )
```

```python
import functools
import math

import jax
import jax.numpy as jnp
from jax import lax
from jax.experimental import pallas as pl
from jax.experimental.pallas import tpu as pltpu
from jax.sharding import Mesh
from jax.sharding import PartitionSpec as P

SCALE = 64.0
MARGIN = 0.5
SOFTEN = 0.01
EPSILON = 1e-06

CLS = ("x", "yl")
CHIPS = ("z", "yh")
LANES = 128
CHUNKS = 3
LIMIT = 24 << 20
VMEM = pl.BlockSpec(memory_space=pltpu.VMEM)
SMEM = pl.BlockSpec(memory_space=pltpu.SMEM)


def exchange(blocks, axes):
    return lax.all_to_all(blocks, axes, 0, 0, tiled=True)


def across(left, right):
    return lax.dot_general(
        left, right, (((0,), (0,)), ((), ())), preferred_element_type=jnp.float32
    )


def row_norm(values):
    return jnp.sqrt(jnp.sum(values * values, axis=1, keepdims=True) + EPSILON)


def packed_columns(*columns):
    rows = columns[0].shape[0]
    lane = lax.broadcasted_iota(jnp.int32, (rows, LANES), 1)
    block = jnp.zeros((rows, LANES), jnp.float32)
    for at, column in enumerate(columns):
        rest = column
        for part in range(3):
            term = rest.astype(jnp.bfloat16).astype(jnp.float32)
            block = jnp.where(lane == 3 * at + part, term, block)
            rest = rest - term
    return block.astype(jnp.bfloat16)


def unpacked_column(block, at):
    lane = lax.broadcasted_iota(jnp.int32, block.shape, 1)
    inside = (lane >= 3 * at) & (lane < 3 * at + 3)
    return jnp.sum(jnp.where(inside, block, 0.0), axis=1, keepdims=True)


def placed(array, space=pltpu.VMEM):
    return pltpu.with_memory_space_constraint(array, space)


def half_of(place_ref, other):
    core = lax.rem(place_ref[0], 2)
    return 1 - core if other else core


def first_of(place_ref, classes):
    return lax.div(place_ref[0], 2) * classes


def call(kernel, name, operands, results, **options):
    specs = [SMEM if operand.ndim == 1 else VMEM for operand in operands]
    operands = [operand if operand.ndim == 1 else placed(operand) for operand in operands]
    return pl.pallas_call(
        kernel,
        in_specs=specs,
        out_specs=[VMEM] * len(results),
        out_shape=[pltpu.VMEM(shape, dtype) for shape, dtype in results],
        compiler_params=pltpu.CompilerParams(vmem_limit_bytes=LIMIT),
        name=name,
        **options,
    )(*operands)


def target_mask(first, labels, rows, classes):
    lane = lax.broadcasted_iota(jnp.int32, (rows, LANES), 1)
    return jnp.concatenate(
        [labels == lane + (first + at) for at in range(0, classes, LANES)], axis=1
    )


def spread_labels(labels_row):
    faces = labels_row.shape[1]
    return jnp.transpose(jnp.broadcast_to(labels_row, (LANES, faces)))


def embed_kernel(
    place_ref, features_ref, fc_ref, class_ref, labels_ref, sent_ref, unit_ref,
    left_ref, right_ref, total_ref, left_sem, right_sem
):
    width = fc_ref.shape[1]
    inputs, faces = features_ref.shape
    classes = class_ref.shape[0]
    ends = [inputs * at // CHUNKS // LANES * LANES for at in range(CHUNKS)] + [inputs]
    copies = []
    for at in range(CHUNKS):
        rows = pl.ds(ends[at], ends[at + 1] - ends[at])
        pair = (
            pltpu.make_async_copy(features_ref.at[rows, :], left_ref.at[rows, :], left_sem.at[at]),
            pltpu.make_async_copy(fc_ref.at[rows, :], right_ref.at[rows, :], right_sem.at[at]),
        )
        for copy in pair:
            copy.start()
        copies.append(pair)

    class_f = class_ref[...].astype(jnp.float32)
    unit_ref[...] = (class_f / row_norm(class_f)).astype(jnp.bfloat16)
    labels = spread_labels(labels_ref[...])
    chosen = target_mask(first_of(place_ref, classes), labels, faces, classes)
    chosen = jnp.where(chosen, 1.0, 0.0).astype(jnp.bfloat16)
    target_part = jnp.dot(chosen, unit_ref[...], preferred_element_type=jnp.float32)
    sent_ref[:, width:] = target_part.astype(jnp.bfloat16)

    for at in range(CHUNKS):
        for copy in copies[at]:
            copy.wait()
        here = slice(ends[at], ends[at + 1])
        part = across(left_ref[here, :], right_ref[here, :])
        if at > 0:
            part = part + total_ref[...]
        if at < CHUNKS - 1:
            total_ref[...] = part
        else:
            sent_ref[:, :width] = part.astype(jnp.bfloat16)


def embed(place, features, fc_weight, class_weight, labels):
    inputs, faces = features.shape
    classes, width = class_weight.shape
    anywhere = pl.BlockSpec(memory_space=pltpu.HBM)
    return pl.pallas_call(
        embed_kernel,
        in_specs=[SMEM, anywhere, anywhere, VMEM, VMEM],
        out_specs=[VMEM, VMEM],
        out_shape=[
            pltpu.VMEM((faces, 2 * width), jnp.bfloat16),
            pltpu.VMEM((classes, width), jnp.bfloat16),
        ],
        scratch_shapes=[
            pltpu.VMEM((inputs, faces), jnp.bfloat16),
            pltpu.VMEM((inputs, width), jnp.bfloat16),
            pltpu.VMEM((faces, width), jnp.float32),
            pltpu.SemaphoreType.DMA((CHUNKS,)),
            pltpu.SemaphoreType.DMA((CHUNKS,)),
        ],
        compiler_params=pltpu.CompilerParams(vmem_limit_bytes=LIMIT),
        name="embed",
    )(
        place,
        placed(features, pltpu.HBM),
        placed(fc_weight, pltpu.HBM),
        placed(class_weight),
        placed(labels),
    )


def cosine_kernel(place_ref, units_ref, class_ref, labels_ref, pull_ref, others_ref):
    faces, width = units_ref.shape
    classes = class_ref.shape[0]
    step = 128
    labels = spread_labels(labels_ref[...])
    for at in range(0, faces, step):
        here = slice(at, at + step)
        cosine = lax.dot_general(
            units_ref[here, :],
            class_ref[...],
            (((1,), (1,)), ((), ())),
            preferred_element_type=jnp.float32,
        )
        is_target = target_mask(first_of(place_ref, classes), labels[here, :], step, classes)
        powers = jnp.exp(SCALE * cosine)
        others = jnp.where(is_target, 0.0, powers)
        others_ref[here, :] = jnp.where(is_target, -1.0, powers)
        pull = jnp.dot(
            others.astype(jnp.bfloat16), class_ref[...], preferred_element_type=jnp.float32
        )
        pull_ref[here, :width] = pull.astype(jnp.bfloat16)
        pull_ref[here, width:] = packed_columns(jnp.sum(others, axis=1, keepdims=True))


def cosines(place, units, class_unit, labels):
    faces, width = units.shape
    classes = class_unit.shape[0]
    return call(
        cosine_kernel,
        "cosines",
        (place, units, class_unit, labels),
        [((faces, width + LANES), jnp.bfloat16), ((faces, classes), jnp.float32)],
    )


def raw_grad_kernel(loss_weight, pulls_ref, raw_ref, target_ref, sent_ref):
    width = raw_ref.shape[1]
    pulls = jnp.sum(pulls_ref[...].astype(jnp.float32), axis=0)
    pull, rest = pulls[:, :width], unpacked_column(pulls[:, width:], 0)
    raw_embed, target = raw_ref[...], target_ref[...]
    embed_norm = row_norm(raw_embed)
    unit_f = raw_embed / embed_norm
    unit = unit_f.astype(jnp.bfloat16).astype(jnp.float32)
    cos_t = jnp.sum(unit * target, axis=1, keepdims=True)
    sine_t = jnp.sqrt(1.0 + SOFTEN - cos_t * cos_t)
    power_t = jnp.exp(SCALE * (cos_t * math.cos(MARGIN) - sine_t * math.sin(MARGIN)))
    slope_t = SCALE * (math.cos(MARGIN) + math.sin(MARGIN) * cos_t / sine_t)
    inverse = loss_weight / (rest + power_t)
    pull_scale = SCALE * inverse
    target_scale = rest * inverse * slope_t
    unit_grad = pull * pull_scale - target * target_scale
    raw_grad = (
        unit_grad - unit_f * jnp.sum(unit_f * unit_grad, axis=1, keepdims=True)
    ) / embed_norm
    raw_grad = raw_grad.astype(jnp.bfloat16)
    scales = packed_columns(pull_scale, target_scale)
    for copy in range(sent_ref.shape[0]):
        sent_ref[copy, :, :width] = raw_grad
        sent_ref[copy, :, width:] = scales


def raw_grads(loss_weight, pulls, raw_embed, target_unit):
    return call(
        functools.partial(raw_grad_kernel, loss_weight),
        "raw_grads",
        (pulls, raw_embed, target_unit),
        [(pulls.shape, jnp.bfloat16)],
    )[0]


def parts_kernel(
    other, place_ref, features_ref, grads_ref, units_ref, others_ref, class_ref, out_ref
):
    chips = out_ref.shape[0]
    classes, width = class_ref.shape
    groups = width // LANES
    inputs = features_ref.shape[0]
    rows = inputs // (2 * chips * 8) * 8
    main = 2 * chips * rows
    half = half_of(place_ref, other)
    grads = grads_ref[:, :width]
    some = chips // 2
    for at in range(0, chips, some):
        first = pl.multiple_of(half * (chips * rows) + at * rows, LANES)
        part = jnp.dot(
            features_ref[pl.ds(first, some * rows), :], grads, preferred_element_type=jnp.float32
        )
        part = part.astype(out_ref.dtype).reshape(some, rows, width)
        for group in range(groups):
            out_ref[at : at + some, group * rows : (group + 1) * rows, :] = part[
                :, :, group * LANES : (group + 1) * LANES
            ]

    each = (inputs - main) // 2
    over = jnp.dot(
        features_ref[pl.ds(pl.multiple_of(main + half * each, each), each), :],
        grads,
        preferred_element_type=jnp.float32,
    ).astype(out_ref.dtype)
    base = groups * rows
    used = each // 8 * groups
    for tile in range(used):
        row, group = tile // groups * 8, tile % groups * LANES
        out_ref[tile, base + groups * 8 :, :] = over[row : row + 8, group : group + LANES]
    out_ref[used:, base + groups * 8 :, :] = jnp.zeros(
        (chips - used, 8, LANES), out_ref.dtype
    )

    scales = grads_ref[:, width:].astype(jnp.float32)
    pull_scale, target_scale = unpacked_column(scales, 0), unpacked_column(scales, 1)
    count = classes // 2
    first = pl.multiple_of(half * count, LANES)
    others = others_ref[:, pl.ds(first, count)]
    cos_grad = jnp.where(others < 0.0, -target_scale, others * pull_scale)
    part = across(cos_grad.astype(jnp.bfloat16), units_ref[...])
    class_f = class_ref[pl.ds(first, count), :].astype(jnp.float32)
    class_norm = row_norm(class_f)
    class_unit = class_f / class_norm
    part = (part - class_unit * jnp.sum(class_unit * part, axis=1, keepdims=True)) / class_norm
    part = part.astype(out_ref.dtype).reshape(chips, 8, width)
    for group in range(groups):
        out_ref[:, base + group * 8 : base + (group + 1) * 8, :] = part[
            :, :, group * LANES : (group + 1) * LANES
        ]


def parts(other, place, dtype, chips, features, grads, units, others, class_weight):
    groups = class_weight.shape[1] // LANES
    rows = features.shape[0] // (2 * chips * 8) * 8
    height = groups * rows + groups * 8 + 8
    return call(
        functools.partial(parts_kernel, other),
        "parts",
        (place, features, grads, units, others, class_weight),
        [((chips, height, LANES), dtype)],
    )[0]


def assemble_kernel(other, place_ref, source_ref, *refs):
    fc_ref, class_ref, fc_half, fc_over, class_half, sems = refs[-6:]
    chips = source_ref.shape[0]
    inputs, width = fc_ref.shape
    groups = width // LANES
    rows = inputs // (2 * chips * 8) * 8
    main = 2 * chips * rows
    each = (inputs - main) // 2
    base = groups * rows
    count = class_ref.shape[0] // 2
    half = half_of(place_ref, other)

    for group in range(groups):
        lanes = slice(group * LANES, (group + 1) * LANES)
        block = source_ref[:, base + group * 8 : base + (group + 1) * 8, :].astype(jnp.float32)
        class_half[:, lanes] = block.reshape(count, LANES).astype(jnp.bfloat16)
        for strip in range(each // 8):
            fc_over[strip * 8 : strip * 8 + 8, lanes] = source_ref[
                strip * groups + group, base + groups * 8 :, :
            ]
    copies = [
        pltpu.make_async_copy(
            class_half, class_ref.at[pl.ds(pl.multiple_of(half * count, count), count), :], sems.at[0]
        ),
        pltpu.make_async_copy(
            fc_over, fc_ref.at[pl.ds(pl.multiple_of(main + half * each, each), each), :], sems.at[1]
        ),
    ]
    for copy in copies:
        copy.start()
    some = chips // 4
    for at in range(0, chips, some):
        for group in range(groups):
            lanes = slice(group * LANES, (group + 1) * LANES)
            block = source_ref[at : at + some, group * rows : (group + 1) * rows, :]
            block = block.astype(jnp.float32).reshape(some * rows, LANES)
            fc_half[at * rows : (at + some) * rows, lanes] = block.astype(jnp.bfloat16)
        first = pl.multiple_of(half * (chips * rows) + at * rows, some * rows)
        copies.append(
            pltpu.make_async_copy(
                fc_half.at[at * rows : (at + some) * rows, :],
                fc_ref.at[pl.ds(first, some * rows), :],
                sems.at[2 + at // some],
            )
        )
        copies[-1].start()
    for copy in copies:
        copy.wait()


def assemble(other, place, source, inputs, classes, width, *into):
    chips = source.shape[0]
    groups = width // LANES
    rows = inputs // (2 * chips * 8) * 8
    each = (inputs - 2 * chips * rows) // 2
    anywhere = pl.BlockSpec(memory_space=pltpu.HBM)
    return pl.pallas_call(
        functools.partial(assemble_kernel, other),
        in_specs=[SMEM, VMEM] + [anywhere] * len(into),
        out_specs=[anywhere, anywhere],
        out_shape=[
            jax.ShapeDtypeStruct((inputs, width), jnp.bfloat16),
            jax.ShapeDtypeStruct((classes, width), jnp.bfloat16),
        ],
        scratch_shapes=[
            pltpu.VMEM((chips * rows, width), jnp.bfloat16),
            pltpu.VMEM((each, width), jnp.bfloat16),
            pltpu.VMEM((classes // 2, width), jnp.bfloat16),
            pltpu.SemaphoreType.DMA((6,)),
        ],
        input_output_aliases={2 + at: at for at in range(len(into))},
        compiler_params=pltpu.CompilerParams(vmem_limit_bytes=LIMIT),
        name="assemble",
    )(place, placed(source), *into)


def shards(features, fc_weight, class_weight, labels):
    faces, inputs = features.shape
    features = features.T
    classes, width = class_weight.shape
    n_cls = lax.axis_size(CLS)
    chips = lax.axis_size(CHIPS)
    loss_weight = 1.0 / math.sqrt(faces * chips * lax.axis_size("core"))
    place = (lax.axis_index(CLS) * 2 + lax.axis_index("core")).reshape(1)
    labels = labels.reshape(1, faces)

    sent, class_unit = embed(place, features, fc_weight, class_weight, labels)
    got = exchange(sent, CLS).reshape(n_cls, faces // n_cls, 2 * width)
    got = jnp.sum(got.astype(jnp.float32), axis=0)
    raw_embed, target_unit = got[:, :width], got[:, width:]
    unit = (raw_embed / row_norm(raw_embed)).astype(jnp.bfloat16)
    units = exchange(jnp.broadcast_to(unit, (n_cls,) + unit.shape), CLS)
    units = units.reshape(faces, width)

    pull, others = cosines(place, units, class_unit, labels)
    got = exchange(pull, CLS).reshape(n_cls, faces // n_cls, width + LANES)
    sent = raw_grads(loss_weight, got, raw_embed, target_unit)
    grads = exchange(sent, CLS).reshape(faces, width + LANES)

    swap = [(0, 1), (1, 0)]
    operands = (features, grads, units, others, class_weight)
    theirs = lax.ppermute(parts(True, place, jnp.bfloat16, chips, *operands), "core", swap)
    mine = parts(False, place, jnp.float32, chips, *operands)
    mine = (mine + theirs.astype(jnp.float32)).astype(jnp.bfloat16)
    done = jnp.sum(exchange(mine, CHIPS).astype(jnp.float32), axis=0).astype(jnp.bfloat16)
    mine = exchange(jnp.broadcast_to(done, (chips,) + done.shape), CHIPS)
    theirs = lax.ppermute(mine, "core", swap)
    sizes = (inputs, classes, width)
    written = assemble(False, place, mine, *sizes)
    return tuple(assemble(True, place, theirs, *sizes, *written))


def solution(mesh):
    fine = Mesh(mesh.devices.reshape(8, 4, 2, 4, 2), ("z", "yh", "core", "x", "yl"))
    dp = ("z", "yh", "core")
    specs = (P(dp, CLS), P(CLS, None), P(CLS, None), P(dp))
    return jax.shard_map(
        shards,
        mesh=fine,
        in_specs=specs,
        out_specs=(P(CLS, None), P(CLS, None)),
        check_vma=False,
    )
```

```python
import functools
import math

import jax
import jax.numpy as jnp
from jax import lax
from jax.experimental import pallas as pl
from jax.experimental.pallas import tpu as pltpu
from jax.sharding import Mesh
from jax.sharding import PartitionSpec as P

SCALE = 64.0
MARGIN = 0.5
SOFTEN = 0.01
EPSILON = 1e-06

CLS = ("x", "yl")
CHIPS = ("zh", "yh")
LANES = 128
CHUNKS = 3
LIMIT = 24 << 20
VMEM = pl.BlockSpec(memory_space=pltpu.VMEM)
SMEM = pl.BlockSpec(memory_space=pltpu.SMEM)


def exchange(blocks, axes):
    return lax.all_to_all(blocks, axes, 0, 0, tiled=True)


def across(left, right):
    return lax.dot_general(
        left, right, (((0,), (0,)), ((), ())), preferred_element_type=jnp.float32
    )


def row_norm(values):
    return jnp.sqrt(jnp.sum(values * values, axis=1, keepdims=True) + EPSILON)


def packed_columns(*columns):
    rows = columns[0].shape[0]
    lane = lax.broadcasted_iota(jnp.int32, (rows, LANES), 1)
    block = jnp.zeros((rows, LANES), jnp.float32)
    for at, column in enumerate(columns):
        rest = column
        for part in range(3):
            term = rest.astype(jnp.bfloat16).astype(jnp.float32)
            block = jnp.where(lane == 3 * at + part, term, block)
            rest = rest - term
    return block.astype(jnp.bfloat16)


def unpacked_column(block, at):
    lane = lax.broadcasted_iota(jnp.int32, block.shape, 1)
    inside = (lane >= 3 * at) & (lane < 3 * at + 3)
    return jnp.sum(jnp.where(inside, block, 0.0), axis=1, keepdims=True)


def placed(array, space=pltpu.VMEM):
    return pltpu.with_memory_space_constraint(array, space)


def half_of(place_ref, other):
    core = lax.rem(place_ref[0], 2)
    return 1 - core if other else core


def parity_of(place_ref, other):
    odd = lax.rem(lax.div(place_ref[0], 2), 2)
    return 1 - odd if other else odd


def first_of(place_ref, classes):
    return lax.div(place_ref[0], 4) * classes


def call(kernel, name, operands, results, **options):
    specs = [SMEM if operand.ndim == 1 else VMEM for operand in operands]
    operands = [operand if operand.ndim == 1 else placed(operand) for operand in operands]
    return pl.pallas_call(
        kernel,
        in_specs=specs,
        out_specs=[VMEM] * len(results),
        out_shape=[pltpu.VMEM(shape, dtype) for shape, dtype in results],
        compiler_params=pltpu.CompilerParams(vmem_limit_bytes=LIMIT),
        name=name,
        **options,
    )(*operands)


def target_mask(first, labels, rows, classes):
    lane = lax.broadcasted_iota(jnp.int32, (rows, LANES), 1)
    return jnp.concatenate(
        [labels == lane + (first + at) for at in range(0, classes, LANES)], axis=1
    )


def spread_labels(labels_row):
    faces = labels_row.shape[1]
    return jnp.transpose(jnp.broadcast_to(labels_row, (LANES, faces)))


def embed_kernel(
    place_ref, features_ref, fc_ref, class_ref, labels_ref, sent_ref, unit_ref,
    left_ref, right_ref, total_ref, left_sem, right_sem
):
    width = fc_ref.shape[1]
    inputs, faces = features_ref.shape
    classes = class_ref.shape[0]
    ends = [inputs * at // CHUNKS // LANES * LANES for at in range(CHUNKS)] + [inputs]
    copies = []
    for at in range(CHUNKS):
        rows = pl.ds(ends[at], ends[at + 1] - ends[at])
        pair = (
            pltpu.make_async_copy(features_ref.at[rows, :], left_ref.at[rows, :], left_sem.at[at]),
            pltpu.make_async_copy(fc_ref.at[rows, :], right_ref.at[rows, :], right_sem.at[at]),
        )
        for copy in pair:
            copy.start()
        copies.append(pair)

    class_f = class_ref[...].astype(jnp.float32)
    unit_ref[...] = (class_f / row_norm(class_f)).astype(jnp.bfloat16)
    labels = spread_labels(labels_ref[...])
    chosen = target_mask(first_of(place_ref, classes), labels, faces, classes)
    chosen = jnp.where(chosen, 1.0, 0.0).astype(jnp.bfloat16)
    target_part = jnp.dot(chosen, unit_ref[...], preferred_element_type=jnp.float32)
    sent_ref[:, width:] = target_part.astype(jnp.bfloat16)

    for at in range(CHUNKS):
        for copy in copies[at]:
            copy.wait()
        here = slice(ends[at], ends[at + 1])
        part = across(left_ref[here, :], right_ref[here, :])
        if at > 0:
            part = part + total_ref[...]
        if at < CHUNKS - 1:
            total_ref[...] = part
        else:
            sent_ref[:, :width] = part.astype(jnp.bfloat16)


def embed(place, features, fc_weight, class_weight, labels):
    inputs, faces = features.shape
    classes, width = class_weight.shape
    anywhere = pl.BlockSpec(memory_space=pltpu.HBM)
    return pl.pallas_call(
        embed_kernel,
        in_specs=[SMEM, anywhere, anywhere, VMEM, VMEM],
        out_specs=[VMEM, VMEM],
        out_shape=[
            pltpu.VMEM((faces, 2 * width), jnp.bfloat16),
            pltpu.VMEM((classes, width), jnp.bfloat16),
        ],
        scratch_shapes=[
            pltpu.VMEM((inputs, faces), jnp.bfloat16),
            pltpu.VMEM((inputs, width), jnp.bfloat16),
            pltpu.VMEM((faces, width), jnp.float32),
            pltpu.SemaphoreType.DMA((CHUNKS,)),
            pltpu.SemaphoreType.DMA((CHUNKS,)),
        ],
        compiler_params=pltpu.CompilerParams(vmem_limit_bytes=LIMIT),
        name="embed",
    )(
        place,
        placed(features, pltpu.HBM),
        placed(fc_weight, pltpu.HBM),
        placed(class_weight),
        placed(labels),
    )


def cosine_kernel(place_ref, units_ref, class_ref, labels_ref, pull_ref, others_ref):
    faces, width = units_ref.shape
    classes = class_ref.shape[0]
    step = 128
    labels = spread_labels(labels_ref[...])
    for at in range(0, faces, step):
        here = slice(at, at + step)
        cosine = lax.dot_general(
            units_ref[here, :],
            class_ref[...],
            (((1,), (1,)), ((), ())),
            preferred_element_type=jnp.float32,
        )
        is_target = target_mask(first_of(place_ref, classes), labels[here, :], step, classes)
        powers = jnp.exp(SCALE * cosine)
        others = jnp.where(is_target, 0.0, powers)
        others_ref[here, :] = jnp.where(is_target, -1.0, powers)
        pull = jnp.dot(
            others.astype(jnp.bfloat16), class_ref[...], preferred_element_type=jnp.float32
        )
        pull_ref[here, :width] = pull.astype(jnp.bfloat16)
        pull_ref[here, width:] = packed_columns(jnp.sum(others, axis=1, keepdims=True))


def cosines(place, units, class_unit, labels):
    faces, width = units.shape
    classes = class_unit.shape[0]
    return call(
        cosine_kernel,
        "cosines",
        (place, units, class_unit, labels),
        [((faces, width + LANES), jnp.bfloat16), ((faces, classes), jnp.float32)],
    )


def raw_grad_kernel(loss_weight, pulls_ref, raw_ref, target_ref, sent_ref):
    width = raw_ref.shape[1]
    pulls = jnp.sum(pulls_ref[...].astype(jnp.float32), axis=0)
    pull, rest = pulls[:, :width], unpacked_column(pulls[:, width:], 0)
    raw_embed, target = raw_ref[...], target_ref[...]
    embed_norm = row_norm(raw_embed)
    unit_f = raw_embed / embed_norm
    unit = unit_f.astype(jnp.bfloat16).astype(jnp.float32)
    cos_t = jnp.sum(unit * target, axis=1, keepdims=True)
    sine_t = jnp.sqrt(1.0 + SOFTEN - cos_t * cos_t)
    power_t = jnp.exp(SCALE * (cos_t * math.cos(MARGIN) - sine_t * math.sin(MARGIN)))
    slope_t = SCALE * (math.cos(MARGIN) + math.sin(MARGIN) * cos_t / sine_t)
    inverse = loss_weight / (rest + power_t)
    pull_scale = SCALE * inverse
    target_scale = rest * inverse * slope_t
    unit_grad = pull * pull_scale - target * target_scale
    raw_grad = (
        unit_grad - unit_f * jnp.sum(unit_f * unit_grad, axis=1, keepdims=True)
    ) / embed_norm
    raw_grad = raw_grad.astype(jnp.bfloat16)
    scales = packed_columns(pull_scale, target_scale)
    for copy in range(sent_ref.shape[0]):
        sent_ref[copy, :, :width] = raw_grad
        sent_ref[copy, :, width:] = scales


def raw_grads(loss_weight, pulls, raw_embed, target_unit):
    return call(
        functools.partial(raw_grad_kernel, loss_weight),
        "raw_grads",
        (pulls, raw_embed, target_unit),
        [(pulls.shape, jnp.bfloat16)],
    )[0]


def block_sizes(inputs, width, blocks):
    rows = inputs // (2 * blocks * 8) * 8
    return rows, width // LANES, 2 * blocks * rows


def parts_kernel(
    other, place_ref, features_ref, grads_ref, units_ref, others_ref, class_ref, out_ref
):
    blocks = out_ref.shape[0]
    some = blocks // 2
    classes, width = class_ref.shape
    inputs = features_ref.shape[0]
    rows, groups, main = block_sizes(inputs, width, blocks)
    base = groups * rows
    half = half_of(place_ref, other)
    grads = grads_ref[:, :width]
    scales = grads_ref[:, width:].astype(jnp.float32)
    pull_scale, target_scale = unpacked_column(scales, 0), unpacked_column(scales, 1)
    each = (inputs - main) // 2
    over = jnp.dot(
        features_ref[pl.ds(pl.multiple_of(main + half * each, each), each), :],
        grads,
        preferred_element_type=jnp.float32,
    ).astype(out_ref.dtype)
    count = classes // 4

    for at, parity in ((0, parity_of(place_ref, True)), (some, parity_of(place_ref, False))):
        here = slice(at, at + some)
        first = pl.multiple_of((2 * half + parity) * (some * rows), LANES)
        part = jnp.dot(
            features_ref[pl.ds(first, some * rows), :], grads, preferred_element_type=jnp.float32
        )
        part = part.astype(out_ref.dtype).reshape(some, rows, width)
        for group in range(groups):
            out_ref[here, group * rows : (group + 1) * rows, :] = part[
                :, :, group * LANES : (group + 1) * LANES
            ]

        first = pl.multiple_of((2 * half + parity) * count, LANES)
        others = others_ref[:, pl.ds(first, count)]
        cos_grad = jnp.where(others < 0.0, -target_scale, others * pull_scale)
        part = across(cos_grad.astype(jnp.bfloat16), units_ref[...])
        class_f = class_ref[pl.ds(first, count), :].astype(jnp.float32)
        class_norm = row_norm(class_f)
        class_unit = class_f / class_norm
        part = part - class_unit * jnp.sum(class_unit * part, axis=1, keepdims=True)
        part = (part / class_norm).astype(out_ref.dtype).reshape(some, 8, width)
        for group in range(groups):
            out_ref[here, base + group * 8 : base + (group + 1) * 8, :] = part[
                :, :, group * LANES : (group + 1) * LANES
            ]

        strip = jnp.where(parity == 0, over[:8], over[8:])
        for group in range(groups):
            out_ref[at + group, base + groups * 8 :, :] = strip[
                :, group * LANES : (group + 1) * LANES
            ]
        out_ref[at + groups : at + some, base + groups * 8 :, :] = jnp.zeros(
            (some - groups, 8, LANES), out_ref.dtype
        )


def parts(other, place, dtype, blocks, features, grads, units, others, class_weight):
    rows, groups, _ = block_sizes(features.shape[0], class_weight.shape[1], blocks)
    return call(
        functools.partial(parts_kernel, other),
        "parts",
        (place, features, grads, units, others, class_weight),
        [((blocks, groups * (rows + 8) + 8, LANES), dtype)],
    )[0]


def assemble_kernel(pieces, blocks, place_ref, *refs):
    sources = refs[: len(pieces)]
    fc_ref, class_ref, fc_rows, class_rows, over_rows, sems = refs[-6:]
    inputs, width = fc_ref.shape
    rows, groups, main = block_sizes(inputs, width, blocks)
    each = (inputs - main) // 2
    base = groups * rows
    some = blocks // 2
    copies = []
    done = 0

    def send(source, target, at, size):
        copies.append(
            pltpu.make_async_copy(
                source, target.at[pl.ds(pl.multiple_of(at, 8), size), :], sems.at[len(copies)]
            )
        )
        copies[-1].start()

    for number, (piece, source) in enumerate(zip(pieces, sources)):
        other_half, other_parity, start = piece
        half, parity = half_of(place_ref, other_half), parity_of(place_ref, other_parity)
        count = source.shape[0]
        block = (2 * half + parity) * some + start
        fc_here = slice(done * rows, (done + count) * rows)
        class_here = slice(done * 8, (done + count) * 8)
        for group in range(groups):
            lanes = slice(group * LANES, (group + 1) * LANES)
            values = source[:, group * rows : (group + 1) * rows, :].astype(jnp.float32)
            fc_rows[fc_here, lanes] = values.reshape(count * rows, LANES).astype(jnp.bfloat16)
            values = source[:, base + group * 8 : base + (group + 1) * 8, :].astype(jnp.float32)
            class_rows[class_here, lanes] = values.reshape(count * 8, LANES).astype(jnp.bfloat16)
            if start == 0:
                over_rows[number, :, lanes] = source[group, base + groups * 8 :, :]
        send(fc_rows.at[fc_here, :], fc_ref, block * rows, count * rows)
        send(class_rows.at[class_here, :], class_ref, block * 8, count * 8)
        if start == 0:
            send(over_rows.at[number], fc_ref, main + half * each + parity * 8, 8)
        done += count
    for copy in copies:
        copy.wait()


def assemble(place, blocks, sizes, pieces, into):
    inputs, classes, width = sizes
    rows, _, _ = block_sizes(inputs, width, blocks)
    total = sum(source.shape[0] for source in pieces.values())
    anywhere = pl.BlockSpec(memory_space=pltpu.HBM)
    return pl.pallas_call(
        functools.partial(assemble_kernel, tuple(pieces), blocks),
        in_specs=[SMEM] + [VMEM] * len(pieces) + [anywhere] * len(into),
        out_specs=[anywhere, anywhere],
        out_shape=[
            jax.ShapeDtypeStruct((inputs, width), jnp.bfloat16),
            jax.ShapeDtypeStruct((classes, width), jnp.bfloat16),
        ],
        scratch_shapes=[
            pltpu.VMEM((total * rows, width), jnp.bfloat16),
            pltpu.VMEM((total * 8, width), jnp.bfloat16),
            pltpu.VMEM((len(pieces), 8, width), jnp.bfloat16),
            pltpu.SemaphoreType.DMA((3 * len(pieces),)),
        ],
        input_output_aliases={1 + len(pieces) + at: at for at in range(len(into))},
        cost_estimate=pl.CostEstimate(
            flops=0, transcendentals=0, bytes_accessed=total * (rows + 8) * width * 8
        ),
        compiler_params=pltpu.CompilerParams(vmem_limit_bytes=LIMIT),
        name="assemble",
    )(place, *[placed(source) for source in pieces.values()], *into)


def shards(features, fc_weight, class_weight, labels):
    faces, inputs = features.shape
    features = features.T
    classes, width = class_weight.shape
    n_cls = lax.axis_size(CLS)
    chips = lax.axis_size(CHIPS)
    blocks = 2 * chips
    loss_weight = 1.0 / math.sqrt(faces * blocks * lax.axis_size("core"))
    place = (lax.axis_index(CLS) * 2 + lax.axis_index("zl")) * 2 + lax.axis_index("core")
    place = place.reshape(1)
    labels = labels.reshape(1, faces)

    sent, class_unit = embed(place, features, fc_weight, class_weight, labels)
    got = exchange(sent, CLS).reshape(n_cls, faces // n_cls, 2 * width)
    got = jnp.sum(got.astype(jnp.float32), axis=0)
    raw_embed, target_unit = got[:, :width], got[:, width:]
    unit = (raw_embed / row_norm(raw_embed)).astype(jnp.bfloat16)
    units = exchange(jnp.broadcast_to(unit, (n_cls,) + unit.shape), CLS)
    units = units.reshape(faces, width)

    pull, others = cosines(place, units, class_unit, labels)
    got = exchange(pull, CLS).reshape(n_cls, faces // n_cls, width + LANES)
    sent = raw_grads(loss_weight, got, raw_embed, target_unit)
    grads = exchange(sent, CLS).reshape(faces, width + LANES)

    swap = [(0, 1), (1, 0)]
    length = 2 * lax.axis_size("zh")
    pairs = [[(z, z ^ 1) for z in range(length)]]
    pairs.append([(z, (z + 2 * (z % 2) - 1) % length) for z in range(length)])

    def neighbours(values):
        parts_of = (values[: chips // 2], values[chips // 2 :])
        return [lax.ppermute(part, ("zh", "zl"), pair) for part, pair in zip(parts_of, pairs)]

    operands = (blocks, features, grads, units, others, class_weight)
    theirs = lax.ppermute(parts(True, place, jnp.bfloat16, *operands), "core", swap)
    total = parts(False, place, jnp.float32, *operands) + theirs.astype(jnp.float32)
    got = jnp.concatenate(neighbours(total[:chips].astype(jnp.bfloat16)), axis=0)
    mine = (total[chips:] + got.astype(jnp.float32)).astype(jnp.bfloat16)
    done = jnp.sum(exchange(mine, CHIPS).astype(jnp.float32), axis=0).astype(jnp.bfloat16)

    sizes = (inputs, classes, width)
    mine = exchange(jnp.broadcast_to(done, (chips,) + done.shape), CHIPS)
    left, right = neighbours(mine)
    across_own = lax.ppermute(mine, "core", swap)
    across_next = lax.ppermute(jnp.concatenate([left, right], axis=0), "core", swap)
    written = assemble(place, blocks, sizes, {(False, False, 0): mine}, ())
    written = assemble(
        place,
        blocks,
        sizes,
        {
            (False, True, 0): left,
            (False, True, chips // 2): right,
            (True, False, 0): across_own,
        },
        written,
    )
    return tuple(assemble(place, blocks, sizes, {(True, True, 0): across_next}, written))


def solution(mesh):
    fine = Mesh(mesh.devices.reshape(4, 2, 4, 2, 4, 2), ("zh", "zl", "yh", "core", "x", "yl"))
    dp = ("zh", "zl", "yh", "core")
    specs = (P(dp, CLS), P(CLS, None), P(CLS, None), P(dp))
    return jax.shard_map(
        shards,
        mesh=fine,
        in_specs=specs,
        out_specs=(P(CLS, None), P(CLS, None)),
        check_vma=False,
    )
```

```python
import functools
import math

import jax
import jax.numpy as jnp
from jax import lax
from jax.experimental import pallas as pl
from jax.experimental.pallas import tpu as pltpu
from jax.sharding import Mesh
from jax.sharding import PartitionSpec as P

SCALE = 64.0
MARGIN = 0.5
SOFTEN = 0.01
EPSILON = 1e-06

CLS = ("x", "yl")
CHIPS = ("zh", "yh")
LANES = 128
CHUNKS = 3
LIMIT = 24 << 20
VMEM = pl.BlockSpec(memory_space=pltpu.VMEM)
SMEM = pl.BlockSpec(memory_space=pltpu.SMEM)


def exchange(blocks, axes):
    return lax.all_to_all(blocks, axes, 0, 0, tiled=True)


def across(left, right):
    return lax.dot_general(
        left, right, (((0,), (0,)), ((), ())), preferred_element_type=jnp.float32
    )


def row_norm(values):
    return jnp.sqrt(jnp.sum(values * values, axis=1, keepdims=True) + EPSILON)


def packed_columns(*columns):
    rows = columns[0].shape[0]
    lane = lax.broadcasted_iota(jnp.int32, (rows, LANES), 1)
    block = jnp.zeros((rows, LANES), jnp.float32)
    for at, column in enumerate(columns):
        rest = column
        for part in range(3):
            term = rest.astype(jnp.bfloat16).astype(jnp.float32)
            block = jnp.where(lane == 3 * at + part, term, block)
            rest = rest - term
    return block.astype(jnp.bfloat16)


def unpacked_column(block, at):
    lane = lax.broadcasted_iota(jnp.int32, block.shape, 1)
    inside = (lane >= 3 * at) & (lane < 3 * at + 3)
    return jnp.sum(jnp.where(inside, block, 0.0), axis=1, keepdims=True)


def placed(array, space=pltpu.VMEM):
    return pltpu.with_memory_space_constraint(array, space)


def half_of(place_ref, other):
    core = lax.rem(place_ref[0], 2)
    return 1 - core if other else core


def parity_of(place_ref, other):
    odd = lax.rem(lax.div(place_ref[0], 2), 2)
    return 1 - odd if other else odd


def first_of(place_ref, classes):
    return lax.div(place_ref[0], 4) * classes


def call(kernel, name, operands, results, **options):
    specs = [SMEM if operand.ndim == 1 else VMEM for operand in operands]
    operands = [operand if operand.ndim == 1 else placed(operand) for operand in operands]
    return pl.pallas_call(
        kernel,
        in_specs=specs,
        out_specs=[VMEM] * len(results),
        out_shape=[pltpu.VMEM(shape, dtype) for shape, dtype in results],
        compiler_params=pltpu.CompilerParams(vmem_limit_bytes=LIMIT),
        name=name,
        **options,
    )(*operands)


def target_mask(first, labels, rows, classes):
    lane = lax.broadcasted_iota(jnp.int32, (rows, LANES), 1)
    return jnp.concatenate(
        [labels == lane + (first + at) for at in range(0, classes, LANES)], axis=1
    )


def spread_labels(labels_row):
    faces = labels_row.shape[1]
    return jnp.transpose(jnp.broadcast_to(labels_row, (LANES, faces)))


def embed_kernel(
    place_ref, features_ref, fc_ref, class_ref, labels_ref, sent_ref, unit_ref,
    left_ref, right_ref, total_ref, weight_ref, row_ref, sems
):
    width = fc_ref.shape[1]
    inputs, faces = features_ref.shape
    classes = class_ref.shape[0]
    ends = [inputs * at // CHUNKS // LANES * LANES for at in range(CHUNKS)] + [inputs]
    copies = [
        pltpu.make_async_copy(labels_ref, row_ref, sems.at[0]),
        pltpu.make_async_copy(class_ref, weight_ref, sems.at[1]),
    ]
    for at in range(CHUNKS):
        rows = pl.ds(ends[at], ends[at + 1] - ends[at])
        for source, target in ((features_ref, left_ref), (fc_ref, right_ref)):
            copies.append(
                pltpu.make_async_copy(
                    source.at[rows, :], target.at[rows, :], sems.at[len(copies)]
                )
            )
    for copy in copies:
        copy.start()

    copies[0].wait()
    labels = spread_labels(row_ref[...])
    chosen = target_mask(first_of(place_ref, classes), labels, faces, classes)
    chosen = jnp.where(chosen, 1.0, 0.0).astype(jnp.bfloat16)
    copies[1].wait()
    class_f = weight_ref[...].astype(jnp.float32)
    unit_ref[...] = (class_f / row_norm(class_f)).astype(jnp.bfloat16)
    target_part = jnp.dot(chosen, unit_ref[...], preferred_element_type=jnp.float32)
    sent_ref[:, width:] = target_part.astype(jnp.bfloat16)

    for at in range(CHUNKS):
        copies[2 + 2 * at].wait()
        copies[3 + 2 * at].wait()
        here = slice(ends[at], ends[at + 1])
        part = across(left_ref[here, :], right_ref[here, :])
        if at > 0:
            part = part + total_ref[...]
        if at < CHUNKS - 1:
            total_ref[...] = part
        else:
            sent_ref[:, :width] = part.astype(jnp.bfloat16)


def embed(place, features, fc_weight, class_weight, labels):
    inputs, faces = features.shape
    classes, width = class_weight.shape
    arrays = [placed(array, pltpu.HBM) for array in (features, fc_weight, class_weight, labels)]
    return pl.pallas_call(
        embed_kernel,
        in_specs=[SMEM] + [pl.BlockSpec(memory_space=pltpu.HBM)] * len(arrays),
        out_specs=[VMEM, VMEM],
        out_shape=[
            pltpu.VMEM((faces, 2 * width), jnp.bfloat16),
            pltpu.VMEM((classes, width), jnp.bfloat16),
        ],
        scratch_shapes=[
            pltpu.VMEM((inputs, faces), jnp.bfloat16),
            pltpu.VMEM((inputs, width), jnp.bfloat16),
            pltpu.VMEM((faces, width), jnp.float32),
            pltpu.VMEM((classes, width), jnp.bfloat16),
            pltpu.VMEM((1, faces), jnp.int32),
            pltpu.SemaphoreType.DMA((2 + 2 * CHUNKS,)),
        ],
        compiler_params=pltpu.CompilerParams(vmem_limit_bytes=LIMIT),
        name="embed",
    )(place, *arrays)


def cosine_kernel(place_ref, units_ref, class_ref, labels_ref, pull_ref, others_ref):
    faces, width = units_ref.shape
    classes = class_ref.shape[0]
    step = 128
    labels = spread_labels(labels_ref[...])
    for at in range(0, faces, step):
        here = slice(at, at + step)
        cosine = lax.dot_general(
            units_ref[here, :],
            class_ref[...],
            (((1,), (1,)), ((), ())),
            preferred_element_type=jnp.float32,
        )
        is_target = target_mask(first_of(place_ref, classes), labels[here, :], step, classes)
        powers = jnp.exp(SCALE * cosine)
        others = jnp.where(is_target, 0.0, powers)
        others_ref[here, :] = jnp.where(is_target, -1.0, powers)
        pull = jnp.dot(
            others.astype(jnp.bfloat16), class_ref[...], preferred_element_type=jnp.float32
        )
        pull_ref[here, :width] = pull.astype(jnp.bfloat16)
        pull_ref[here, width:] = packed_columns(jnp.sum(others, axis=1, keepdims=True))


def cosines(place, units, class_unit, labels):
    faces, width = units.shape
    classes = class_unit.shape[0]
    return call(
        cosine_kernel,
        "cosines",
        (place, units, class_unit, labels),
        [((faces, width + LANES), jnp.bfloat16), ((faces, classes), jnp.float32)],
    )


def raw_grad_kernel(loss_weight, pulls_ref, raw_ref, target_ref, sent_ref):
    width = raw_ref.shape[1]
    pulls = jnp.sum(pulls_ref[...].astype(jnp.float32), axis=0)
    pull, rest = pulls[:, :width], unpacked_column(pulls[:, width:], 0)
    raw_embed, target = raw_ref[...], target_ref[...]
    embed_norm = row_norm(raw_embed)
    unit_f = raw_embed / embed_norm
    unit = unit_f.astype(jnp.bfloat16).astype(jnp.float32)
    cos_t = jnp.sum(unit * target, axis=1, keepdims=True)
    sine_t = jnp.sqrt(1.0 + SOFTEN - cos_t * cos_t)
    power_t = jnp.exp(SCALE * (cos_t * math.cos(MARGIN) - sine_t * math.sin(MARGIN)))
    slope_t = SCALE * (math.cos(MARGIN) + math.sin(MARGIN) * cos_t / sine_t)
    inverse = loss_weight / (rest + power_t)
    pull_scale = SCALE * inverse
    target_scale = rest * inverse * slope_t
    unit_grad = pull * pull_scale - target * target_scale
    raw_grad = (
        unit_grad - unit_f * jnp.sum(unit_f * unit_grad, axis=1, keepdims=True)
    ) / embed_norm
    raw_grad = raw_grad.astype(jnp.bfloat16)
    scales = packed_columns(pull_scale, target_scale)
    for copy in range(sent_ref.shape[0]):
        sent_ref[copy, :, :width] = raw_grad
        sent_ref[copy, :, width:] = scales


def raw_grads(loss_weight, pulls, raw_embed, target_unit):
    return call(
        functools.partial(raw_grad_kernel, loss_weight),
        "raw_grads",
        (pulls, raw_embed, target_unit),
        [(pulls.shape, jnp.bfloat16)],
    )[0]


def block_sizes(inputs, width, blocks):
    rows = inputs // (2 * blocks * 8) * 8
    return rows, width // LANES, 2 * blocks * rows


def parts_kernel(
    other, place_ref, features_ref, grads_ref, units_ref, others_ref, class_ref, out_ref
):
    blocks = out_ref.shape[0]
    some = blocks // 2
    classes, width = class_ref.shape
    inputs = features_ref.shape[0]
    rows, groups, main = block_sizes(inputs, width, blocks)
    base = groups * rows
    half = half_of(place_ref, other)
    grads = grads_ref[:, :width]
    scales = grads_ref[:, width:].astype(jnp.float32)
    pull_scale, target_scale = unpacked_column(scales, 0), unpacked_column(scales, 1)
    each = (inputs - main) // 2
    over = jnp.dot(
        features_ref[pl.ds(pl.multiple_of(main + half * each, each), each), :],
        grads,
        preferred_element_type=jnp.float32,
    ).astype(out_ref.dtype)
    count = classes // 4

    for at, parity in ((0, parity_of(place_ref, True)), (some, parity_of(place_ref, False))):
        here = slice(at, at + some)
        first = pl.multiple_of((2 * half + parity) * (some * rows), LANES)
        part = jnp.dot(
            features_ref[pl.ds(first, some * rows), :], grads, preferred_element_type=jnp.float32
        )
        part = part.astype(out_ref.dtype).reshape(some, rows, width)
        for group in range(groups):
            out_ref[here, group * rows : (group + 1) * rows, :] = part[
                :, :, group * LANES : (group + 1) * LANES
            ]

        first = pl.multiple_of((2 * half + parity) * count, LANES)
        others = others_ref[:, pl.ds(first, count)]
        cos_grad = jnp.where(others < 0.0, -target_scale, others * pull_scale)
        part = across(cos_grad.astype(jnp.bfloat16), units_ref[...])
        class_f = class_ref[pl.ds(first, count), :].astype(jnp.float32)
        class_norm = row_norm(class_f)
        class_unit = class_f / class_norm
        part = part - class_unit * jnp.sum(class_unit * part, axis=1, keepdims=True)
        part = (part / class_norm).astype(out_ref.dtype).reshape(some, 8, width)
        for group in range(groups):
            out_ref[here, base + group * 8 : base + (group + 1) * 8, :] = part[
                :, :, group * LANES : (group + 1) * LANES
            ]

        strip = jnp.where(parity == 0, over[:8], over[8:])
        for group in range(groups):
            out_ref[at + group, base + groups * 8 :, :] = strip[
                :, group * LANES : (group + 1) * LANES
            ]
        out_ref[at + groups : at + some, base + groups * 8 :, :] = jnp.zeros(
            (some - groups, 8, LANES), out_ref.dtype
        )


def parts(other, place, dtype, blocks, features, grads, units, others, class_weight):
    rows, groups, _ = block_sizes(features.shape[0], class_weight.shape[1], blocks)
    return call(
        functools.partial(parts_kernel, other),
        "parts",
        (place, features, grads, units, others, class_weight),
        [((blocks, groups * (rows + 8) + 8, LANES), dtype)],
    )[0]


def assemble_kernel(pieces, blocks, place_ref, *refs):
    sources = refs[: len(pieces)]
    fc_ref, class_ref, fc_rows, class_rows, over_rows, sems = refs[-6:]
    inputs, width = fc_ref.shape
    rows, groups, main = block_sizes(inputs, width, blocks)
    each = (inputs - main) // 2
    base = groups * rows
    some = blocks // 2
    copies = []
    done = 0

    def send(source, target, at, size):
        copies.append(
            pltpu.make_async_copy(
                source, target.at[pl.ds(pl.multiple_of(at, 8), size), :], sems.at[len(copies)]
            )
        )
        copies[-1].start()

    for number, (piece, source) in enumerate(zip(pieces, sources)):
        half, parity = half_of(place_ref, piece[0]), parity_of(place_ref, piece[1])
        count = source.shape[0]
        block = (2 * half + parity) * some
        fc_here = slice(done * rows, (done + count) * rows)
        class_here = slice(done * 8, (done + count) * 8)
        for group in range(groups):
            lanes = slice(group * LANES, (group + 1) * LANES)
            values = source[:, group * rows : (group + 1) * rows, :].astype(jnp.float32)
            fc_rows[fc_here, lanes] = values.reshape(count * rows, LANES).astype(jnp.bfloat16)
            values = source[:, base + group * 8 : base + (group + 1) * 8, :].astype(jnp.float32)
            class_rows[class_here, lanes] = values.reshape(count * 8, LANES).astype(jnp.bfloat16)
            over_rows[number, :, lanes] = source[group, base + groups * 8 :, :]
        send(fc_rows.at[fc_here, :], fc_ref, block * rows, count * rows)
        send(class_rows.at[class_here, :], class_ref, block * 8, count * 8)
        send(over_rows.at[number], fc_ref, main + half * each + parity * 8, 8)
        done += count
    for copy in copies:
        copy.wait()


def assemble(place, blocks, sizes, pieces, into):
    inputs, classes, width = sizes
    rows, _, _ = block_sizes(inputs, width, blocks)
    total = sum(source.shape[0] for source in pieces.values())
    anywhere = pl.BlockSpec(memory_space=pltpu.HBM)
    return pl.pallas_call(
        functools.partial(assemble_kernel, tuple(pieces), blocks),
        in_specs=[SMEM] + [VMEM] * len(pieces) + [anywhere] * len(into),
        out_specs=[anywhere, anywhere],
        out_shape=[
            jax.ShapeDtypeStruct((inputs, width), jnp.bfloat16),
            jax.ShapeDtypeStruct((classes, width), jnp.bfloat16),
        ],
        scratch_shapes=[
            pltpu.VMEM((total * rows, width), jnp.bfloat16),
            pltpu.VMEM((total * 8, width), jnp.bfloat16),
            pltpu.VMEM((len(pieces), 8, width), jnp.bfloat16),
            pltpu.SemaphoreType.DMA((3 * len(pieces),)),
        ],
        input_output_aliases={1 + len(pieces) + at: at for at in range(len(into))},
        cost_estimate=pl.CostEstimate(
            flops=0, transcendentals=0, bytes_accessed=total * (rows + 8) * width * 8
        ),
        compiler_params=pltpu.CompilerParams(vmem_limit_bytes=LIMIT),
        name="assemble",
    )(place, *[placed(source) for source in pieces.values()], *into)


def shards(features, fc_weight, class_weight, labels):
    faces, inputs = features.shape
    features = features.T
    classes, width = class_weight.shape
    n_cls = lax.axis_size(CLS)
    chips = lax.axis_size(CHIPS)
    blocks = 2 * chips
    loss_weight = 1.0 / math.sqrt(faces * blocks * lax.axis_size("core"))
    place = (lax.axis_index(CLS) * 2 + lax.axis_index("zl")) * 2 + lax.axis_index("core")
    place = place.reshape(1)
    labels = labels.reshape(1, faces)

    sent, class_unit = embed(place, features, fc_weight, class_weight, labels)
    got = exchange(sent, CLS).reshape(n_cls, faces // n_cls, 2 * width)
    got = jnp.sum(got.astype(jnp.float32), axis=0)
    raw_embed, target_unit = got[:, :width], got[:, width:]
    unit = (raw_embed / row_norm(raw_embed)).astype(jnp.bfloat16)
    units = exchange(jnp.broadcast_to(unit, (n_cls,) + unit.shape), CLS)
    units = units.reshape(faces, width)

    pull, others = cosines(place, units, class_unit, labels)
    got = exchange(pull, CLS).reshape(n_cls, faces // n_cls, width + LANES)
    sent = raw_grads(loss_weight, got, raw_embed, target_unit)
    grads = exchange(sent, CLS).reshape(faces, width + LANES)

    swap = [(0, 1), (1, 0)]
    length = 2 * lax.axis_size("zh")
    pairs = []
    for z in range(length):
        pairs.append((2 * z, 2 * (z ^ 1)))
        pairs.append((2 * z + 1, 2 * ((z + 2 * (z % 2) - 1) % length) + 1))
    neighbour = ("zh", "zl", "core")

    operands = (blocks, features, grads, units, others, class_weight)
    theirs = lax.ppermute(parts(True, place, jnp.bfloat16, *operands), "core", swap)
    total = parts(False, place, jnp.float32, *operands) + theirs.astype(jnp.float32)
    got = lax.ppermute(total[:chips].astype(jnp.bfloat16), neighbour, pairs)
    mine = (total[chips:] + got.astype(jnp.float32)).astype(jnp.bfloat16)
    done = jnp.sum(exchange(mine, CHIPS).astype(jnp.float32), axis=0).astype(jnp.bfloat16)

    sizes = (inputs, classes, width)
    mine = exchange(jnp.broadcast_to(done, (chips,) + done.shape), CHIPS)
    next_mine = lax.ppermute(mine, neighbour, pairs)
    across_mine = lax.ppermute(mine, "core", swap)
    written = assemble(place, blocks, sizes, {(False, False): mine}, ())
    next_mine, written = lax.optimization_barrier((next_mine, written))
    across_next = lax.ppermute(next_mine, "core", swap)
    pieces = {(False, True): next_mine, (True, False): across_mine}
    written = assemble(place, blocks, sizes, pieces, written)
    return tuple(assemble(place, blocks, sizes, {(True, True): across_next}, written))


def solution(mesh):
    fine = Mesh(mesh.devices.reshape(4, 2, 4, 2, 4, 2), ("zh", "zl", "yh", "core", "x", "yl"))
    dp = ("zh", "zl", "yh", "core")
    specs = (P(dp, CLS), P(CLS, None), P(CLS, None), P(dp))
    return jax.shard_map(
        shards,
        mesh=fine,
        in_specs=specs,
        out_specs=(P(CLS, None), P(CLS, None)),
        check_vma=False,
    )
```

```python
import functools
import math

import jax
import jax.numpy as jnp
from jax import lax
from jax.experimental import pallas as pl
from jax.experimental.pallas import tpu as pltpu
from jax.sharding import Mesh
from jax.sharding import PartitionSpec as P

SCALE = 64.0
MARGIN = 0.5
SOFTEN = 0.01
EPSILON = 1e-06

CLS = ("x", "yl")
CHIPS = ("zh", "yh")
LANES = 128
CHUNKS = 3
LIMIT = 24 << 20
VMEM = pl.BlockSpec(memory_space=pltpu.VMEM)
SMEM = pl.BlockSpec(memory_space=pltpu.SMEM)


def exchange(blocks, axes):
    return lax.all_to_all(blocks, axes, 0, 0, tiled=True)


def across(left, right):
    return lax.dot_general(
        left, right, (((0,), (0,)), ((), ())), preferred_element_type=jnp.float32
    )


def row_norm(values):
    return jnp.sqrt(jnp.sum(values * values, axis=1, keepdims=True) + EPSILON)


def packed_columns(*columns):
    rows = columns[0].shape[0]
    lane = lax.broadcasted_iota(jnp.int32, (rows, LANES), 1)
    block = jnp.zeros((rows, LANES), jnp.float32)
    for at, column in enumerate(columns):
        rest = column
        for part in range(3):
            term = rest.astype(jnp.bfloat16).astype(jnp.float32)
            block = jnp.where(lane == 3 * at + part, term, block)
            rest = rest - term
    return block.astype(jnp.bfloat16)


def unpacked_column(block, at):
    lane = lax.broadcasted_iota(jnp.int32, block.shape, 1)
    inside = (lane >= 3 * at) & (lane < 3 * at + 3)
    return jnp.sum(jnp.where(inside, block, 0.0), axis=1, keepdims=True)


def placed(array, space=pltpu.VMEM):
    return pltpu.with_memory_space_constraint(array, space)


def half_of(place_ref, other):
    core = lax.rem(place_ref[0], 2)
    return 1 - core if other else core


def parity_of(place_ref, other):
    odd = lax.rem(lax.div(place_ref[0], 2), 2)
    return 1 - odd if other else odd


def first_of(place_ref, classes):
    return lax.div(place_ref[0], 4) * classes


def call(kernel, name, operands, results, **options):
    specs = [SMEM if operand.ndim == 1 else VMEM for operand in operands]
    operands = [operand if operand.ndim == 1 else placed(operand) for operand in operands]
    return pl.pallas_call(
        kernel,
        in_specs=specs,
        out_specs=[VMEM] * len(results),
        out_shape=[pltpu.VMEM(shape, dtype) for shape, dtype in results],
        compiler_params=pltpu.CompilerParams(vmem_limit_bytes=LIMIT),
        name=name,
        **options,
    )(*operands)


def target_mask(first, labels, rows, classes):
    lane = lax.broadcasted_iota(jnp.int32, (rows, LANES), 1)
    return jnp.concatenate(
        [labels == lane + (first + at) for at in range(0, classes, LANES)], axis=1
    )


def spread_labels(labels_row):
    faces = labels_row.shape[1]
    return jnp.transpose(jnp.broadcast_to(labels_row, (LANES, faces)))


def embed_kernel(
    place_ref, features_ref, fc_ref, class_ref, labels_ref, sent_ref, unit_ref,
    left_ref, right_ref, total_ref, weight_ref, row_ref, sems
):
    width = fc_ref.shape[1]
    inputs, faces = features_ref.shape
    classes = class_ref.shape[0]
    ends = [inputs * at // CHUNKS // LANES * LANES for at in range(CHUNKS)] + [inputs]
    copies = [
        pltpu.make_async_copy(labels_ref, row_ref, sems.at[0]),
        pltpu.make_async_copy(class_ref, weight_ref, sems.at[1]),
    ]
    for at in range(CHUNKS):
        rows = pl.ds(ends[at], ends[at + 1] - ends[at])
        for source, target in ((features_ref, left_ref), (fc_ref, right_ref)):
            copies.append(
                pltpu.make_async_copy(
                    source.at[rows, :], target.at[rows, :], sems.at[len(copies)]
                )
            )
    for copy in copies:
        copy.start()

    copies[0].wait()
    labels = spread_labels(row_ref[...])
    chosen = target_mask(first_of(place_ref, classes), labels, faces, classes)
    chosen = jnp.where(chosen, 1.0, 0.0).astype(jnp.bfloat16)
    copies[1].wait()
    class_f = weight_ref[...].astype(jnp.float32)
    unit_ref[...] = (class_f / row_norm(class_f)).astype(jnp.bfloat16)
    target_part = jnp.dot(chosen, unit_ref[...], preferred_element_type=jnp.float32)
    sent_ref[:, width:] = target_part.astype(jnp.bfloat16)

    for at in range(CHUNKS):
        copies[2 + 2 * at].wait()
        copies[3 + 2 * at].wait()
        here = slice(ends[at], ends[at + 1])
        part = across(left_ref[here, :], right_ref[here, :])
        if at > 0:
            part = part + total_ref[...]
        if at < CHUNKS - 1:
            total_ref[...] = part
        else:
            sent_ref[:, :width] = part.astype(jnp.bfloat16)


def embed(place, features, fc_weight, class_weight, labels):
    inputs, faces = features.shape
    classes, width = class_weight.shape
    arrays = [placed(array, pltpu.HBM) for array in (features, fc_weight, class_weight, labels)]
    return pl.pallas_call(
        embed_kernel,
        in_specs=[SMEM] + [pl.BlockSpec(memory_space=pltpu.HBM)] * len(arrays),
        out_specs=[VMEM, VMEM],
        out_shape=[
            pltpu.VMEM((faces, 2 * width), jnp.bfloat16),
            pltpu.VMEM((classes, width), jnp.bfloat16),
        ],
        scratch_shapes=[
            pltpu.VMEM((inputs, faces), jnp.bfloat16),
            pltpu.VMEM((inputs, width), jnp.bfloat16),
            pltpu.VMEM((faces, width), jnp.float32),
            pltpu.VMEM((classes, width), jnp.bfloat16),
            pltpu.VMEM((1, faces), jnp.int32),
            pltpu.SemaphoreType.DMA((2 + 2 * CHUNKS,)),
        ],
        compiler_params=pltpu.CompilerParams(vmem_limit_bytes=LIMIT),
        name="embed",
    )(place, *arrays)


def cosine_kernel(place_ref, units_ref, class_ref, labels_ref, pull_ref, others_ref):
    faces, width = units_ref.shape
    classes = class_ref.shape[0]
    step = 128
    labels = spread_labels(labels_ref[...])
    for at in range(0, faces, step):
        here = slice(at, at + step)
        cosine = lax.dot_general(
            units_ref[here, :],
            class_ref[...],
            (((1,), (1,)), ((), ())),
            preferred_element_type=jnp.float32,
        )
        is_target = target_mask(first_of(place_ref, classes), labels[here, :], step, classes)
        powers = jnp.exp(SCALE * cosine)
        others = jnp.where(is_target, 0.0, powers)
        others_ref[here, :] = jnp.where(is_target, -1.0, powers)
        pull = jnp.dot(
            others.astype(jnp.bfloat16), class_ref[...], preferred_element_type=jnp.float32
        )
        pull_ref[here, :width] = pull.astype(jnp.bfloat16)
        pull_ref[here, width:] = packed_columns(jnp.sum(others, axis=1, keepdims=True))


def cosines(place, units, class_unit, labels):
    faces, width = units.shape
    classes = class_unit.shape[0]
    return call(
        cosine_kernel,
        "cosines",
        (place, units, class_unit, labels),
        [((faces, width + LANES), jnp.bfloat16), ((faces, classes), jnp.float32)],
    )


def raw_grad_kernel(loss_weight, pulls_ref, raw_ref, target_ref, sent_ref):
    width = raw_ref.shape[1]
    pulls = jnp.sum(pulls_ref[...].astype(jnp.float32), axis=0)
    pull, rest = pulls[:, :width], unpacked_column(pulls[:, width:], 0)
    raw_embed, target = raw_ref[...], target_ref[...]
    embed_norm = row_norm(raw_embed)
    unit_f = raw_embed / embed_norm
    unit = unit_f.astype(jnp.bfloat16).astype(jnp.float32)
    cos_t = jnp.sum(unit * target, axis=1, keepdims=True)
    sine_t = jnp.sqrt(1.0 + SOFTEN - cos_t * cos_t)
    power_t = jnp.exp(SCALE * (cos_t * math.cos(MARGIN) - sine_t * math.sin(MARGIN)))
    slope_t = SCALE * (math.cos(MARGIN) + math.sin(MARGIN) * cos_t / sine_t)
    inverse = loss_weight / (rest + power_t)
    pull_scale = SCALE * inverse
    target_scale = rest * inverse * slope_t
    unit_grad = pull * pull_scale - target * target_scale
    raw_grad = (
        unit_grad - unit_f * jnp.sum(unit_f * unit_grad, axis=1, keepdims=True)
    ) / embed_norm
    raw_grad = raw_grad.astype(jnp.bfloat16)
    scales = packed_columns(pull_scale, target_scale)
    for copy in range(sent_ref.shape[0]):
        sent_ref[copy, :, :width] = raw_grad
        sent_ref[copy, :, width:] = scales


def raw_grads(loss_weight, pulls, raw_embed, target_unit):
    return call(
        functools.partial(raw_grad_kernel, loss_weight),
        "raw_grads",
        (pulls, raw_embed, target_unit),
        [(pulls.shape, jnp.bfloat16)],
    )[0]


def block_sizes(inputs, width, blocks):
    rows = inputs // (2 * blocks * 8) * 8
    return rows, width // LANES, 2 * blocks * rows


def parts_kernel(
    other_half, other_parity,
    place_ref, features_ref, grads_ref, units_ref, others_ref, class_ref, out_ref
):
    some = out_ref.shape[0]
    classes, width = class_ref.shape
    inputs = features_ref.shape[0]
    rows, groups, main = block_sizes(inputs, width, 2 * some)
    base = groups * rows
    half, parity = half_of(place_ref, other_half), parity_of(place_ref, other_parity)
    quarter = 2 * half + parity
    grads = grads_ref[:, :width]

    first = pl.multiple_of(quarter * (some * rows), LANES)
    part = jnp.dot(
        features_ref[pl.ds(first, some * rows), :], grads, preferred_element_type=jnp.float32
    )
    part = part.astype(out_ref.dtype).reshape(some, rows, width)
    for group in range(groups):
        out_ref[:, group * rows : (group + 1) * rows, :] = part[
            :, :, group * LANES : (group + 1) * LANES
        ]

    scales = grads_ref[:, width:].astype(jnp.float32)
    pull_scale, target_scale = unpacked_column(scales, 0), unpacked_column(scales, 1)
    count = classes // 4
    first = pl.multiple_of(quarter * count, LANES)
    others = others_ref[:, pl.ds(first, count)]
    cos_grad = jnp.where(others < 0.0, -target_scale, others * pull_scale)
    part = across(cos_grad.astype(jnp.bfloat16), units_ref[...])
    class_f = class_ref[pl.ds(first, count), :].astype(jnp.float32)
    class_norm = row_norm(class_f)
    class_unit = class_f / class_norm
    part = part - class_unit * jnp.sum(class_unit * part, axis=1, keepdims=True)
    part = (part / class_norm).astype(out_ref.dtype).reshape(some, 8, width)
    for group in range(groups):
        out_ref[:, base + group * 8 : base + (group + 1) * 8, :] = part[
            :, :, group * LANES : (group + 1) * LANES
        ]

    each = (inputs - main) // 2
    over = jnp.dot(
        features_ref[pl.ds(pl.multiple_of(main + half * each, each), each), :],
        grads,
        preferred_element_type=jnp.float32,
    ).astype(out_ref.dtype)
    strip = jnp.where(parity == 0, over[:8], over[8:])
    for group in range(groups):
        out_ref[group, base + groups * 8 :, :] = strip[:, group * LANES : (group + 1) * LANES]
    out_ref[groups:, base + groups * 8 :, :] = jnp.zeros((some - groups, 8, LANES), out_ref.dtype)


def parts(quarter, place, dtype, blocks, features, grads, units, others, class_weight):
    width = class_weight.shape[1]
    rows, groups, _ = block_sizes(features.shape[0], width, blocks)
    return call(
        functools.partial(parts_kernel, *quarter),
        "parts",
        (place, features, grads, units, others, class_weight),
        [((blocks // 2, groups * (rows + 8) + 8, LANES), dtype)],
    )[0]


def assemble_kernel(pieces, blocks, place_ref, *refs):
    sources = refs[: len(pieces)]
    fc_ref, class_ref, fc_rows, class_rows, over_rows, sems = refs[-6:]
    inputs, width = fc_ref.shape
    rows, groups, main = block_sizes(inputs, width, blocks)
    each = (inputs - main) // 2
    base = groups * rows
    some = blocks // 2
    copies = []
    done = 0

    def send(source, target, at, size):
        copies.append(
            pltpu.make_async_copy(
                source, target.at[pl.ds(pl.multiple_of(at, 8), size), :], sems.at[len(copies)]
            )
        )
        copies[-1].start()

    for number, (piece, source) in enumerate(zip(pieces, sources)):
        half, parity = half_of(place_ref, piece[0]), parity_of(place_ref, piece[1])
        count = source.shape[0]
        block = (2 * half + parity) * some
        fc_here = slice(done * rows, (done + count) * rows)
        class_here = slice(done * 8, (done + count) * 8)
        for group in range(groups):
            lanes = slice(group * LANES, (group + 1) * LANES)
            values = source[:, group * rows : (group + 1) * rows, :].astype(jnp.float32)
            fc_rows[fc_here, lanes] = values.reshape(count * rows, LANES).astype(jnp.bfloat16)
            values = source[:, base + group * 8 : base + (group + 1) * 8, :].astype(jnp.float32)
            class_rows[class_here, lanes] = values.reshape(count * 8, LANES).astype(jnp.bfloat16)
            over_rows[number, :, lanes] = source[group, base + groups * 8 :, :]
        send(fc_rows.at[fc_here, :], fc_ref, block * rows, count * rows)
        send(class_rows.at[class_here, :], class_ref, block * 8, count * 8)
        send(over_rows.at[number], fc_ref, main + half * each + parity * 8, 8)
        done += count
    for copy in copies:
        copy.wait()


def assemble(place, blocks, sizes, pieces, into):
    inputs, classes, width = sizes
    rows, _, _ = block_sizes(inputs, width, blocks)
    total = sum(source.shape[0] for source in pieces.values())
    anywhere = pl.BlockSpec(memory_space=pltpu.HBM)
    return pl.pallas_call(
        functools.partial(assemble_kernel, tuple(pieces), blocks),
        in_specs=[SMEM] + [VMEM] * len(pieces) + [anywhere] * len(into),
        out_specs=[anywhere, anywhere],
        out_shape=[
            jax.ShapeDtypeStruct((inputs, width), jnp.bfloat16),
            jax.ShapeDtypeStruct((classes, width), jnp.bfloat16),
        ],
        scratch_shapes=[
            pltpu.VMEM((total * rows, width), jnp.bfloat16),
            pltpu.VMEM((total * 8, width), jnp.bfloat16),
            pltpu.VMEM((len(pieces), 8, width), jnp.bfloat16),
            pltpu.SemaphoreType.DMA((3 * len(pieces),)),
        ],
        input_output_aliases={1 + len(pieces) + at: at for at in range(len(into))},
        cost_estimate=pl.CostEstimate(
            flops=0, transcendentals=0, bytes_accessed=total * (rows + 8) * width * 8
        ),
        compiler_params=pltpu.CompilerParams(vmem_limit_bytes=LIMIT),
        name="assemble",
    )(place, *[placed(source) for source in pieces.values()], *into)


def shards(features, fc_weight, class_weight, labels):
    faces, inputs = features.shape
    features = features.T
    classes, width = class_weight.shape
    n_cls = lax.axis_size(CLS)
    chips = lax.axis_size(CHIPS)
    blocks = 2 * chips
    loss_weight = 1.0 / math.sqrt(faces * blocks * lax.axis_size("core"))
    place = (lax.axis_index(CLS) * 2 + lax.axis_index("zl")) * 2 + lax.axis_index("core")
    place = place.reshape(1)
    labels = labels.reshape(1, faces)

    sent, class_unit = embed(place, features, fc_weight, class_weight, labels)
    got = exchange(sent, CLS).reshape(n_cls, faces // n_cls, 2 * width)
    got = jnp.sum(got.astype(jnp.float32), axis=0)
    raw_embed, target_unit = got[:, :width], got[:, width:]
    unit = (raw_embed / row_norm(raw_embed)).astype(jnp.bfloat16)
    units = exchange(jnp.broadcast_to(unit, (n_cls,) + unit.shape), CLS)
    units = units.reshape(faces, width)

    pull, others = cosines(place, units, class_unit, labels)
    got = exchange(pull, CLS).reshape(n_cls, faces // n_cls, width + LANES)
    sent = raw_grads(loss_weight, got, raw_embed, target_unit)
    grads = exchange(sent, CLS).reshape(faces, width + LANES)

    swap = [(0, 1), (1, 0)]
    length = 2 * lax.axis_size("zh")
    pairs = []
    for z in range(length):
        pairs.append((2 * z, 2 * (z ^ 1)))
        pairs.append((2 * z + 1, 2 * ((z + 2 * (z % 2) - 1) % length) + 1))
    neighbour = ("zh", "zl", "core")

    operands = (blocks, features, grads, units, others, class_weight)
    theirs = parts((True, True), place, jnp.bfloat16, *operands)
    theirs = lax.ppermute(theirs, "core", swap)
    sent = parts((False, True), place, jnp.float32, *operands) + theirs.astype(jnp.float32)
    sent, later = lax.optimization_barrier((sent.astype(jnp.bfloat16), place))
    got = lax.ppermute(sent, neighbour, pairs)
    theirs = parts((True, False), later, jnp.bfloat16, *operands)
    theirs = lax.ppermute(theirs, "core", swap)
    mine = parts((False, False), later, jnp.float32, *operands) + got.astype(jnp.float32)
    mine = lax.optimization_barrier(mine)
    mine = (mine + theirs.astype(jnp.float32)).astype(jnp.bfloat16)
    done = jnp.sum(exchange(mine, CHIPS).astype(jnp.float32), axis=0).astype(jnp.bfloat16)

    sizes = (inputs, classes, width)
    mine = exchange(jnp.broadcast_to(done, (chips,) + done.shape), CHIPS)
    next_mine = lax.ppermute(mine, neighbour, pairs)
    across_mine = lax.ppermute(mine, "core", swap)
    written = assemble(place, blocks, sizes, {(False, False): mine}, ())
    next_mine, written = lax.optimization_barrier((next_mine, written))
    across_next = lax.ppermute(next_mine, "core", swap)
    pieces = {(False, True): next_mine, (True, False): across_mine}
    written = assemble(place, blocks, sizes, pieces, written)
    return tuple(assemble(place, blocks, sizes, {(True, True): across_next}, written))


def solution(mesh):
    fine = Mesh(mesh.devices.reshape(4, 2, 4, 2, 4, 2), ("zh", "zl", "yh", "core", "x", "yl"))
    dp = ("zh", "zl", "yh", "core")
    specs = (P(dp, CLS), P(CLS, None), P(CLS, None), P(dp))
    return jax.shard_map(
        shards,
        mesh=fine,
        in_specs=specs,
        out_specs=(P(CLS, None), P(CLS, None)),
        check_vma=False,
    )
```

```python
import functools
import math

import jax
import jax.numpy as jnp
from jax import lax
from jax.experimental import pallas as pl
from jax.experimental.pallas import tpu as pltpu
from jax.sharding import Mesh
from jax.sharding import PartitionSpec as P

SCALE = 64.0
MARGIN = 0.5
SOFTEN = 0.01
EPSILON = 1e-06

CLS = ("x", "yl")
CHIPS = ("zh", "yh")
LANES = 128
CHUNKS = 2
MARK = 1024.0
STEP = 256
LIMIT = 24 << 20
VMEM = pl.BlockSpec(memory_space=pltpu.VMEM)
SMEM = pl.BlockSpec(memory_space=pltpu.SMEM)


def exchange(blocks, axes):
    return lax.all_to_all(blocks, axes, 0, 0, tiled=True)


def across(left, right):
    return lax.dot_general(
        left, right, (((0,), (0,)), ((), ())), preferred_element_type=jnp.float32
    )


def row_norm(values):
    return jnp.sqrt(jnp.sum(values * values, axis=1, keepdims=True) + EPSILON)


def packed_columns(*columns):
    rows = columns[0].shape[0]
    lane = lax.broadcasted_iota(jnp.int32, (rows, LANES), 1)
    block = jnp.zeros((rows, LANES), jnp.float32)
    for at, column in enumerate(columns):
        rest = column
        for part in range(3):
            term = rest.astype(jnp.bfloat16).astype(jnp.float32)
            block = jnp.where(lane == 3 * at + part, term, block)
            rest = rest - term
    return block


def unpacked_column(block, at):
    lane = lax.broadcasted_iota(jnp.int32, block.shape, 1)
    inside = (lane >= 3 * at) & (lane < 3 * at + 3)
    return jnp.sum(jnp.where(inside, block, 0.0), axis=1, keepdims=True)


def placed(array, space=pltpu.VMEM):
    return pltpu.with_memory_space_constraint(array, space)


def half_of(place_ref, other):
    core = lax.rem(place_ref[0], 2)
    return 1 - core if other else core


def parity_of(place_ref, other):
    odd = lax.rem(lax.div(place_ref[0], 2), 2)
    return 1 - odd if other else odd


def first_of(place_ref, classes):
    return lax.div(place_ref[0], 4) * classes


def call(kernel, name, operands, results, **options):
    specs = [SMEM if operand.ndim == 1 else VMEM for operand in operands]
    operands = [operand if operand.ndim == 1 else placed(operand) for operand in operands]
    return pl.pallas_call(
        kernel,
        in_specs=specs,
        out_specs=[VMEM] * len(results),
        out_shape=[pltpu.VMEM(shape, dtype) for shape, dtype in results],
        compiler_params=pltpu.CompilerParams(vmem_limit_bytes=LIMIT),
        name=name,
        **options,
    )(*operands)


def target_mask(first, labels, rows, classes):
    lane = lax.broadcasted_iota(jnp.int32, (rows, LANES), 1)
    return jnp.concatenate(
        [labels == lane + (first + at) for at in range(0, classes, LANES)], axis=1
    )


def spread_labels(labels_row):
    faces = labels_row.shape[1]
    return jnp.transpose(jnp.broadcast_to(labels_row, (LANES, faces)))


def embed_kernel(
    place_ref, features_ref, fc_ref, class_ref, labels_ref, sent_ref, unit_ref,
    left_ref, right_ref, total_ref, weight_ref, row_ref, sems
):
    width = fc_ref.shape[1]
    inputs, faces = features_ref.shape
    classes = class_ref.shape[0]
    ends = [inputs * at // CHUNKS // LANES * LANES for at in range(CHUNKS)] + [inputs]
    copies = [
        pltpu.make_async_copy(labels_ref, row_ref, sems.at[0]),
        pltpu.make_async_copy(class_ref, weight_ref, sems.at[1]),
    ]
    for at in range(CHUNKS):
        rows = pl.ds(ends[at], ends[at + 1] - ends[at])
        for source, target in ((features_ref, left_ref), (fc_ref, right_ref)):
            copies.append(
                pltpu.make_async_copy(
                    source.at[rows, :], target.at[rows, :], sems.at[len(copies)]
                )
            )
    for copy in copies:
        copy.start()

    copies[0].wait()
    labels = spread_labels(row_ref[...])
    chosen = target_mask(first_of(place_ref, classes), labels, faces, classes)
    chosen = jnp.where(chosen, 1.0, 0.0).astype(jnp.bfloat16)
    copies[1].wait()
    class_f = weight_ref[...].astype(jnp.float32)
    unit_ref[...] = (class_f / row_norm(class_f)).astype(jnp.bfloat16)
    target_part = jnp.dot(chosen, unit_ref[...], preferred_element_type=jnp.float32)
    sent_ref[:, width:] = target_part.astype(jnp.bfloat16)

    for at in range(CHUNKS):
        copies[2 + 2 * at].wait()
        copies[3 + 2 * at].wait()
        here = slice(ends[at], ends[at + 1])
        part = across(left_ref[here, :], right_ref[here, :])
        if at > 0:
            part = part + total_ref[...]
        if at < CHUNKS - 1:
            total_ref[...] = part
        else:
            sent_ref[:, :width] = part.astype(jnp.bfloat16)


def embed(place, features, fc_weight, class_weight, labels):
    inputs, faces = features.shape
    classes, width = class_weight.shape
    arrays = [placed(array, pltpu.HBM) for array in (features, fc_weight, class_weight, labels)]
    return pl.pallas_call(
        embed_kernel,
        in_specs=[SMEM] + [pl.BlockSpec(memory_space=pltpu.HBM)] * len(arrays),
        out_specs=[VMEM, VMEM],
        out_shape=[
            pltpu.VMEM((faces, 2 * width), jnp.bfloat16),
            pltpu.VMEM((classes, width), jnp.bfloat16),
        ],
        scratch_shapes=[
            pltpu.VMEM((inputs, faces), jnp.bfloat16),
            pltpu.VMEM((inputs, width), jnp.bfloat16),
            pltpu.VMEM((faces, width), jnp.float32),
            pltpu.VMEM((classes, width), jnp.bfloat16),
            pltpu.VMEM((1, faces), jnp.int32),
            pltpu.SemaphoreType.DMA((2 + 2 * CHUNKS,)),
        ],
        compiler_params=pltpu.CompilerParams(vmem_limit_bytes=LIMIT),
        name="embed",
    )(place, *arrays)


def target_terms(cosine):
    sine = jnp.sqrt(1.0 + SOFTEN - cosine * cosine)
    logit = SCALE * (cosine * math.cos(MARGIN) - sine * math.sin(MARGIN))
    slope = SCALE * (math.cos(MARGIN) + math.sin(MARGIN) * cosine / sine)
    return logit, slope


def cosine_kernel(place_ref, units_ref, class_ref, labels_ref, pull_ref, others_ref):
    faces, width = units_ref.shape
    classes = class_ref.shape[0]
    peers = pull_ref.shape[0]
    owned = faces // peers
    step = STEP
    first = first_of(place_ref, classes)
    labels = spread_labels(labels_ref[...])
    for at in range(0, faces, step):
        here = slice(at, at + step)
        cosine = lax.dot_general(
            units_ref[here, :],
            class_ref[...],
            (((1,), (1,)), ((), ())),
            preferred_element_type=jnp.float32,
        )
        label = labels[here, :]
        is_target = target_mask(first, label, step, classes)
        powers = jnp.exp(SCALE * cosine)
        others = jnp.where(is_target, 0.0, powers)
        pull = jnp.dot(
            others.astype(jnp.bfloat16), class_ref[...], preferred_element_type=jnp.float32
        )
        pull_ref[at // owned : (at + step) // owned, :owned, :] = pull.astype(
            jnp.bfloat16
        ).reshape(step // owned, owned, width)
        cos_t = jnp.sum(jnp.where(is_target, cosine, 0.0), axis=1, keepdims=True)
        logit, slope = target_terms(cos_t)
        others_ref[here, :] = jnp.where(is_target, -(slope + MARK), powers)
        mine = ((label >= first) & (label < first + classes))[:, :1]
        power_t = jnp.where(mine, jnp.exp(logit), 0.0)
        sums = packed_columns(jnp.sum(others, axis=1, keepdims=True), power_t)
        sums = jnp.transpose(sums)[:8].astype(jnp.bfloat16)
        for peer in range(peers):
            pull_ref[peer, owned:, here] = sums


def cosines(place, units, class_unit, labels, peers):
    faces, width = units.shape
    classes = class_unit.shape[0]
    return call(
        cosine_kernel,
        "cosines",
        (place, units, class_unit, labels),
        [
            ((peers, faces // peers + 8, width), jnp.bfloat16),
            ((faces, classes), jnp.float32),
        ],
    )


def raw_grad_kernel(
    loss_weight, place_ref, pulls_ref, raw_ref, target_ref, sent_ref, scales_ref
):
    owned, width = raw_ref.shape
    pulls = pulls_ref[0].astype(jnp.float32)
    for peer in range(1, pulls_ref.shape[0]):
        pulls = pulls + pulls_ref[peer].astype(jnp.float32)
    sums = jnp.concatenate([pulls[owned:], jnp.zeros((LANES - 8, width), jnp.float32)], axis=0)
    sums = jnp.transpose(sums)
    rest, power_t = unpacked_column(sums, 0), unpacked_column(sums, 1)
    inverse = loss_weight / (rest + power_t)
    lane = lax.broadcasted_iota(jnp.int32, sums.shape, 1)
    scales_ref[...] = jnp.where(lane == 0, SCALE * inverse, rest * inverse)
    own = pl.ds(pl.multiple_of(lax.div(place_ref[0], 4) * owned, owned), owned)
    scales = scales_ref[own, :]
    pull_scale, rest_scale = scales[:, 0:1], scales[:, 1:2]

    raw_embed, target = raw_ref[...], target_ref[...]
    embed_norm = row_norm(raw_embed)
    unit_f = raw_embed / embed_norm
    unit = unit_f.astype(jnp.bfloat16).astype(jnp.float32)
    _, slope = target_terms(jnp.sum(unit * target, axis=1, keepdims=True))
    unit_grad = pulls[:owned] * pull_scale - target * (rest_scale * slope)
    raw_grad = (
        unit_grad - unit_f * jnp.sum(unit_f * unit_grad, axis=1, keepdims=True)
    ) / embed_norm
    raw_grad = raw_grad.astype(jnp.bfloat16)
    for copy in range(sent_ref.shape[0]):
        sent_ref[copy] = raw_grad


def raw_grads(loss_weight, place, pulls, raw_embed, target_unit):
    peers = pulls.shape[0]
    owned, width = raw_embed.shape
    return call(
        functools.partial(raw_grad_kernel, loss_weight),
        "raw_grads",
        (place, pulls, raw_embed, target_unit),
        [((peers, owned, width), jnp.bfloat16), ((peers * owned, LANES), jnp.float32)],
    )


def block_sizes(inputs, width, blocks):
    rows = inputs // (2 * blocks * 8) * 8
    return rows, width // LANES, 2 * blocks * rows


def parts_kernel(
    other_half, other_parity,
    place_ref, features_ref, grads_ref, scales_ref, units_ref, others_ref, class_ref, out_ref
):
    some = out_ref.shape[0]
    classes, width = class_ref.shape
    inputs = features_ref.shape[0]
    rows, groups, main = block_sizes(inputs, width, 2 * some)
    base = groups * rows
    half, parity = half_of(place_ref, other_half), parity_of(place_ref, other_parity)
    quarter = 2 * half + parity
    grads = grads_ref[...]

    first = pl.multiple_of(quarter * (some * rows), LANES)
    part = jnp.dot(
        features_ref[pl.ds(first, some * rows), :], grads, preferred_element_type=jnp.float32
    )
    part = part.astype(out_ref.dtype).reshape(some, rows, width)
    for group in range(groups):
        out_ref[:, group * rows : (group + 1) * rows, :] = part[
            :, :, group * LANES : (group + 1) * LANES
        ]

    scales = scales_ref[...]
    pull_scale, rest_scale = scales[:, 0:1], scales[:, 1:2]
    count = classes // 4
    first = pl.multiple_of(quarter * count, LANES)
    others = others_ref[:, pl.ds(first, count)]
    cos_grad = jnp.where(others < 0.0, (others + MARK) * rest_scale, others * pull_scale)
    part = across(cos_grad.astype(jnp.bfloat16), units_ref[...])
    class_f = class_ref[pl.ds(first, count), :].astype(jnp.float32)
    class_norm = row_norm(class_f)
    class_unit = class_f / class_norm
    part = part - class_unit * jnp.sum(class_unit * part, axis=1, keepdims=True)
    part = (part / class_norm).astype(out_ref.dtype).reshape(some, 8, width)
    for group in range(groups):
        out_ref[:, base + group * 8 : base + (group + 1) * 8, :] = part[
            :, :, group * LANES : (group + 1) * LANES
        ]

    each = (inputs - main) // 2
    over = jnp.dot(
        features_ref[pl.ds(pl.multiple_of(main + half * each, each), each), :],
        grads,
        preferred_element_type=jnp.float32,
    ).astype(out_ref.dtype)
    strip = jnp.where(parity == 0, over[:8], over[8:])
    for group in range(groups):
        out_ref[group, base + groups * 8 :, :] = strip[:, group * LANES : (group + 1) * LANES]
    out_ref[groups:, base + groups * 8 :, :] = jnp.zeros((some - groups, 8, LANES), out_ref.dtype)


def parts(quarter, place, dtype, blocks, features, grads, scales, units, others, class_weight):
    width = class_weight.shape[1]
    rows, groups, _ = block_sizes(features.shape[0], width, blocks)
    return call(
        functools.partial(parts_kernel, *quarter),
        "parts",
        (place, features, grads, scales, units, others, class_weight),
        [((blocks // 2, groups * (rows + 8) + 8, LANES), dtype)],
    )[0]


def assemble_kernel(pieces, blocks, place_ref, *refs):
    sources = refs[: len(pieces)]
    fc_ref, class_ref, fc_rows, class_rows, over_rows, sems = refs[-6:]
    inputs, width = fc_ref.shape
    rows, groups, main = block_sizes(inputs, width, blocks)
    each = (inputs - main) // 2
    base = groups * rows
    some = blocks // 2
    copies = []
    done = 0

    def send(source, target, at, size):
        copies.append(
            pltpu.make_async_copy(
                source, target.at[pl.ds(pl.multiple_of(at, 8), size), :], sems.at[len(copies)]
            )
        )
        copies[-1].start()

    for number, (piece, source) in enumerate(zip(pieces, sources)):
        half, parity = half_of(place_ref, piece[0]), parity_of(place_ref, piece[1])
        count = source.shape[0]
        block = (2 * half + parity) * some
        fc_here = slice(done * rows, (done + count) * rows)
        class_here = slice(done * 8, (done + count) * 8)
        for group in range(groups):
            lanes = slice(group * LANES, (group + 1) * LANES)
            values = source[:, group * rows : (group + 1) * rows, :].astype(jnp.float32)
            fc_rows[fc_here, lanes] = values.reshape(count * rows, LANES).astype(jnp.bfloat16)
            values = source[:, base + group * 8 : base + (group + 1) * 8, :].astype(jnp.float32)
            class_rows[class_here, lanes] = values.reshape(count * 8, LANES).astype(jnp.bfloat16)
            over_rows[number, :, lanes] = source[group, base + groups * 8 :, :]
        send(fc_rows.at[fc_here, :], fc_ref, block * rows, count * rows)
        send(class_rows.at[class_here, :], class_ref, block * 8, count * 8)
        send(over_rows.at[number], fc_ref, main + half * each + parity * 8, 8)
        done += count
    for copy in copies:
        copy.wait()


def assemble(place, blocks, sizes, pieces, into):
    inputs, classes, width = sizes
    rows, _, _ = block_sizes(inputs, width, blocks)
    total = sum(source.shape[0] for source in pieces.values())
    anywhere = pl.BlockSpec(memory_space=pltpu.HBM)
    return pl.pallas_call(
        functools.partial(assemble_kernel, tuple(pieces), blocks),
        in_specs=[SMEM] + [VMEM] * len(pieces) + [anywhere] * len(into),
        out_specs=[anywhere, anywhere],
        out_shape=[
            jax.ShapeDtypeStruct((inputs, width), jnp.bfloat16),
            jax.ShapeDtypeStruct((classes, width), jnp.bfloat16),
        ],
        scratch_shapes=[
            pltpu.VMEM((total * rows, width), jnp.bfloat16),
            pltpu.VMEM((total * 8, width), jnp.bfloat16),
            pltpu.VMEM((len(pieces), 8, width), jnp.bfloat16),
            pltpu.SemaphoreType.DMA((3 * len(pieces),)),
        ],
        input_output_aliases={1 + len(pieces) + at: at for at in range(len(into))},
        cost_estimate=pl.CostEstimate(
            flops=0, transcendentals=0, bytes_accessed=total * (rows + 8) * width * 8
        ),
        compiler_params=pltpu.CompilerParams(vmem_limit_bytes=LIMIT),
        name="assemble",
    )(place, *[placed(source) for source in pieces.values()], *into)


def shards(features, fc_weight, class_weight, labels):
    faces, inputs = features.shape
    features = features.T
    classes, width = class_weight.shape
    n_cls = lax.axis_size(CLS)
    chips = lax.axis_size(CHIPS)
    blocks = 2 * chips
    loss_weight = 1.0 / math.sqrt(faces * blocks * lax.axis_size("core"))
    place = (lax.axis_index(CLS) * 2 + lax.axis_index("zl")) * 2 + lax.axis_index("core")
    place = place.reshape(1)
    labels = labels.reshape(1, faces)

    sent, class_unit = embed(place, features, fc_weight, class_weight, labels)
    got = exchange(sent, CLS).reshape(n_cls, faces // n_cls, 2 * width)
    got = jnp.sum(got.astype(jnp.float32), axis=0)
    raw_embed, target_unit = got[:, :width], got[:, width:]
    unit = (raw_embed / row_norm(raw_embed)).astype(jnp.bfloat16)
    units = exchange(jnp.broadcast_to(unit, (n_cls,) + unit.shape), CLS)
    units = units.reshape(faces, width)

    pull, others = cosines(place, units, class_unit, labels, n_cls)
    got = exchange(pull, CLS)
    sent, scales = raw_grads(loss_weight, place, got, raw_embed, target_unit)
    grads = exchange(sent, CLS).reshape(faces, width)

    swap = [(0, 1), (1, 0)]
    length = 2 * lax.axis_size("zh")
    pairs = []
    for z in range(length):
        pairs.append((2 * z, 2 * (z ^ 1)))
        pairs.append((2 * z + 1, 2 * ((z + 2 * (z % 2) - 1) % length) + 1))
    neighbour = ("zh", "zl", "core")

    operands = (blocks, features, grads, scales, units, others, class_weight)
    theirs = parts((True, True), place, jnp.bfloat16, *operands)
    theirs = lax.ppermute(theirs, "core", swap)
    sent = parts((False, True), place, jnp.float32, *operands) + theirs.astype(jnp.float32)
    sent, later = lax.optimization_barrier((sent.astype(jnp.bfloat16), place))
    got = lax.ppermute(sent, neighbour, pairs)
    theirs = parts((True, False), later, jnp.bfloat16, *operands)
    theirs = lax.ppermute(theirs, "core", swap)
    mine = parts((False, False), later, jnp.float32, *operands) + got.astype(jnp.float32)
    mine = lax.optimization_barrier(mine)
    mine = (mine + theirs.astype(jnp.float32)).astype(jnp.bfloat16)
    done = jnp.sum(exchange(mine, CHIPS).astype(jnp.float32), axis=0).astype(jnp.bfloat16)

    sizes = (inputs, classes, width)
    mine = exchange(jnp.broadcast_to(done, (chips,) + done.shape), CHIPS)
    next_mine = lax.ppermute(mine, neighbour, pairs)
    across_mine = lax.ppermute(mine, "core", swap)
    written = assemble(place, blocks, sizes, {(False, False): mine}, ())
    next_mine, written = lax.optimization_barrier((next_mine, written))
    across_next = lax.ppermute(next_mine, "core", swap)
    pieces = {(False, True): next_mine, (True, False): across_mine}
    written = assemble(place, blocks, sizes, pieces, written)
    return tuple(assemble(place, blocks, sizes, {(True, True): across_next}, written))


def solution(mesh):
    fine = Mesh(mesh.devices.reshape(4, 2, 4, 2, 4, 2), ("zh", "zl", "yh", "core", "x", "yl"))
    dp = ("zh", "zl", "yh", "core")
    specs = (P(dp, CLS), P(CLS, None), P(CLS, None), P(dp))
    return jax.shard_map(
        shards,
        mesh=fine,
        in_specs=specs,
        out_specs=(P(CLS, None), P(CLS, None)),
        check_vma=False,
    )
```

```python
import functools
import math

import jax
import jax.numpy as jnp
from jax import lax
from jax.experimental import pallas as pl
from jax.experimental.pallas import tpu as pltpu
from jax.sharding import Mesh
from jax.sharding import PartitionSpec as P

SCALE = 64.0
MARGIN = 0.5
SOFTEN = 0.01
EPSILON = 1e-06

CLS = ("x", "yl")
CHIPS = ("zh", "yh")
LANES = 128
CHUNKS = 2
MARK = 1024.0
STEP = 256
LIMIT = 24 << 20
VMEM = pl.BlockSpec(memory_space=pltpu.VMEM)
SMEM = pl.BlockSpec(memory_space=pltpu.SMEM)


def exchange(blocks, axes):
    return lax.all_to_all(blocks, axes, 0, 0, tiled=True)


def across(left, right):
    return lax.dot_general(
        left, right, (((0,), (0,)), ((), ())), preferred_element_type=jnp.float32
    )


def row_norm(values):
    return jnp.sqrt(jnp.sum(values * values, axis=1, keepdims=True) + EPSILON)


def packed_columns(*columns):
    rows = columns[0].shape[0]
    lane = lax.broadcasted_iota(jnp.int32, (rows, LANES), 1)
    block = jnp.zeros((rows, LANES), jnp.float32)
    for at, column in enumerate(columns):
        rest = column
        for part in range(3):
            term = rest.astype(jnp.bfloat16).astype(jnp.float32)
            block = jnp.where(lane == 3 * at + part, term, block)
            rest = rest - term
    return block


def unpacked_column(block, at):
    lane = lax.broadcasted_iota(jnp.int32, block.shape, 1)
    inside = (lane >= 3 * at) & (lane < 3 * at + 3)
    return jnp.sum(jnp.where(inside, block, 0.0), axis=1, keepdims=True)


def placed(array, space=pltpu.VMEM):
    return pltpu.with_memory_space_constraint(array, space)


def half_of(place_ref, other):
    core = lax.rem(place_ref[0], 2)
    return 1 - core if other else core


def parity_of(place_ref, other):
    odd = lax.rem(lax.div(place_ref[0], 2), 2)
    return 1 - odd if other else odd


def first_of(place_ref, classes):
    return lax.div(place_ref[0], 4) * classes


def call(kernel, name, operands, results, **options):
    specs = [SMEM if operand.ndim == 1 else VMEM for operand in operands]
    operands = [operand if operand.ndim == 1 else placed(operand) for operand in operands]
    return pl.pallas_call(
        kernel,
        in_specs=specs,
        out_specs=[VMEM] * len(results),
        out_shape=[pltpu.VMEM(shape, dtype) for shape, dtype in results],
        compiler_params=pltpu.CompilerParams(vmem_limit_bytes=LIMIT),
        name=name,
        **options,
    )(*operands)


def target_mask(first, labels, rows, classes):
    lane = lax.broadcasted_iota(jnp.int32, (rows, LANES), 1)
    return jnp.concatenate(
        [labels == lane + (first + at) for at in range(0, classes, LANES)], axis=1
    )


def spread_labels(labels_row):
    faces = labels_row.shape[1]
    return jnp.transpose(jnp.broadcast_to(labels_row, (LANES, faces)))


def embed_kernel(
    place_ref, features_ref, fc_ref, class_ref, labels_ref, sent_ref, unit_ref,
    left_ref, right_ref, total_ref, weight_ref, row_ref, sems
):
    width = fc_ref.shape[1]
    inputs, faces = features_ref.shape
    classes = class_ref.shape[0]
    ends = [inputs * at // CHUNKS // LANES * LANES for at in range(CHUNKS)] + [inputs]
    copies = [
        pltpu.make_async_copy(labels_ref, row_ref, sems.at[0]),
        pltpu.make_async_copy(class_ref, weight_ref, sems.at[1]),
    ]
    for at in range(CHUNKS):
        rows = pl.ds(ends[at], ends[at + 1] - ends[at])
        for source, target in ((features_ref, left_ref), (fc_ref, right_ref)):
            copies.append(
                pltpu.make_async_copy(
                    source.at[rows, :], target.at[rows, :], sems.at[len(copies)]
                )
            )
    for copy in copies:
        copy.start()

    copies[0].wait()
    labels = spread_labels(row_ref[...])
    chosen = target_mask(first_of(place_ref, classes), labels, faces, classes)
    chosen = jnp.where(chosen, 1.0, 0.0).astype(jnp.bfloat16)
    copies[1].wait()
    class_f = weight_ref[...].astype(jnp.float32)
    unit_ref[...] = (class_f * (1.0 / row_norm(class_f))).astype(jnp.bfloat16)
    target_part = jnp.dot(chosen, unit_ref[...], preferred_element_type=jnp.float32)
    sent_ref[:, width:] = target_part.astype(jnp.bfloat16)

    for at in range(CHUNKS):
        copies[2 + 2 * at].wait()
        copies[3 + 2 * at].wait()
        here = slice(ends[at], ends[at + 1])
        part = across(left_ref[here, :], right_ref[here, :])
        if at > 0:
            part = part + total_ref[...]
        if at < CHUNKS - 1:
            total_ref[...] = part
        else:
            sent_ref[:, :width] = part.astype(jnp.bfloat16)


def embed(place, features, fc_weight, class_weight, labels):
    inputs, faces = features.shape
    classes, width = class_weight.shape
    arrays = [placed(array, pltpu.HBM) for array in (features, fc_weight, class_weight, labels)]
    return pl.pallas_call(
        embed_kernel,
        in_specs=[SMEM] + [pl.BlockSpec(memory_space=pltpu.HBM)] * len(arrays),
        out_specs=[VMEM, VMEM],
        out_shape=[
            pltpu.VMEM((faces, 2 * width), jnp.bfloat16),
            pltpu.VMEM((classes, width), jnp.bfloat16),
        ],
        scratch_shapes=[
            pltpu.VMEM((inputs, faces), jnp.bfloat16),
            pltpu.VMEM((inputs, width), jnp.bfloat16),
            pltpu.VMEM((faces, width), jnp.float32),
            pltpu.VMEM((classes, width), jnp.bfloat16),
            pltpu.VMEM((1, faces), jnp.int32),
            pltpu.SemaphoreType.DMA((2 + 2 * CHUNKS,)),
        ],
        compiler_params=pltpu.CompilerParams(vmem_limit_bytes=LIMIT),
        name="embed",
    )(place, *arrays)


def units_kernel(got_ref, raw_ref, target_ref, sent_ref):
    width = raw_ref.shape[1]
    got = got_ref[0].astype(jnp.float32)
    for peer in range(1, got_ref.shape[0]):
        got = got + got_ref[peer].astype(jnp.float32)
    raw_embed = got[:, :width]
    raw_ref[...] = raw_embed
    target_ref[...] = got[:, width:]
    unit = (raw_embed * (1.0 / row_norm(raw_embed))).astype(jnp.bfloat16)
    for copy in range(sent_ref.shape[0]):
        sent_ref[copy] = unit


def unit_rows(got):
    peers, owned, both = got.shape
    rows = (owned, both // 2)
    return call(
        units_kernel,
        "units",
        (got,),
        [(rows, jnp.float32), (rows, jnp.float32), ((peers,) + rows, jnp.bfloat16)],
    )


def target_terms(cosine):
    sine = jnp.sqrt(1.0 + SOFTEN - cosine * cosine)
    logit = SCALE * (cosine * math.cos(MARGIN) - sine * math.sin(MARGIN))
    slope = SCALE * (math.cos(MARGIN) + math.sin(MARGIN) * cosine / sine)
    return logit, slope


def cosine_kernel(place_ref, units_ref, class_ref, labels_ref, pull_ref, others_ref):
    faces, width = units_ref.shape
    classes = class_ref.shape[0]
    peers = pull_ref.shape[0]
    owned = faces // peers
    step = STEP
    first = first_of(place_ref, classes)
    labels = spread_labels(labels_ref[...])
    for at in range(0, faces, step):
        here = slice(at, at + step)
        cosine = lax.dot_general(
            units_ref[here, :],
            class_ref[...],
            (((1,), (1,)), ((), ())),
            preferred_element_type=jnp.float32,
        )
        label = labels[here, :]
        is_target = target_mask(first, label, step, classes)
        powers = jnp.exp(SCALE * cosine)
        others = jnp.where(is_target, 0.0, powers)
        pull = jnp.dot(
            others.astype(jnp.bfloat16), class_ref[...], preferred_element_type=jnp.float32
        )
        pull_ref[at // owned : (at + step) // owned, :owned, :] = pull.astype(
            jnp.bfloat16
        ).reshape(step // owned, owned, width)
        cos_t = jnp.sum(jnp.where(is_target, cosine, 0.0), axis=1, keepdims=True)
        logit, slope = target_terms(cos_t)
        others_ref[here, :] = jnp.where(is_target, -(slope + MARK), powers)
        mine = ((label >= first) & (label < first + classes))[:, :1]
        power_t = jnp.where(mine, jnp.exp(logit), 0.0)
        sums = packed_columns(jnp.sum(others, axis=1, keepdims=True), power_t)
        sums = jnp.transpose(sums)[:8].astype(jnp.bfloat16)
        for peer in range(peers):
            pull_ref[peer, owned:, here] = sums


def cosines(place, units, class_unit, labels, peers):
    faces, width = units.shape
    classes = class_unit.shape[0]
    return call(
        cosine_kernel,
        "cosines",
        (place, units, class_unit, labels),
        [
            ((peers, faces // peers + 8, width), jnp.bfloat16),
            ((faces, classes), jnp.float32),
        ],
    )


def raw_grad_kernel(
    loss_weight, place_ref, pulls_ref, raw_ref, target_ref, sent_ref, scales_ref
):
    owned, width = raw_ref.shape
    pulls = pulls_ref[0].astype(jnp.float32)
    for peer in range(1, pulls_ref.shape[0]):
        pulls = pulls + pulls_ref[peer].astype(jnp.float32)
    sums = jnp.concatenate([pulls[owned:], jnp.zeros((LANES - 8, width), jnp.float32)], axis=0)
    sums = jnp.transpose(sums)
    rest, power_t = unpacked_column(sums, 0), unpacked_column(sums, 1)
    inverse = loss_weight / (rest + power_t)
    lane = lax.broadcasted_iota(jnp.int32, sums.shape, 1)
    scales_ref[...] = jnp.where(lane == 0, SCALE * inverse, rest * inverse)
    own = pl.ds(pl.multiple_of(lax.div(place_ref[0], 4) * owned, owned), owned)
    scales = scales_ref[own, :]
    pull_scale, rest_scale = scales[:, 0:1], scales[:, 1:2]

    raw_embed, target = raw_ref[...], target_ref[...]
    inverse_norm = 1.0 / row_norm(raw_embed)
    unit_f = raw_embed * inverse_norm
    unit = unit_f.astype(jnp.bfloat16).astype(jnp.float32)
    _, slope = target_terms(jnp.sum(unit * target, axis=1, keepdims=True))
    unit_grad = pulls[:owned] * pull_scale - target * (rest_scale * slope)
    raw_grad = (
        unit_grad - unit_f * jnp.sum(unit_f * unit_grad, axis=1, keepdims=True)
    ) * inverse_norm
    raw_grad = raw_grad.astype(jnp.bfloat16)
    for copy in range(sent_ref.shape[0]):
        sent_ref[copy] = raw_grad


def raw_grads(loss_weight, place, pulls, raw_embed, target_unit):
    peers = pulls.shape[0]
    owned, width = raw_embed.shape
    return call(
        functools.partial(raw_grad_kernel, loss_weight),
        "raw_grads",
        (place, pulls, raw_embed, target_unit),
        [((peers, owned, width), jnp.bfloat16), ((peers * owned, LANES), jnp.float32)],
    )


def block_sizes(inputs, width, blocks):
    rows = inputs // (2 * blocks * 8) * 8
    return rows, width // LANES, 2 * blocks * rows


def parts_kernel(
    other_half, other_parity,
    place_ref, features_ref, grads_ref, scales_ref, units_ref, others_ref, class_ref, out_ref
):
    some = out_ref.shape[0]
    classes, width = class_ref.shape
    inputs = features_ref.shape[0]
    rows, groups, main = block_sizes(inputs, width, 2 * some)
    base = groups * rows
    half, parity = half_of(place_ref, other_half), parity_of(place_ref, other_parity)
    quarter = 2 * half + parity
    grads = grads_ref[...]

    first = pl.multiple_of(quarter * (some * rows), LANES)
    part = jnp.dot(
        features_ref[pl.ds(first, some * rows), :], grads, preferred_element_type=jnp.float32
    )
    part = part.astype(out_ref.dtype).reshape(some, rows, width)
    for group in range(groups):
        out_ref[:, group * rows : (group + 1) * rows, :] = part[
            :, :, group * LANES : (group + 1) * LANES
        ]

    scales = scales_ref[...]
    pull_scale, rest_scale = scales[:, 0:1], scales[:, 1:2]
    count = classes // 4
    first = pl.multiple_of(quarter * count, LANES)
    others = others_ref[:, pl.ds(first, count)]
    cos_grad = jnp.where(others < 0.0, (others + MARK) * rest_scale, others * pull_scale)
    part = across(cos_grad.astype(jnp.bfloat16), units_ref[...])
    class_f = class_ref[pl.ds(first, count), :].astype(jnp.float32)
    inverse = 1.0 / row_norm(class_f)
    along = jnp.sum(class_f * part, axis=1, keepdims=True) * (inverse * inverse)
    part = ((part - class_f * along) * inverse).astype(out_ref.dtype).reshape(some, 8, width)
    for group in range(groups):
        out_ref[:, base + group * 8 : base + (group + 1) * 8, :] = part[
            :, :, group * LANES : (group + 1) * LANES
        ]

    each = (inputs - main) // 2
    over = jnp.dot(
        features_ref[pl.ds(pl.multiple_of(main + half * each, each), each), :],
        grads,
        preferred_element_type=jnp.float32,
    ).astype(out_ref.dtype)
    strip = jnp.where(parity == 0, over[:8], over[8:])
    for group in range(groups):
        out_ref[group, base + groups * 8 :, :] = strip[:, group * LANES : (group + 1) * LANES]
    out_ref[groups:, base + groups * 8 :, :] = jnp.zeros((some - groups, 8, LANES), out_ref.dtype)


def parts(quarter, place, dtype, blocks, features, grads, scales, units, others, class_weight):
    width = class_weight.shape[1]
    rows, groups, _ = block_sizes(features.shape[0], width, blocks)
    return call(
        functools.partial(parts_kernel, *quarter),
        "parts",
        (place, features, grads, scales, units, others, class_weight),
        [((blocks // 2, groups * (rows + 8) + 8, LANES), dtype)],
    )[0]


def assemble_kernel(pieces, blocks, place_ref, *refs):
    sources = refs[: len(pieces)]
    fc_ref, class_ref, fc_rows, class_rows, over_rows, sems = refs[-6:]
    inputs, width = fc_ref.shape
    rows, groups, main = block_sizes(inputs, width, blocks)
    each = (inputs - main) // 2
    base = groups * rows
    some = blocks // 2
    copies = []
    done = 0

    def send(source, target, at, size):
        copies.append(
            pltpu.make_async_copy(
                source, target.at[pl.ds(pl.multiple_of(at, 8), size), :], sems.at[len(copies)]
            )
        )
        copies[-1].start()

    for number, (piece, source) in enumerate(zip(pieces, sources)):
        half, parity = half_of(place_ref, piece[0]), parity_of(place_ref, piece[1])
        count = source.shape[0]
        block = (2 * half + parity) * some
        for at in range(0, count, count // 2):
            fc_here = slice((done + at) * rows, (done + at + count // 2) * rows)
            for group in range(groups):
                values = source[
                    at : at + count // 2, group * rows : (group + 1) * rows, :
                ].astype(jnp.float32)
                fc_rows[fc_here, group * LANES : (group + 1) * LANES] = values.reshape(
                    count // 2 * rows, LANES
                ).astype(jnp.bfloat16)
            send(fc_rows.at[fc_here, :], fc_ref, (block + at) * rows, count // 2 * rows)
        class_here = slice(done * 8, (done + count) * 8)
        for group in range(groups):
            lanes = slice(group * LANES, (group + 1) * LANES)
            values = source[:, base + group * 8 : base + (group + 1) * 8, :].astype(jnp.float32)
            class_rows[class_here, lanes] = values.reshape(count * 8, LANES).astype(jnp.bfloat16)
            over_rows[number, :, lanes] = source[group, base + groups * 8 :, :]
        send(class_rows.at[class_here, :], class_ref, block * 8, count * 8)
        send(over_rows.at[number], fc_ref, main + half * each + parity * 8, 8)
        done += count
    for copy in copies:
        copy.wait()


def assemble(place, blocks, sizes, pieces, into):
    inputs, classes, width = sizes
    rows, _, _ = block_sizes(inputs, width, blocks)
    total = sum(source.shape[0] for source in pieces.values())
    anywhere = pl.BlockSpec(memory_space=pltpu.HBM)
    return pl.pallas_call(
        functools.partial(assemble_kernel, tuple(pieces), blocks),
        in_specs=[SMEM] + [VMEM] * len(pieces) + [anywhere] * len(into),
        out_specs=[anywhere, anywhere],
        out_shape=[
            jax.ShapeDtypeStruct((inputs, width), jnp.bfloat16),
            jax.ShapeDtypeStruct((classes, width), jnp.bfloat16),
        ],
        scratch_shapes=[
            pltpu.VMEM((total * rows, width), jnp.bfloat16),
            pltpu.VMEM((total * 8, width), jnp.bfloat16),
            pltpu.VMEM((len(pieces), 8, width), jnp.bfloat16),
            pltpu.SemaphoreType.DMA((4 * len(pieces),)),
        ],
        input_output_aliases={1 + len(pieces) + at: at for at in range(len(into))},
        cost_estimate=pl.CostEstimate(
            flops=0, transcendentals=0, bytes_accessed=total * (rows + 8) * width * 8
        ),
        compiler_params=pltpu.CompilerParams(vmem_limit_bytes=LIMIT),
        name="assemble",
    )(place, *[placed(source) for source in pieces.values()], *into)


def shards(features, fc_weight, class_weight, labels):
    faces, inputs = features.shape
    features = features.T
    classes, width = class_weight.shape
    n_cls = lax.axis_size(CLS)
    chips = lax.axis_size(CHIPS)
    blocks = 2 * chips
    loss_weight = 1.0 / math.sqrt(faces * blocks * lax.axis_size("core"))
    place = (lax.axis_index(CLS) * 2 + lax.axis_index("zl")) * 2 + lax.axis_index("core")
    place = place.reshape(1)
    labels = labels.reshape(1, faces)

    sent, class_unit = embed(place, features, fc_weight, class_weight, labels)
    got = exchange(sent, CLS).reshape(n_cls, faces // n_cls, 2 * width)
    raw_embed, target_unit, sent = unit_rows(got)
    units = exchange(sent, CLS)
    units = units.reshape(faces, width)

    pull, others = cosines(place, units, class_unit, labels, n_cls)
    got = exchange(pull, CLS)
    sent, scales = raw_grads(loss_weight, place, got, raw_embed, target_unit)
    grads = exchange(sent, CLS).reshape(faces, width)

    swap = [(0, 1), (1, 0)]
    length = 2 * lax.axis_size("zh")
    pairs = []
    for z in range(length):
        pairs.append((2 * z, 2 * (z ^ 1)))
        pairs.append((2 * z + 1, 2 * ((z + 2 * (z % 2) - 1) % length) + 1))
    neighbour = ("zh", "zl", "core")

    operands = (blocks, features, grads, scales, units, others, class_weight)
    theirs = parts((True, True), place, jnp.bfloat16, *operands)
    theirs = lax.ppermute(theirs, "core", swap)
    sent = parts((False, True), place, jnp.float32, *operands) + theirs.astype(jnp.float32)
    sent, later = lax.optimization_barrier((sent.astype(jnp.bfloat16), place))
    got = lax.ppermute(sent, neighbour, pairs)
    theirs = parts((True, False), later, jnp.bfloat16, *operands)
    theirs = lax.ppermute(theirs, "core", swap)
    mine = parts((False, False), later, jnp.float32, *operands) + got.astype(jnp.float32)
    mine = lax.optimization_barrier(mine)
    mine = (mine + theirs.astype(jnp.float32)).astype(jnp.bfloat16)
    done = jnp.sum(exchange(mine, CHIPS).astype(jnp.float32), axis=0).astype(jnp.bfloat16)

    sizes = (inputs, classes, width)
    mine = exchange(jnp.broadcast_to(done, (chips,) + done.shape), CHIPS)
    next_mine = lax.ppermute(mine, neighbour, pairs)
    across_mine = lax.ppermute(mine, "core", swap)
    written = assemble(place, blocks, sizes, {(False, False): mine}, ())
    next_mine, written = lax.optimization_barrier((next_mine, written))
    across_next = lax.ppermute(next_mine, "core", swap)
    pieces = {(False, True): next_mine, (True, False): across_mine}
    written = assemble(place, blocks, sizes, pieces, written)
    return tuple(assemble(place, blocks, sizes, {(True, True): across_next}, written))


def solution(mesh):
    fine = Mesh(mesh.devices.reshape(4, 2, 4, 2, 4, 2), ("zh", "zl", "yh", "core", "x", "yl"))
    dp = ("zh", "zl", "yh", "core")
    specs = (P(dp, CLS), P(CLS, None), P(CLS, None), P(dp))
    return jax.shard_map(
        shards,
        mesh=fine,
        in_specs=specs,
        out_specs=(P(CLS, None), P(CLS, None)),
        check_vma=False,
    )
```

```python
import functools
import math

import jax
import jax.numpy as jnp
from jax import lax
from jax.experimental import pallas as pl
from jax.experimental.pallas import tpu as pltpu
from jax.sharding import Mesh
from jax.sharding import PartitionSpec as P

SCALE = 64.0
MARGIN = 0.5
SOFTEN = 0.01
EPSILON = 1e-06

CLS = ("x", "yl")
CHIPS = ("zh", "yh")
LANES = 128
CHUNKS = 2
MARK = 1024.0
STEP = 256
LIMIT = 24 << 20
VMEM = pl.BlockSpec(memory_space=pltpu.VMEM)
SMEM = pl.BlockSpec(memory_space=pltpu.SMEM)


def exchange(blocks, axes):
    return lax.all_to_all(blocks, axes, 0, 0, tiled=True)


def across(left, right):
    return lax.dot_general(
        left, right, (((0,), (0,)), ((), ())), preferred_element_type=jnp.float32
    )


def row_norm(values):
    return jnp.sqrt(jnp.sum(values * values, axis=1, keepdims=True) + EPSILON)


def packed_columns(*columns):
    rows = columns[0].shape[0]
    lane = lax.broadcasted_iota(jnp.int32, (rows, LANES), 1)
    block = jnp.zeros((rows, LANES), jnp.float32)
    for at, column in enumerate(columns):
        rest = column
        for part in range(3):
            term = rest.astype(jnp.bfloat16).astype(jnp.float32)
            block = jnp.where(lane == 3 * at + part, term, block)
            rest = rest - term
    return block


def unpacked_column(block, at):
    lane = lax.broadcasted_iota(jnp.int32, block.shape, 1)
    inside = (lane >= 3 * at) & (lane < 3 * at + 3)
    return jnp.sum(jnp.where(inside, block, 0.0), axis=1, keepdims=True)


def placed(array, space=pltpu.VMEM):
    return pltpu.with_memory_space_constraint(array, space)


def half_of(place_ref, other):
    core = lax.rem(place_ref[0], 2)
    return 1 - core if other else core


def parity_of(place_ref, other):
    odd = lax.rem(lax.div(place_ref[0], 2), 2)
    return 1 - odd if other else odd


def first_of(place_ref, classes):
    return lax.div(place_ref[0], 4) * classes


def call(kernel, name, operands, results, **options):
    specs = [SMEM if operand.ndim == 1 else VMEM for operand in operands]
    operands = [operand if operand.ndim == 1 else placed(operand) for operand in operands]
    return pl.pallas_call(
        kernel,
        in_specs=specs,
        out_specs=[VMEM] * len(results),
        out_shape=[pltpu.VMEM(shape, dtype) for shape, dtype in results],
        compiler_params=pltpu.CompilerParams(vmem_limit_bytes=LIMIT),
        name=name,
        **options,
    )(*operands)


def target_mask(first, labels, rows, classes):
    lane = lax.broadcasted_iota(jnp.int32, (rows, LANES), 1)
    return jnp.concatenate(
        [labels == lane + (first + at) for at in range(0, classes, LANES)], axis=1
    )


def spread_labels(labels_row):
    faces = labels_row.shape[1]
    return jnp.transpose(jnp.broadcast_to(labels_row, (LANES, faces)))


def bit_of(place_ref, level):
    return lax.rem(lax.div(place_ref[0], 4 << level), 2)


def targets_kernel(place_ref, class_ref, labels_ref, keep_ref, send_ref, unit_ref, rows_ref):
    classes, width = class_ref.shape
    faces = labels_ref.shape[1]
    class_f = class_ref[...].astype(jnp.float32)
    unit_ref[...] = (class_f * (1.0 / row_norm(class_f))).astype(jnp.bfloat16)
    labels = spread_labels(labels_ref[...])
    chosen = target_mask(first_of(place_ref, classes), labels, faces, classes)
    chosen = jnp.where(chosen, 1.0, 0.0).astype(jnp.bfloat16)
    rows = jnp.dot(chosen, unit_ref[...], preferred_element_type=jnp.float32)
    rows_ref[...] = rows.astype(jnp.bfloat16).reshape(rows_ref.shape)
    bit = bit_of(place_ref, 0)
    for at in range(keep_ref.shape[0]):
        keep_ref[at] = rows_ref[2 * at + bit]
        send_ref[at] = rows_ref[2 * at + 1 - bit]


def target_rows(place, class_weight, labels, peers):
    classes, width = class_weight.shape
    faces = labels.shape[1]
    half = ((peers // 2, faces // peers, width), jnp.bfloat16)
    return call(
        targets_kernel,
        "targets",
        (place, class_weight, labels),
        [half, half, ((classes, width), jnp.bfloat16)],
        scratch_shapes=[pltpu.VMEM((peers, faces // peers, width), jnp.bfloat16)],
    )


def halve_kernel(level, place_ref, kept_ref, got_ref, keep_ref, send_ref):
    bit = bit_of(place_ref, level)
    for at in range(keep_ref.shape[0]):
        keep_ref[at] = kept_ref[2 * at + bit] + got_ref[2 * at + bit]
        send_ref[at] = kept_ref[2 * at + 1 - bit] + got_ref[2 * at + 1 - bit]


def halve(level, place, kept, got):
    half = ((kept.shape[0] // 2,) + kept.shape[1:], kept.dtype)
    return call(
        functools.partial(halve_kernel, level), "halve", (place, kept, got), [half, half]
    )


def embed_kernel(features_ref, fc_ref, sent_ref, left_ref, right_ref, total_ref, sems):
    inputs = features_ref.shape[0]
    ends = [inputs * at // CHUNKS // LANES * LANES for at in range(CHUNKS)] + [inputs]
    copies = []
    for at in range(CHUNKS):
        rows = pl.ds(ends[at], ends[at + 1] - ends[at])
        for source, target in ((features_ref, left_ref), (fc_ref, right_ref)):
            copies.append(
                pltpu.make_async_copy(
                    source.at[rows, :], target.at[rows, :], sems.at[len(copies)]
                )
            )
    for copy in copies:
        copy.start()
    for at in range(CHUNKS):
        copies[2 * at].wait()
        copies[2 * at + 1].wait()
        here = slice(ends[at], ends[at + 1])
        part = across(left_ref[here, :], right_ref[here, :])
        if at > 0:
            part = part + total_ref[...]
        if at < CHUNKS - 1:
            total_ref[...] = part
        else:
            sent_ref[...] = part.astype(jnp.bfloat16)


def embed(features, fc_weight):
    inputs, faces = features.shape
    width = fc_weight.shape[1]
    arrays = [placed(array, pltpu.HBM) for array in (features, fc_weight)]
    return pl.pallas_call(
        embed_kernel,
        in_specs=[pl.BlockSpec(memory_space=pltpu.HBM)] * len(arrays),
        out_specs=VMEM,
        out_shape=pltpu.VMEM((faces, width), jnp.bfloat16),
        scratch_shapes=[
            pltpu.VMEM((inputs, faces), jnp.bfloat16),
            pltpu.VMEM((inputs, width), jnp.bfloat16),
            pltpu.VMEM((faces, width), jnp.float32),
            pltpu.SemaphoreType.DMA((2 * CHUNKS,)),
        ],
        compiler_params=pltpu.CompilerParams(vmem_limit_bytes=LIMIT),
        name="embed",
    )(*arrays)


def units_kernel(got_ref, raw_ref, sent_ref):
    raw_embed = got_ref[0].astype(jnp.float32)
    for peer in range(1, got_ref.shape[0]):
        raw_embed = raw_embed + got_ref[peer].astype(jnp.float32)
    raw_ref[...] = raw_embed
    unit = (raw_embed * (1.0 / row_norm(raw_embed))).astype(jnp.bfloat16)
    for copy in range(sent_ref.shape[0]):
        sent_ref[copy] = unit


def unit_rows(got):
    rows = got.shape[1:]
    return call(
        units_kernel, "units", (got,), [(rows, jnp.float32), (got.shape, jnp.bfloat16)]
    )


def target_terms(cosine):
    sine = jnp.sqrt(1.0 + SOFTEN - cosine * cosine)
    logit = SCALE * (cosine * math.cos(MARGIN) - sine * math.sin(MARGIN))
    slope = SCALE * (math.cos(MARGIN) + math.sin(MARGIN) * cosine / sine)
    return logit, slope


def cosine_kernel(place_ref, units_ref, class_ref, labels_ref, pull_ref, others_ref):
    faces, width = units_ref.shape
    classes = class_ref.shape[0]
    peers = pull_ref.shape[0]
    owned = faces // peers
    step = STEP
    first = first_of(place_ref, classes)
    labels = spread_labels(labels_ref[...])
    for at in range(0, faces, step):
        here = slice(at, at + step)
        cosine = lax.dot_general(
            units_ref[here, :],
            class_ref[...],
            (((1,), (1,)), ((), ())),
            preferred_element_type=jnp.float32,
        )
        label = labels[here, :]
        is_target = target_mask(first, label, step, classes)
        powers = jnp.exp(SCALE * cosine)
        others = jnp.where(is_target, 0.0, powers)
        pull = jnp.dot(
            others.astype(jnp.bfloat16), class_ref[...], preferred_element_type=jnp.float32
        )
        pull_ref[at // owned : (at + step) // owned, :owned, :] = pull.astype(
            jnp.bfloat16
        ).reshape(step // owned, owned, width)
        cos_t = jnp.sum(jnp.where(is_target, cosine, 0.0), axis=1, keepdims=True)
        logit, slope = target_terms(cos_t)
        others_ref[here, :] = jnp.where(is_target, -(slope + MARK), powers)
        mine = ((label >= first) & (label < first + classes))[:, :1]
        power_t = jnp.where(mine, jnp.exp(logit), 0.0)
        sums = packed_columns(jnp.sum(others, axis=1, keepdims=True), power_t)
        sums = jnp.transpose(sums)[:8].astype(jnp.bfloat16)
        for peer in range(peers):
            pull_ref[peer, owned:, here] = sums


def cosines(place, units, class_unit, labels, peers):
    faces, width = units.shape
    classes = class_unit.shape[0]
    return call(
        cosine_kernel,
        "cosines",
        (place, units, class_unit, labels),
        [
            ((peers, faces // peers + 8, width), jnp.bfloat16),
            ((faces, classes), jnp.float32),
        ],
    )


def raw_grad_kernel(
    loss_weight, place_ref, pulls_ref, raw_ref, kept_ref, got_ref, sent_ref, scales_ref
):
    owned, width = raw_ref.shape
    pulls = pulls_ref[0].astype(jnp.float32)
    for peer in range(1, pulls_ref.shape[0]):
        pulls = pulls + pulls_ref[peer].astype(jnp.float32)
    sums = jnp.concatenate([pulls[owned:], jnp.zeros((LANES - 8, width), jnp.float32)], axis=0)
    sums = jnp.transpose(sums)
    rest, power_t = unpacked_column(sums, 0), unpacked_column(sums, 1)
    inverse = loss_weight / (rest + power_t)
    lane = lax.broadcasted_iota(jnp.int32, sums.shape, 1)
    scales_ref[...] = jnp.where(lane == 0, SCALE * inverse, rest * inverse)
    own = pl.ds(pl.multiple_of(lax.div(place_ref[0], 4) * owned, owned), owned)
    scales = scales_ref[own, :]
    pull_scale, rest_scale = scales[:, 0:1], scales[:, 1:2]

    raw_embed = raw_ref[...]
    target = (kept_ref[0] + got_ref[0]).astype(jnp.float32)
    inverse_norm = 1.0 / row_norm(raw_embed)
    unit_f = raw_embed * inverse_norm
    unit = unit_f.astype(jnp.bfloat16).astype(jnp.float32)
    _, slope = target_terms(jnp.sum(unit * target, axis=1, keepdims=True))
    unit_grad = pulls[:owned] * pull_scale - target * (rest_scale * slope)
    raw_grad = (
        unit_grad - unit_f * jnp.sum(unit_f * unit_grad, axis=1, keepdims=True)
    ) * inverse_norm
    raw_grad = raw_grad.astype(jnp.bfloat16)
    for copy in range(sent_ref.shape[0]):
        sent_ref[copy] = raw_grad


def raw_grads(loss_weight, place, pulls, raw_embed, kept, got):
    peers = pulls.shape[0]
    owned, width = raw_embed.shape
    return call(
        functools.partial(raw_grad_kernel, loss_weight),
        "raw_grads",
        (place, pulls, raw_embed, kept, got),
        [((peers, owned, width), jnp.bfloat16), ((peers * owned, LANES), jnp.float32)],
    )


def block_sizes(inputs, width, blocks):
    rows = inputs // (2 * blocks * 8) * 8
    return rows, width // LANES, 2 * blocks * rows


def parts_kernel(
    other_half, other_parity,
    place_ref, features_ref, grads_ref, scales_ref, units_ref, others_ref, class_ref, out_ref
):
    some = out_ref.shape[0]
    classes, width = class_ref.shape
    inputs = features_ref.shape[0]
    rows, groups, main = block_sizes(inputs, width, 2 * some)
    base = groups * rows
    half, parity = half_of(place_ref, other_half), parity_of(place_ref, other_parity)
    quarter = 2 * half + parity
    grads = grads_ref[...]

    first = pl.multiple_of(quarter * (some * rows), LANES)
    part = jnp.dot(
        features_ref[pl.ds(first, some * rows), :], grads, preferred_element_type=jnp.float32
    )
    part = part.astype(out_ref.dtype).reshape(some, rows, width)
    for group in range(groups):
        out_ref[:, group * rows : (group + 1) * rows, :] = part[
            :, :, group * LANES : (group + 1) * LANES
        ]

    scales = scales_ref[...]
    pull_scale, rest_scale = scales[:, 0:1], scales[:, 1:2]
    count = classes // 4
    first = pl.multiple_of(quarter * count, LANES)
    others = others_ref[:, pl.ds(first, count)]
    cos_grad = jnp.where(others < 0.0, (others + MARK) * rest_scale, others * pull_scale)
    part = across(cos_grad.astype(jnp.bfloat16), units_ref[...])
    class_f = class_ref[pl.ds(first, count), :].astype(jnp.float32)
    inverse = 1.0 / row_norm(class_f)
    along = jnp.sum(class_f * part, axis=1, keepdims=True) * (inverse * inverse)
    part = ((part - class_f * along) * inverse).astype(out_ref.dtype).reshape(some, 8, width)
    for group in range(groups):
        out_ref[:, base + group * 8 : base + (group + 1) * 8, :] = part[
            :, :, group * LANES : (group + 1) * LANES
        ]

    each = (inputs - main) // 2
    over = jnp.dot(
        features_ref[pl.ds(pl.multiple_of(main + half * each, each), each), :],
        grads,
        preferred_element_type=jnp.float32,
    ).astype(out_ref.dtype)
    strip = jnp.where(parity == 0, over[:8], over[8:])
    for group in range(groups):
        out_ref[group, base + groups * 8 :, :] = strip[:, group * LANES : (group + 1) * LANES]
    out_ref[groups:, base + groups * 8 :, :] = jnp.zeros((some - groups, 8, LANES), out_ref.dtype)


def parts(quarter, place, dtype, blocks, features, grads, scales, units, others, class_weight):
    width = class_weight.shape[1]
    rows, groups, _ = block_sizes(features.shape[0], width, blocks)
    return call(
        functools.partial(parts_kernel, *quarter),
        "parts",
        (place, features, grads, scales, units, others, class_weight),
        [((blocks // 2, groups * (rows + 8) + 8, LANES), dtype)],
    )[0]


def assemble_kernel(pieces, blocks, place_ref, *refs):
    sources = refs[: len(pieces)]
    fc_ref, class_ref, fc_rows, class_rows, over_rows, sems = refs[-6:]
    inputs, width = fc_ref.shape
    rows, groups, main = block_sizes(inputs, width, blocks)
    each = (inputs - main) // 2
    base = groups * rows
    some = blocks // 2
    copies = []
    done = 0

    def send(source, target, at, size):
        copies.append(
            pltpu.make_async_copy(
                source, target.at[pl.ds(pl.multiple_of(at, 8), size), :], sems.at[len(copies)]
            )
        )
        copies[-1].start()

    for number, (piece, source) in enumerate(zip(pieces, sources)):
        half, parity = half_of(place_ref, piece[0]), parity_of(place_ref, piece[1])
        count = source.shape[0]
        block = (2 * half + parity) * some
        for at in range(0, count, count // 2):
            fc_here = slice((done + at) * rows, (done + at + count // 2) * rows)
            for group in range(groups):
                values = source[
                    at : at + count // 2, group * rows : (group + 1) * rows, :
                ].astype(jnp.float32)
                fc_rows[fc_here, group * LANES : (group + 1) * LANES] = values.reshape(
                    count // 2 * rows, LANES
                ).astype(jnp.bfloat16)
            send(fc_rows.at[fc_here, :], fc_ref, (block + at) * rows, count // 2 * rows)
        class_here = slice(done * 8, (done + count) * 8)
        for group in range(groups):
            lanes = slice(group * LANES, (group + 1) * LANES)
            values = source[:, base + group * 8 : base + (group + 1) * 8, :].astype(jnp.float32)
            class_rows[class_here, lanes] = values.reshape(count * 8, LANES).astype(jnp.bfloat16)
            over_rows[number, :, lanes] = source[group, base + groups * 8 :, :]
        send(class_rows.at[class_here, :], class_ref, block * 8, count * 8)
        send(over_rows.at[number], fc_ref, main + half * each + parity * 8, 8)
        done += count
    for copy in copies:
        copy.wait()


def assemble(place, blocks, sizes, pieces, into):
    inputs, classes, width = sizes
    rows, _, _ = block_sizes(inputs, width, blocks)
    total = sum(source.shape[0] for source in pieces.values())
    anywhere = pl.BlockSpec(memory_space=pltpu.HBM)
    return pl.pallas_call(
        functools.partial(assemble_kernel, tuple(pieces), blocks),
        in_specs=[SMEM] + [VMEM] * len(pieces) + [anywhere] * len(into),
        out_specs=[anywhere, anywhere],
        out_shape=[
            jax.ShapeDtypeStruct((inputs, width), jnp.bfloat16),
            jax.ShapeDtypeStruct((classes, width), jnp.bfloat16),
        ],
        scratch_shapes=[
            pltpu.VMEM((total * rows, width), jnp.bfloat16),
            pltpu.VMEM((total * 8, width), jnp.bfloat16),
            pltpu.VMEM((len(pieces), 8, width), jnp.bfloat16),
            pltpu.SemaphoreType.DMA((4 * len(pieces),)),
        ],
        input_output_aliases={1 + len(pieces) + at: at for at in range(len(into))},
        cost_estimate=pl.CostEstimate(
            flops=0, transcendentals=0, bytes_accessed=total * (rows + 8) * width * 8
        ),
        compiler_params=pltpu.CompilerParams(vmem_limit_bytes=LIMIT),
        name="assemble",
    )(place, *[placed(source) for source in pieces.values()], *into)


def shards(features, fc_weight, class_weight, labels):
    faces, inputs = features.shape
    features = features.T
    classes, width = class_weight.shape
    n_cls = lax.axis_size(CLS)
    chips = lax.axis_size(CHIPS)
    blocks = 2 * chips
    loss_weight = 1.0 / math.sqrt(faces * blocks * lax.axis_size("core"))
    place = (lax.axis_index(CLS) * 2 + lax.axis_index("zl")) * 2 + lax.axis_index("core")
    place = place.reshape(1)
    labels = labels.reshape(1, faces)

    swap = [(0, 1), (1, 0)]
    kept, away, class_unit = target_rows(place, class_weight, labels, n_cls)
    away = lax.ppermute(away, "yl", swap)
    got = exchange(embed(features, fc_weight), CLS).reshape(n_cls, faces // n_cls, width)
    got, kept, away = lax.optimization_barrier((got, kept, away))
    raw_embed, sent = unit_rows(got)
    kept, away = halve(1, place, kept, away)
    away = lax.ppermute(away, "x", [(x, x ^ 1) for x in range(4)])
    units = exchange(sent, CLS)
    units, kept, away = lax.optimization_barrier((units, kept, away))
    units = units.reshape(faces, width)

    pull, others = cosines(place, units, class_unit, labels, n_cls)
    kept, away = halve(2, place, kept, away)
    away = lax.ppermute(away, "x", [(x, x ^ 2) for x in range(4)])
    got = exchange(pull, CLS)
    sent, scales = raw_grads(loss_weight, place, got, raw_embed, kept, away)
    grads = exchange(sent, CLS).reshape(faces, width)

    swap = [(0, 1), (1, 0)]
    length = 2 * lax.axis_size("zh")
    pairs = []
    for z in range(length):
        pairs.append((2 * z, 2 * (z ^ 1)))
        pairs.append((2 * z + 1, 2 * ((z + 2 * (z % 2) - 1) % length) + 1))
    neighbour = ("zh", "zl", "core")

    operands = (blocks, features, grads, scales, units, others, class_weight)
    theirs = parts((True, True), place, jnp.bfloat16, *operands)
    theirs = lax.ppermute(theirs, "core", swap)
    sent = parts((False, True), place, jnp.float32, *operands) + theirs.astype(jnp.float32)
    sent, later = lax.optimization_barrier((sent.astype(jnp.bfloat16), place))
    got = lax.ppermute(sent, neighbour, pairs)
    theirs = parts((True, False), later, jnp.bfloat16, *operands)
    theirs = lax.ppermute(theirs, "core", swap)
    mine = parts((False, False), later, jnp.float32, *operands) + got.astype(jnp.float32)
    mine = lax.optimization_barrier(mine)
    mine = (mine + theirs.astype(jnp.float32)).astype(jnp.bfloat16)
    done = jnp.sum(exchange(mine, CHIPS).astype(jnp.float32), axis=0).astype(jnp.bfloat16)

    sizes = (inputs, classes, width)
    mine = exchange(jnp.broadcast_to(done, (chips,) + done.shape), CHIPS)
    next_mine = lax.ppermute(mine, neighbour, pairs)
    across_mine = lax.ppermute(mine, "core", swap)
    written = assemble(place, blocks, sizes, {(False, False): mine}, ())
    next_mine, written = lax.optimization_barrier((next_mine, written))
    across_next = lax.ppermute(next_mine, "core", swap)
    pieces = {(False, True): next_mine, (True, False): across_mine}
    written = assemble(place, blocks, sizes, pieces, written)
    return tuple(assemble(place, blocks, sizes, {(True, True): across_next}, written))


def solution(mesh):
    fine = Mesh(mesh.devices.reshape(4, 2, 4, 2, 4, 2), ("zh", "zl", "yh", "core", "x", "yl"))
    dp = ("zh", "zl", "yh", "core")
    specs = (P(dp, CLS), P(CLS, None), P(CLS, None), P(dp))
    return jax.shard_map(
        shards,
        mesh=fine,
        in_specs=specs,
        out_specs=(P(CLS, None), P(CLS, None)),
        check_vma=False,
    )
```

```python
import functools
import math

import jax
import jax.numpy as jnp
from jax import lax
from jax.experimental import pallas as pl
from jax.experimental.pallas import tpu as pltpu
from jax.sharding import Mesh
from jax.sharding import PartitionSpec as P

SCALE = 64.0
MARGIN = 0.5
SOFTEN = 0.01
EPSILON = 1e-06

CLS = ("x", "yl")
CHIPS = ("zh", "yh")
LANES = 128
CHUNKS = 2
MARK = 1024.0
STEP = 512
LIMIT = 24 << 20
VMEM = pl.BlockSpec(memory_space=pltpu.VMEM)
SMEM = pl.BlockSpec(memory_space=pltpu.SMEM)


def exchange(blocks, axes):
    return lax.all_to_all(blocks, axes, 0, 0, tiled=True)


def across(left, right):
    return lax.dot_general(
        left, right, (((0,), (0,)), ((), ())), preferred_element_type=jnp.float32
    )


def row_norm(values):
    return jnp.sqrt(jnp.sum(values * values, axis=1, keepdims=True) + EPSILON)


def packed_columns(*columns):
    rows = columns[0].shape[0]
    lane = lax.broadcasted_iota(jnp.int32, (rows, LANES), 1)
    block = jnp.zeros((rows, LANES), jnp.float32)
    for at, column in enumerate(columns):
        rest = column
        for part in range(3):
            term = rest.astype(jnp.bfloat16).astype(jnp.float32)
            block = jnp.where(lane == 3 * at + part, term, block)
            rest = rest - term
    return block


def unpacked_column(block, at):
    lane = lax.broadcasted_iota(jnp.int32, block.shape, 1)
    inside = (lane >= 3 * at) & (lane < 3 * at + 3)
    return jnp.sum(jnp.where(inside, block, 0.0), axis=1, keepdims=True)


def placed(array, space=pltpu.VMEM):
    return pltpu.with_memory_space_constraint(array, space)


def half_of(place_ref, other):
    core = lax.rem(place_ref[0], 2)
    return 1 - core if other else core


def parity_of(place_ref, other):
    odd = lax.rem(lax.div(place_ref[0], 2), 2)
    return 1 - odd if other else odd


def first_of(place_ref, classes):
    return lax.div(place_ref[0], 4) * classes


def call(kernel, name, operands, results, **options):
    specs = [SMEM if operand.ndim == 1 else VMEM for operand in operands]
    operands = [operand if operand.ndim == 1 else placed(operand) for operand in operands]
    return pl.pallas_call(
        kernel,
        in_specs=specs,
        out_specs=[VMEM] * len(results),
        out_shape=[pltpu.VMEM(shape, dtype) for shape, dtype in results],
        compiler_params=pltpu.CompilerParams(vmem_limit_bytes=LIMIT),
        name=name,
        **options,
    )(*operands)


def target_mask(first, labels, rows, classes):
    lane = lax.broadcasted_iota(jnp.int32, (rows, LANES), 1)
    return jnp.concatenate(
        [labels == lane + (first + at) for at in range(0, classes, LANES)], axis=1
    )


def spread_labels(labels_row):
    faces = labels_row.shape[1]
    return jnp.transpose(jnp.broadcast_to(labels_row, (LANES, faces)))


def embed_kernel(
    place_ref, features_ref, fc_ref, class_ref, labels_ref, sent_ref, unit_ref,
    left_ref, right_ref, total_ref, weight_ref, row_ref, sems
):
    width = fc_ref.shape[1]
    inputs, faces = features_ref.shape
    classes = class_ref.shape[0]
    ends = [inputs * at // CHUNKS // LANES * LANES for at in range(CHUNKS)] + [inputs]
    copies = [
        pltpu.make_async_copy(labels_ref, row_ref, sems.at[0]),
        pltpu.make_async_copy(class_ref, weight_ref, sems.at[1]),
    ]
    for at in range(CHUNKS):
        rows = pl.ds(ends[at], ends[at + 1] - ends[at])
        for source, target in ((features_ref, left_ref), (fc_ref, right_ref)):
            copies.append(
                pltpu.make_async_copy(
                    source.at[rows, :], target.at[rows, :], sems.at[len(copies)]
                )
            )
    for copy in copies:
        copy.start()

    copies[0].wait()
    labels = spread_labels(row_ref[...])
    chosen = target_mask(first_of(place_ref, classes), labels, faces, classes)
    chosen = jnp.where(chosen, 1.0, 0.0).astype(jnp.bfloat16)
    copies[1].wait()
    class_f = weight_ref[...].astype(jnp.float32)
    unit_ref[...] = (class_f * (1.0 / row_norm(class_f))).astype(jnp.bfloat16)
    target_part = jnp.dot(chosen, unit_ref[...], preferred_element_type=jnp.float32)
    sent_ref[:, width:] = target_part.astype(jnp.bfloat16)

    for at in range(CHUNKS):
        copies[2 + 2 * at].wait()
        copies[3 + 2 * at].wait()
        here = slice(ends[at], ends[at + 1])
        part = across(left_ref[here, :], right_ref[here, :])
        if at > 0:
            part = part + total_ref[...]
        if at < CHUNKS - 1:
            total_ref[...] = part
        else:
            sent_ref[:, :width] = part.astype(jnp.bfloat16)


def embed(place, features, fc_weight, class_weight, labels):
    inputs, faces = features.shape
    classes, width = class_weight.shape
    arrays = [placed(array, pltpu.HBM) for array in (features, fc_weight, class_weight, labels)]
    return pl.pallas_call(
        embed_kernel,
        in_specs=[SMEM] + [pl.BlockSpec(memory_space=pltpu.HBM)] * len(arrays),
        out_specs=[VMEM, VMEM],
        out_shape=[
            pltpu.VMEM((faces, 2 * width), jnp.bfloat16),
            pltpu.VMEM((classes, width), jnp.bfloat16),
        ],
        scratch_shapes=[
            pltpu.VMEM((inputs, faces), jnp.bfloat16),
            pltpu.VMEM((inputs, width), jnp.bfloat16),
            pltpu.VMEM((faces, width), jnp.float32),
            pltpu.VMEM((classes, width), jnp.bfloat16),
            pltpu.VMEM((1, faces), jnp.int32),
            pltpu.SemaphoreType.DMA((2 + 2 * CHUNKS,)),
        ],
        compiler_params=pltpu.CompilerParams(vmem_limit_bytes=LIMIT),
        name="embed",
    )(place, *arrays)


def units_kernel(got_ref, raw_ref, target_ref, sent_ref):
    width = raw_ref.shape[1]
    got = got_ref[0].astype(jnp.float32)
    for peer in range(1, got_ref.shape[0]):
        got = got + got_ref[peer].astype(jnp.float32)
    raw_embed = got[:, :width]
    raw_ref[...] = raw_embed
    target_ref[...] = got[:, width:]
    unit = (raw_embed * (1.0 / row_norm(raw_embed))).astype(jnp.bfloat16)
    for copy in range(sent_ref.shape[0]):
        sent_ref[copy] = unit


def unit_rows(got):
    peers, owned, both = got.shape
    rows = (owned, both // 2)
    return call(
        units_kernel,
        "units",
        (got,),
        [(rows, jnp.float32), (rows, jnp.float32), ((peers,) + rows, jnp.bfloat16)],
    )


def target_terms(cosine):
    sine = jnp.sqrt(1.0 + SOFTEN - cosine * cosine)
    logit = SCALE * (cosine * math.cos(MARGIN) - sine * math.sin(MARGIN))
    slope = SCALE * (math.cos(MARGIN) + math.sin(MARGIN) * cosine / sine)
    return logit, slope


def cosine_kernel(place_ref, units_ref, class_ref, labels_ref, pull_ref, others_ref):
    faces, width = units_ref.shape
    classes = class_ref.shape[0]
    peers = pull_ref.shape[0]
    owned = faces // peers
    step = STEP
    first = first_of(place_ref, classes)
    labels = spread_labels(labels_ref[...])
    for at in range(0, faces, step):
        here = slice(at, at + step)
        cosine = lax.dot_general(
            units_ref[here, :],
            class_ref[...],
            (((1,), (1,)), ((), ())),
            preferred_element_type=jnp.float32,
        )
        label = labels[here, :]
        is_target = target_mask(first, label, step, classes)
        powers = jnp.exp(SCALE * cosine)
        others = jnp.where(is_target, 0.0, powers)
        pull = jnp.dot(
            others.astype(jnp.bfloat16), class_ref[...], preferred_element_type=jnp.float32
        )
        pull_ref[at // owned : (at + step) // owned, :owned, :] = pull.astype(
            jnp.bfloat16
        ).reshape(step // owned, owned, width)
        cos_t = jnp.sum(jnp.where(is_target, cosine, 0.0), axis=1, keepdims=True)
        logit, slope = target_terms(cos_t)
        others_ref[here, :] = jnp.where(is_target, -(slope + MARK), powers)
        mine = ((label >= first) & (label < first + classes))[:, :1]
        power_t = jnp.where(mine, jnp.exp(logit), 0.0)
        sums = packed_columns(jnp.sum(others, axis=1, keepdims=True), power_t)
        sums = jnp.transpose(sums)[:8].astype(jnp.bfloat16)
        for peer in range(peers):
            pull_ref[peer, owned:, here] = sums


def cosines(place, units, class_unit, labels, peers):
    faces, width = units.shape
    classes = class_unit.shape[0]
    return call(
        cosine_kernel,
        "cosines",
        (place, units, class_unit, labels),
        [
            ((peers, faces // peers + 8, width), jnp.bfloat16),
            ((faces, classes), jnp.float32),
        ],
    )


def raw_grad_kernel(
    loss_weight, place_ref, pulls_ref, raw_ref, target_ref, sent_ref, scales_ref
):
    owned, width = raw_ref.shape
    pulls = pulls_ref[0].astype(jnp.float32)
    for peer in range(1, pulls_ref.shape[0]):
        pulls = pulls + pulls_ref[peer].astype(jnp.float32)
    sums = jnp.concatenate([pulls[owned:], jnp.zeros((LANES - 8, width), jnp.float32)], axis=0)
    sums = jnp.transpose(sums)
    rest, power_t = unpacked_column(sums, 0), unpacked_column(sums, 1)
    inverse = loss_weight / (rest + power_t)
    lane = lax.broadcasted_iota(jnp.int32, sums.shape, 1)
    scales_ref[...] = jnp.where(lane == 0, SCALE * inverse, rest * inverse)
    own = pl.ds(pl.multiple_of(lax.div(place_ref[0], 4) * owned, owned), owned)
    scales = scales_ref[own, :]
    pull_scale, rest_scale = scales[:, 0:1], scales[:, 1:2]

    raw_embed, target = raw_ref[...], target_ref[...]
    inverse_norm = 1.0 / row_norm(raw_embed)
    unit_f = raw_embed * inverse_norm
    unit = unit_f.astype(jnp.bfloat16).astype(jnp.float32)
    _, slope = target_terms(jnp.sum(unit * target, axis=1, keepdims=True))
    unit_grad = pulls[:owned] * pull_scale - target * (rest_scale * slope)
    raw_grad = (
        unit_grad - unit_f * jnp.sum(unit_f * unit_grad, axis=1, keepdims=True)
    ) * inverse_norm
    raw_grad = raw_grad.astype(jnp.bfloat16)
    for copy in range(sent_ref.shape[0]):
        sent_ref[copy] = raw_grad


def raw_grads(loss_weight, place, pulls, raw_embed, target_unit):
    peers = pulls.shape[0]
    owned, width = raw_embed.shape
    return call(
        functools.partial(raw_grad_kernel, loss_weight),
        "raw_grads",
        (place, pulls, raw_embed, target_unit),
        [((peers, owned, width), jnp.bfloat16), ((peers * owned, LANES), jnp.float32)],
    )


def block_sizes(inputs, width, blocks):
    rows = inputs // (2 * blocks * 8) * 8
    return rows, width // LANES, 2 * blocks * rows


def parts_kernel(
    other_half, other_parity,
    place_ref, features_ref, grads_ref, scales_ref, units_ref, others_ref, class_ref, out_ref
):
    some = out_ref.shape[0]
    classes, width = class_ref.shape
    inputs = features_ref.shape[0]
    rows, groups, main = block_sizes(inputs, width, 2 * some)
    base = groups * rows
    half, parity = half_of(place_ref, other_half), parity_of(place_ref, other_parity)
    quarter = 2 * half + parity
    grads = grads_ref[...]

    first = pl.multiple_of(quarter * (some * rows), LANES)
    part = jnp.dot(
        features_ref[pl.ds(first, some * rows), :], grads, preferred_element_type=jnp.float32
    )
    part = part.astype(out_ref.dtype).reshape(some, rows, width)
    for group in range(groups):
        out_ref[:, group * rows : (group + 1) * rows, :] = part[
            :, :, group * LANES : (group + 1) * LANES
        ]

    scales = scales_ref[...]
    pull_scale, rest_scale = scales[:, 0:1], scales[:, 1:2]
    count = classes // 4
    first = pl.multiple_of(quarter * count, LANES)
    others = others_ref[:, pl.ds(first, count)]
    cos_grad = jnp.where(others < 0.0, (others + MARK) * rest_scale, others * pull_scale)
    part = across(cos_grad.astype(jnp.bfloat16), units_ref[...])
    class_f = class_ref[pl.ds(first, count), :].astype(jnp.float32)
    inverse = 1.0 / row_norm(class_f)
    along = jnp.sum(class_f * part, axis=1, keepdims=True) * (inverse * inverse)
    part = ((part - class_f * along) * inverse).astype(out_ref.dtype).reshape(some, 8, width)
    for group in range(groups):
        out_ref[:, base + group * 8 : base + (group + 1) * 8, :] = part[
            :, :, group * LANES : (group + 1) * LANES
        ]

    each = (inputs - main) // 2
    over = jnp.dot(
        features_ref[pl.ds(pl.multiple_of(main + half * each, each), each), :],
        grads,
        preferred_element_type=jnp.float32,
    ).astype(out_ref.dtype)
    strip = jnp.where(parity == 0, over[:8], over[8:])
    for group in range(groups):
        out_ref[group, base + groups * 8 :, :] = strip[:, group * LANES : (group + 1) * LANES]
    out_ref[groups:, base + groups * 8 :, :] = jnp.zeros((some - groups, 8, LANES), out_ref.dtype)


def parts(quarter, place, dtype, blocks, features, grads, scales, units, others, class_weight):
    width = class_weight.shape[1]
    rows, groups, _ = block_sizes(features.shape[0], width, blocks)
    return call(
        functools.partial(parts_kernel, *quarter),
        "parts",
        (place, features, grads, scales, units, others, class_weight),
        [((blocks // 2, groups * (rows + 8) + 8, LANES), dtype)],
    )[0]


def total_kernel(got_ref, sent_ref):
    total = got_ref[0].astype(jnp.float32)
    for peer in range(1, got_ref.shape[0]):
        total = total + got_ref[peer].astype(jnp.float32)
    total = total.astype(jnp.bfloat16)
    for copy in range(sent_ref.shape[0]):
        sent_ref[copy] = total


def totals(got):
    return call(total_kernel, "totals", (got,), [(got.shape, jnp.bfloat16)])[0]


def assemble_kernel(pieces, blocks, place_ref, *refs):
    sources = refs[: len(pieces)]
    fc_ref, class_ref, fc_rows, class_rows, over_rows, sems = refs[-6:]
    inputs, width = fc_ref.shape
    rows, groups, main = block_sizes(inputs, width, blocks)
    each = (inputs - main) // 2
    base = groups * rows
    some = blocks // 2
    copies = []
    done = 0

    def send(source, target, at, size):
        copies.append(
            pltpu.make_async_copy(
                source, target.at[pl.ds(pl.multiple_of(at, 8), size), :], sems.at[len(copies)]
            )
        )
        copies[-1].start()

    for number, (piece, source) in enumerate(zip(pieces, sources)):
        half, parity = half_of(place_ref, piece[0]), parity_of(place_ref, piece[1])
        count = source.shape[0]
        block = (2 * half + parity) * some
        for at in range(0, count, count // 2):
            fc_here = slice((done + at) * rows, (done + at + count // 2) * rows)
            for group in range(groups):
                values = source[
                    at : at + count // 2, group * rows : (group + 1) * rows, :
                ].astype(jnp.float32)
                fc_rows[fc_here, group * LANES : (group + 1) * LANES] = values.reshape(
                    count // 2 * rows, LANES
                ).astype(jnp.bfloat16)
            send(fc_rows.at[fc_here, :], fc_ref, (block + at) * rows, count // 2 * rows)
        class_here = slice(done * 8, (done + count) * 8)
        for group in range(groups):
            lanes = slice(group * LANES, (group + 1) * LANES)
            values = source[:, base + group * 8 : base + (group + 1) * 8, :].astype(jnp.float32)
            class_rows[class_here, lanes] = values.reshape(count * 8, LANES).astype(jnp.bfloat16)
            over_rows[number, :, lanes] = source[group, base + groups * 8 :, :]
        send(class_rows.at[class_here, :], class_ref, block * 8, count * 8)
        send(over_rows.at[number], fc_ref, main + half * each + parity * 8, 8)
        done += count
    for copy in copies:
        copy.wait()


def assemble(place, blocks, sizes, pieces, into):
    inputs, classes, width = sizes
    rows, _, _ = block_sizes(inputs, width, blocks)
    total = sum(source.shape[0] for source in pieces.values())
    anywhere = pl.BlockSpec(memory_space=pltpu.HBM)
    return pl.pallas_call(
        functools.partial(assemble_kernel, tuple(pieces), blocks),
        in_specs=[SMEM] + [VMEM] * len(pieces) + [anywhere] * len(into),
        out_specs=[anywhere, anywhere],
        out_shape=[
            jax.ShapeDtypeStruct((inputs, width), jnp.bfloat16),
            jax.ShapeDtypeStruct((classes, width), jnp.bfloat16),
        ],
        scratch_shapes=[
            pltpu.VMEM((total * rows, width), jnp.bfloat16),
            pltpu.VMEM((total * 8, width), jnp.bfloat16),
            pltpu.VMEM((len(pieces), 8, width), jnp.bfloat16),
            pltpu.SemaphoreType.DMA((4 * len(pieces),)),
        ],
        input_output_aliases={1 + len(pieces) + at: at for at in range(len(into))},
        cost_estimate=pl.CostEstimate(
            flops=0, transcendentals=0, bytes_accessed=total * (rows + 8) * width * 8
        ),
        compiler_params=pltpu.CompilerParams(vmem_limit_bytes=LIMIT),
        name="assemble",
    )(place, *[placed(source) for source in pieces.values()], *into)


def shards(features, fc_weight, class_weight, labels):
    faces, inputs = features.shape
    features = features.T
    classes, width = class_weight.shape
    n_cls = lax.axis_size(CLS)
    chips = lax.axis_size(CHIPS)
    blocks = 2 * chips
    loss_weight = 1.0 / math.sqrt(faces * blocks * lax.axis_size("core"))
    place = (lax.axis_index(CLS) * 2 + lax.axis_index("zl")) * 2 + lax.axis_index("core")
    place = place.reshape(1)
    labels = labels.reshape(1, faces)

    sent, class_unit = embed(place, features, fc_weight, class_weight, labels)
    got = exchange(sent, CLS).reshape(n_cls, faces // n_cls, 2 * width)
    raw_embed, target_unit, sent = unit_rows(got)
    units = exchange(sent, CLS)
    units = units.reshape(faces, width)

    pull, others = cosines(place, units, class_unit, labels, n_cls)
    got = exchange(pull, CLS)
    sent, scales = raw_grads(loss_weight, place, got, raw_embed, target_unit)
    grads = exchange(sent, CLS).reshape(faces, width)

    swap = [(0, 1), (1, 0)]
    length = 2 * lax.axis_size("zh")
    pairs = []
    for z in range(length):
        pairs.append((2 * z, 2 * (z ^ 1)))
        pairs.append((2 * z + 1, 2 * ((z + 2 * (z % 2) - 1) % length) + 1))
    neighbour = ("zh", "zl", "core")

    operands = (blocks, features, grads, scales, units, others, class_weight)
    theirs = parts((True, True), place, jnp.bfloat16, *operands)
    theirs = lax.ppermute(theirs, "core", swap)
    sent = parts((False, True), place, jnp.float32, *operands) + theirs.astype(jnp.float32)
    sent, later = lax.optimization_barrier((sent.astype(jnp.bfloat16), place))
    got = lax.ppermute(sent, neighbour, pairs)
    theirs = parts((True, False), later, jnp.bfloat16, *operands)
    theirs = lax.ppermute(theirs, "core", swap)
    mine = parts((False, False), later, jnp.float32, *operands) + got.astype(jnp.float32)
    mine = lax.optimization_barrier(mine)
    mine = (mine + theirs.astype(jnp.float32)).astype(jnp.bfloat16)
    sizes = (inputs, classes, width)
    mine = exchange(totals(exchange(mine, CHIPS)), CHIPS)
    next_mine = lax.ppermute(mine, neighbour, pairs)
    across_mine = lax.ppermute(mine, "core", swap)
    written = assemble(place, blocks, sizes, {(False, False): mine}, ())
    next_mine, written = lax.optimization_barrier((next_mine, written))
    across_next = lax.ppermute(next_mine, "core", swap)
    pieces = {(False, True): next_mine, (True, False): across_mine}
    written = assemble(place, blocks, sizes, pieces, written)
    return tuple(assemble(place, blocks, sizes, {(True, True): across_next}, written))


def solution(mesh):
    fine = Mesh(mesh.devices.reshape(4, 2, 4, 2, 4, 2), ("zh", "zl", "yh", "core", "x", "yl"))
    dp = ("zh", "zl", "yh", "core")
    specs = (P(dp, CLS), P(CLS, None), P(CLS, None), P(dp))
    return jax.shard_map(
        shards,
        mesh=fine,
        in_specs=specs,
        out_specs=(P(CLS, None), P(CLS, None)),
        check_vma=False,
    )
```

```python
import functools
import math

import jax
import jax.numpy as jnp
from jax import lax
from jax.experimental import pallas as pl
from jax.experimental.pallas import tpu as pltpu
from jax.sharding import Mesh
from jax.sharding import PartitionSpec as P

SCALE = 64.0
MARGIN = 0.5
SOFTEN = 0.01
EPSILON = 1e-06

CLS = ("x", "yl")
CHIPS = ("zh", "yh")
LANES = 128
CHUNKS = 2
MARK = 1024.0
STEP = 512
LIMIT = 24 << 20
VMEM = pl.BlockSpec(memory_space=pltpu.VMEM)
SMEM = pl.BlockSpec(memory_space=pltpu.SMEM)


def exchange(blocks, axes):
    return lax.all_to_all(blocks, axes, 0, 0, tiled=True)


def across(left, right):
    return lax.dot_general(
        left, right, (((0,), (0,)), ((), ())), preferred_element_type=jnp.float32
    )


def row_norm(values):
    return jnp.sqrt(jnp.sum(values * values, axis=1, keepdims=True) + EPSILON)


def packed_columns(*columns):
    rows = columns[0].shape[0]
    lane = lax.broadcasted_iota(jnp.int32, (rows, LANES), 1)
    block = jnp.zeros((rows, LANES), jnp.float32)
    for at, column in enumerate(columns):
        rest = column
        for part in range(3):
            term = rest.astype(jnp.bfloat16).astype(jnp.float32)
            block = jnp.where(lane == 3 * at + part, term, block)
            rest = rest - term
    return block


def unpacked_column(block, at):
    lane = lax.broadcasted_iota(jnp.int32, block.shape, 1)
    inside = (lane >= 3 * at) & (lane < 3 * at + 3)
    return jnp.sum(jnp.where(inside, block, 0.0), axis=1, keepdims=True)


def placed(array, space=pltpu.VMEM):
    return pltpu.with_memory_space_constraint(array, space)


def half_of(place_ref, other):
    core = lax.rem(place_ref[0], 2)
    return 1 - core if other else core


def parity_of(place_ref, other):
    odd = lax.rem(lax.div(place_ref[0], 2), 2)
    return 1 - odd if other else odd


def first_of(place_ref, classes):
    return lax.div(place_ref[0], 4) * classes


def call(kernel, name, operands, results, **options):
    specs = [SMEM if operand.ndim == 1 else VMEM for operand in operands]
    operands = [operand if operand.ndim == 1 else placed(operand) for operand in operands]
    return pl.pallas_call(
        kernel,
        in_specs=specs,
        out_specs=[VMEM] * len(results),
        out_shape=[pltpu.VMEM(shape, dtype) for shape, dtype in results],
        compiler_params=pltpu.CompilerParams(vmem_limit_bytes=LIMIT),
        name=name,
        **options,
    )(*operands)


def target_mask(first, labels, rows, classes):
    lane = lax.broadcasted_iota(jnp.int32, (rows, LANES), 1)
    return jnp.concatenate(
        [labels == lane + (first + at) for at in range(0, classes, LANES)], axis=1
    )


def spread_labels(labels_row):
    faces = labels_row.shape[1]
    return jnp.transpose(jnp.broadcast_to(labels_row, (LANES, faces)))


def embed_kernel(
    place_ref, features_ref, fc_ref, class_ref, labels_ref, sent_ref, unit_ref,
    left_ref, right_ref, total_ref, weight_ref, row_ref, sems
):
    width = fc_ref.shape[1]
    inputs, faces = features_ref.shape
    classes = class_ref.shape[0]
    ends = [inputs * at // CHUNKS // LANES * LANES for at in range(CHUNKS)] + [inputs]
    copies = [
        pltpu.make_async_copy(labels_ref, row_ref, sems.at[0]),
        pltpu.make_async_copy(class_ref, weight_ref, sems.at[1]),
    ]
    for at in range(CHUNKS):
        rows = pl.ds(ends[at], ends[at + 1] - ends[at])
        for source, target in ((features_ref, left_ref), (fc_ref, right_ref)):
            copies.append(
                pltpu.make_async_copy(
                    source.at[rows, :], target.at[rows, :], sems.at[len(copies)]
                )
            )
    for copy in copies:
        copy.start()

    copies[0].wait()
    labels = spread_labels(row_ref[...])
    chosen = target_mask(first_of(place_ref, classes), labels, faces, classes)
    chosen = jnp.where(chosen, 1.0, 0.0).astype(jnp.bfloat16)
    copies[1].wait()
    class_f = weight_ref[...].astype(jnp.float32)
    unit_ref[...] = (class_f * (1.0 / row_norm(class_f))).astype(jnp.bfloat16)
    target_part = jnp.dot(chosen, unit_ref[...], preferred_element_type=jnp.float32)
    sent_ref[:, width:] = target_part.astype(jnp.bfloat16)

    for at in range(CHUNKS):
        copies[2 + 2 * at].wait()
        copies[3 + 2 * at].wait()
        here = slice(ends[at], ends[at + 1])
        part = across(left_ref[here, :], right_ref[here, :])
        if at > 0:
            part = part + total_ref[...]
        if at < CHUNKS - 1:
            total_ref[...] = part
        else:
            sent_ref[:, :width] = part.astype(jnp.bfloat16)


def embed(place, features, fc_weight, class_weight, labels):
    inputs, faces = features.shape
    classes, width = class_weight.shape
    arrays = [placed(array, pltpu.HBM) for array in (features, fc_weight, class_weight, labels)]
    return pl.pallas_call(
        embed_kernel,
        in_specs=[SMEM] + [pl.BlockSpec(memory_space=pltpu.HBM)] * len(arrays),
        out_specs=[VMEM, VMEM],
        out_shape=[
            pltpu.VMEM((faces, 2 * width), jnp.bfloat16),
            pltpu.VMEM((classes, width), jnp.bfloat16),
        ],
        scratch_shapes=[
            pltpu.VMEM((inputs, faces), jnp.bfloat16),
            pltpu.VMEM((inputs, width), jnp.bfloat16),
            pltpu.VMEM((faces, width), jnp.float32),
            pltpu.VMEM((classes, width), jnp.bfloat16),
            pltpu.VMEM((1, faces), jnp.int32),
            pltpu.SemaphoreType.DMA((2 + 2 * CHUNKS,)),
        ],
        compiler_params=pltpu.CompilerParams(vmem_limit_bytes=LIMIT),
        name="embed",
    )(place, *arrays)


def units_kernel(got_ref, raw_ref, target_ref, sent_ref):
    width = raw_ref.shape[1]
    got = got_ref[0].astype(jnp.float32)
    for peer in range(1, got_ref.shape[0]):
        got = got + got_ref[peer].astype(jnp.float32)
    raw_embed = got[:, :width]
    raw_ref[...] = raw_embed
    target_ref[...] = got[:, width:]
    unit = (raw_embed * (1.0 / row_norm(raw_embed))).astype(jnp.bfloat16)
    for copy in range(sent_ref.shape[0]):
        sent_ref[copy] = unit


def unit_rows(got):
    peers, owned, both = got.shape
    rows = (owned, both // 2)
    return call(
        units_kernel,
        "units",
        (got,),
        [(rows, jnp.float32), (rows, jnp.float32), ((peers,) + rows, jnp.bfloat16)],
    )


def target_terms(cosine):
    sine = jnp.sqrt(1.0 + SOFTEN - cosine * cosine)
    logit = SCALE * (cosine * math.cos(MARGIN) - sine * math.sin(MARGIN))
    slope = SCALE * (math.cos(MARGIN) + math.sin(MARGIN) * cosine / sine)
    return logit, slope


def cosine_kernel(place_ref, units_ref, class_ref, labels_ref, pull_ref, others_ref):
    faces, width = units_ref.shape
    classes = class_ref.shape[0]
    peers = pull_ref.shape[0]
    owned = faces // peers
    step = STEP
    first = first_of(place_ref, classes)
    labels = spread_labels(labels_ref[...])
    for at in range(0, faces, step):
        here = slice(at, at + step)
        cosine = lax.dot_general(
            units_ref[here, :],
            class_ref[...],
            (((1,), (1,)), ((), ())),
            preferred_element_type=jnp.float32,
        )
        label = labels[here, :]
        is_target = target_mask(first, label, step, classes)
        powers = jnp.exp(SCALE * cosine)
        others = jnp.where(is_target, 0.0, powers)
        pull = jnp.dot(
            others.astype(jnp.bfloat16), class_ref[...], preferred_element_type=jnp.float32
        )
        pull_ref[at // owned : (at + step) // owned, :owned, :] = pull.astype(
            jnp.bfloat16
        ).reshape(step // owned, owned, width)
        cos_t = jnp.sum(jnp.where(is_target, cosine, 0.0), axis=1, keepdims=True)
        logit, slope = target_terms(cos_t)
        others_ref[here, :] = jnp.where(is_target, -(slope + MARK), powers)
        mine = ((label >= first) & (label < first + classes))[:, :1]
        power_t = jnp.where(mine, jnp.exp(logit), 0.0)
        sums = packed_columns(jnp.sum(others, axis=1, keepdims=True), power_t)
        sums = jnp.transpose(sums)[:8].astype(jnp.bfloat16)
        for peer in range(peers):
            pull_ref[peer, owned:, here] = sums


def cosines(place, units, class_unit, labels, peers):
    faces, width = units.shape
    classes = class_unit.shape[0]
    return call(
        cosine_kernel,
        "cosines",
        (place, units, class_unit, labels),
        [
            ((peers, faces // peers + 8, width), jnp.bfloat16),
            ((faces, classes), jnp.float32),
        ],
    )


def raw_grad_kernel(
    loss_weight, place_ref, pulls_ref, raw_ref, target_ref, sent_ref, scales_ref
):
    owned, width = raw_ref.shape
    pulls = pulls_ref[0].astype(jnp.float32)
    for peer in range(1, pulls_ref.shape[0]):
        pulls = pulls + pulls_ref[peer].astype(jnp.float32)
    sums = jnp.concatenate([pulls[owned:], jnp.zeros((LANES - 8, width), jnp.float32)], axis=0)
    sums = jnp.transpose(sums)
    rest, power_t = unpacked_column(sums, 0), unpacked_column(sums, 1)
    inverse = loss_weight / (rest + power_t)
    lane = lax.broadcasted_iota(jnp.int32, sums.shape, 1)
    scales_ref[...] = jnp.where(lane == 0, SCALE * inverse, rest * inverse)
    own = pl.ds(pl.multiple_of(lax.div(place_ref[0], 4) * owned, owned), owned)
    scales = scales_ref[own, :]
    pull_scale, rest_scale = scales[:, 0:1], scales[:, 1:2]

    raw_embed, target = raw_ref[...], target_ref[...]
    inverse_norm = 1.0 / row_norm(raw_embed)
    unit_f = raw_embed * inverse_norm
    unit = unit_f.astype(jnp.bfloat16).astype(jnp.float32)
    _, slope = target_terms(jnp.sum(unit * target, axis=1, keepdims=True))
    unit_grad = pulls[:owned] * pull_scale - target * (rest_scale * slope)
    raw_grad = (
        unit_grad - unit_f * jnp.sum(unit_f * unit_grad, axis=1, keepdims=True)
    ) * inverse_norm
    raw_grad = raw_grad.astype(jnp.bfloat16)
    for copy in range(sent_ref.shape[0]):
        sent_ref[copy] = raw_grad


def raw_grads(loss_weight, place, pulls, raw_embed, target_unit):
    peers = pulls.shape[0]
    owned, width = raw_embed.shape
    return call(
        functools.partial(raw_grad_kernel, loss_weight),
        "raw_grads",
        (place, pulls, raw_embed, target_unit),
        [((peers, owned, width), jnp.bfloat16), ((peers * owned, LANES), jnp.float32)],
    )


def block_sizes(inputs, width, blocks):
    rows = inputs // (2 * blocks * 8) * 8
    return rows, width // LANES, 2 * blocks * rows


def parts_kernel(
    other_half, other_parity,
    place_ref, features_ref, grads_ref, scales_ref, units_ref, others_ref, class_ref, out_ref
):
    some = out_ref.shape[0]
    classes, width = class_ref.shape
    inputs = features_ref.shape[0]
    rows, groups, main = block_sizes(inputs, width, 2 * some)
    base = groups * rows
    half, parity = half_of(place_ref, other_half), parity_of(place_ref, other_parity)
    quarter = 2 * half + parity
    grads = grads_ref[...]

    first = pl.multiple_of(quarter * (some * rows), LANES)
    part = jnp.dot(
        features_ref[pl.ds(first, some * rows), :], grads, preferred_element_type=jnp.float32
    )
    part = part.astype(out_ref.dtype).reshape(some, rows, width)
    for group in range(groups):
        out_ref[:, group * rows : (group + 1) * rows, :] = part[
            :, :, group * LANES : (group + 1) * LANES
        ]

    scales = scales_ref[...]
    pull_scale, rest_scale = scales[:, 0:1], scales[:, 1:2]
    count = classes // 4
    first = pl.multiple_of(quarter * count, LANES)
    others = others_ref[:, pl.ds(first, count)]
    cos_grad = jnp.where(others < 0.0, (others + MARK) * rest_scale, others * pull_scale)
    part = across(cos_grad.astype(jnp.bfloat16), units_ref[...])
    class_f = class_ref[pl.ds(first, count), :].astype(jnp.float32)
    inverse = 1.0 / row_norm(class_f)
    along = jnp.sum(class_f * part, axis=1, keepdims=True) * (inverse * inverse)
    part = ((part - class_f * along) * inverse).astype(out_ref.dtype).reshape(some, 8, width)
    for group in range(groups):
        out_ref[:, base + group * 8 : base + (group + 1) * 8, :] = part[
            :, :, group * LANES : (group + 1) * LANES
        ]

    each = (inputs - main) // 2
    over = jnp.dot(
        features_ref[pl.ds(pl.multiple_of(main + half * each, each), each), :],
        grads,
        preferred_element_type=jnp.float32,
    ).astype(out_ref.dtype)
    strip = jnp.where(parity == 0, over[:8], over[8:])
    for group in range(groups):
        out_ref[group, base + groups * 8 :, :] = strip[:, group * LANES : (group + 1) * LANES]
    out_ref[groups:, base + groups * 8 :, :] = jnp.zeros((some - groups, 8, LANES), out_ref.dtype)


def parts(quarter, place, dtype, blocks, features, grads, scales, units, others, class_weight):
    width = class_weight.shape[1]
    rows, groups, _ = block_sizes(features.shape[0], width, blocks)
    return call(
        functools.partial(parts_kernel, *quarter),
        "parts",
        (place, features, grads, scales, units, others, class_weight),
        [((blocks // 2, groups * (rows + 8) + 8, LANES), dtype)],
    )[0]


def total_kernel(got_ref, sent_ref):
    total = got_ref[0].astype(jnp.float32)
    for peer in range(1, got_ref.shape[0]):
        total = total + got_ref[peer].astype(jnp.float32)
    total = total.astype(jnp.bfloat16)
    for copy in range(sent_ref.shape[0]):
        sent_ref[copy] = total


def totals(got):
    return call(total_kernel, "totals", (got,), [(got.shape, jnp.bfloat16)])[0]


def assemble_kernel(pieces, blocks, place_ref, *refs):
    sources = refs[: len(pieces)]
    fc_ref, class_ref, fc_rows, class_rows, over_rows, sems = refs[-6:]
    inputs, width = fc_ref.shape
    rows, groups, main = block_sizes(inputs, width, blocks)
    each = (inputs - main) // 2
    base = groups * rows
    some = blocks // 2
    copies = []
    done = 0

    def send(source, target, at, size):
        copies.append(
            pltpu.make_async_copy(
                source, target.at[pl.ds(pl.multiple_of(at, 8), size), :], sems.at[len(copies)]
            )
        )
        copies[-1].start()

    for number, (piece, source) in enumerate(zip(pieces, sources)):
        half, parity = half_of(place_ref, piece[0]), parity_of(place_ref, piece[1])
        count = source.shape[0]
        block = (2 * half + parity) * some
        for at in range(0, count, count // 2):
            fc_here = slice((done + at) * rows, (done + at + count // 2) * rows)
            for group in range(groups):
                values = source[
                    at : at + count // 2, group * rows : (group + 1) * rows, :
                ].astype(jnp.float32)
                fc_rows[fc_here, group * LANES : (group + 1) * LANES] = values.reshape(
                    count // 2 * rows, LANES
                ).astype(jnp.bfloat16)
            send(fc_rows.at[fc_here, :], fc_ref, (block + at) * rows, count // 2 * rows)
        class_here = slice(done * 8, (done + count) * 8)
        for group in range(groups):
            lanes = slice(group * LANES, (group + 1) * LANES)
            values = source[:, base + group * 8 : base + (group + 1) * 8, :].astype(jnp.float32)
            class_rows[class_here, lanes] = values.reshape(count * 8, LANES).astype(jnp.bfloat16)
            over_rows[number, :, lanes] = source[group, base + groups * 8 :, :]
        send(class_rows.at[class_here, :], class_ref, block * 8, count * 8)
        send(over_rows.at[number], fc_ref, main + half * each + parity * 8, 8)
        done += count
    for copy in copies:
        copy.wait()


def assemble(place, blocks, sizes, pieces, into):
    inputs, classes, width = sizes
    rows, _, _ = block_sizes(inputs, width, blocks)
    total = sum(source.shape[0] for source in pieces.values())
    anywhere = pl.BlockSpec(memory_space=pltpu.HBM)
    return pl.pallas_call(
        functools.partial(assemble_kernel, tuple(pieces), blocks),
        in_specs=[SMEM] + [VMEM] * len(pieces) + [anywhere] * len(into),
        out_specs=[anywhere, anywhere],
        out_shape=[
            jax.ShapeDtypeStruct((inputs, width), jnp.bfloat16),
            jax.ShapeDtypeStruct((classes, width), jnp.bfloat16),
        ],
        scratch_shapes=[
            pltpu.VMEM((total * rows, width), jnp.bfloat16),
            pltpu.VMEM((total * 8, width), jnp.bfloat16),
            pltpu.VMEM((len(pieces), 8, width), jnp.bfloat16),
            pltpu.SemaphoreType.DMA((4 * len(pieces),)),
        ],
        input_output_aliases={1 + len(pieces) + at: at for at in range(len(into))},
        cost_estimate=pl.CostEstimate(
            flops=0, transcendentals=0, bytes_accessed=total * (rows + 8) * width * 8
        ),
        compiler_params=pltpu.CompilerParams(vmem_limit_bytes=LIMIT),
        name="assemble",
    )(place, *[placed(source) for source in pieces.values()], *into)


def shards(features, fc_weight, class_weight, labels):
    faces, inputs = features.shape
    features = features.T
    classes, width = class_weight.shape
    n_cls = lax.axis_size(CLS)
    chips = lax.axis_size(CHIPS)
    blocks = 2 * chips
    loss_weight = 1.0 / math.sqrt(faces * blocks * lax.axis_size("core"))
    place = (lax.axis_index(CLS) * 2 + lax.axis_index("zl")) * 2 + lax.axis_index("core")
    place = place.reshape(1)
    labels = labels.reshape(1, faces)

    sent, class_unit = embed(place, features, fc_weight, class_weight, labels)
    got = exchange(sent, CLS).reshape(n_cls, faces // n_cls, 2 * width)
    raw_embed, target_unit, sent = unit_rows(got)
    units = exchange(sent, CLS)
    units = units.reshape(faces, width)

    pull, others = cosines(place, units, class_unit, labels, n_cls)
    got = exchange(pull, CLS)
    sent, scales = raw_grads(loss_weight, place, got, raw_embed, target_unit)
    grads = exchange(sent, CLS).reshape(faces, width)

    swap = [(0, 1), (1, 0)]
    length = 2 * lax.axis_size("zh")
    pairs = []
    for z in range(length):
        pairs.append((2 * z, 2 * (z ^ 1)))
        pairs.append((2 * z + 1, 2 * ((z + 2 * (z % 2) - 1) % length) + 1))
    neighbour = ("zh", "zl", "core")

    operands = (blocks, features, grads, scales, units, others, class_weight)
    theirs = parts((True, True), place, jnp.bfloat16, *operands)
    theirs = lax.ppermute(theirs, "core", swap)
    sent = parts((False, True), place, jnp.float32, *operands) + theirs.astype(jnp.float32)
    sent, later = lax.optimization_barrier((sent.astype(jnp.bfloat16), place))
    got = lax.ppermute(sent, neighbour, pairs)
    theirs = parts((True, False), later, jnp.bfloat16, *operands)
    theirs = lax.ppermute(theirs, "core", swap)
    mine = parts((False, False), later, jnp.float32, *operands) + got.astype(jnp.float32)
    mine = lax.optimization_barrier(mine)
    mine = (mine + theirs.astype(jnp.float32)).astype(jnp.bfloat16)
    sizes = (inputs, classes, width)
    mine = exchange(totals(exchange(mine, CHIPS)), CHIPS)
    crossed = []
    for z in range(length):
        crossed.append((2 * z, 2 * ((z + 2 * (z % 2) - 1) % length) + 1))
        crossed.append((2 * z + 1, 2 * (z ^ 1)))
    next_mine = lax.ppermute(mine, neighbour, pairs)
    next_across = lax.ppermute(mine, neighbour, crossed)
    across_mine = lax.ppermute(mine, "core", swap)
    written = assemble(place, blocks, sizes, {(False, False): mine}, ())
    pieces = {(False, True): next_mine, (True, False): across_mine}
    written = assemble(place, blocks, sizes, pieces, written)
    return tuple(assemble(place, blocks, sizes, {(True, True): next_across}, written))


def solution(mesh):
    fine = Mesh(mesh.devices.reshape(4, 2, 4, 2, 4, 2), ("zh", "zl", "yh", "core", "x", "yl"))
    dp = ("zh", "zl", "yh", "core")
    specs = (P(dp, CLS), P(CLS, None), P(CLS, None), P(dp))
    return jax.shard_map(
        shards,
        mesh=fine,
        in_specs=specs,
        out_specs=(P(CLS, None), P(CLS, None)),
        check_vma=False,
    )
```

```python
import functools
import math

import jax
import jax.numpy as jnp
from jax import lax
from jax.experimental import pallas as pl
from jax.experimental.pallas import tpu as pltpu
from jax.sharding import Mesh
from jax.sharding import PartitionSpec as P

SCALE = 64.0
MARGIN = 0.5
SOFTEN = 0.01
EPSILON = 1e-06

CLS = ("x", "yl")
CHIPS = ("ya", "za", "yb", "zb")
LANES = 128
CHUNKS = 2
MARK = 1024.0
STEP = 512
LIMIT = 24 << 20
VMEM = pl.BlockSpec(memory_space=pltpu.VMEM)
SMEM = pl.BlockSpec(memory_space=pltpu.SMEM)


def exchange(blocks, axes):
    return lax.all_to_all(blocks, axes, 0, 0, tiled=True)


def across(left, right):
    return lax.dot_general(
        left, right, (((0,), (0,)), ((), ())), preferred_element_type=jnp.float32
    )


def row_norm(values):
    return jnp.sqrt(jnp.sum(values * values, axis=1, keepdims=True) + EPSILON)


def packed_columns(*columns):
    rows = columns[0].shape[0]
    lane = lax.broadcasted_iota(jnp.int32, (rows, LANES), 1)
    block = jnp.zeros((rows, LANES), jnp.float32)
    for at, column in enumerate(columns):
        rest = column
        for part in range(3):
            term = rest.astype(jnp.bfloat16).astype(jnp.float32)
            block = jnp.where(lane == 3 * at + part, term, block)
            rest = rest - term
    return block


def unpacked_column(block, at):
    lane = lax.broadcasted_iota(jnp.int32, block.shape, 1)
    inside = (lane >= 3 * at) & (lane < 3 * at + 3)
    return jnp.sum(jnp.where(inside, block, 0.0), axis=1, keepdims=True)


def placed(array, space=pltpu.VMEM):
    return pltpu.with_memory_space_constraint(array, space)


def half_of(place_ref, other):
    core = lax.rem(place_ref[0], 2)
    return 1 - core if other else core


def parity_of(place_ref, other):
    odd = lax.rem(lax.div(place_ref[0], 2), 2)
    return 1 - odd if other else odd


def first_of(place_ref, classes):
    return lax.div(place_ref[0], 4) * classes


def call(kernel, name, operands, results, **options):
    specs = [SMEM if operand.ndim == 1 else VMEM for operand in operands]
    operands = [operand if operand.ndim == 1 else placed(operand) for operand in operands]
    return pl.pallas_call(
        kernel,
        in_specs=specs,
        out_specs=[VMEM] * len(results),
        out_shape=[pltpu.VMEM(shape, dtype) for shape, dtype in results],
        compiler_params=pltpu.CompilerParams(vmem_limit_bytes=LIMIT),
        name=name,
        **options,
    )(*operands)


def target_mask(first, labels, rows, classes):
    lane = lax.broadcasted_iota(jnp.int32, (rows, LANES), 1)
    return jnp.concatenate(
        [labels == lane + (first + at) for at in range(0, classes, LANES)], axis=1
    )


def spread_labels(labels_row):
    faces = labels_row.shape[1]
    return jnp.transpose(jnp.broadcast_to(labels_row, (LANES, faces)))


def embed_kernel(
    place_ref, features_ref, fc_ref, class_ref, labels_ref, sent_ref, unit_ref,
    left_ref, right_ref, total_ref, weight_ref, row_ref, sems
):
    width = fc_ref.shape[1]
    inputs, faces = features_ref.shape
    classes = class_ref.shape[0]
    ends = [inputs * at // CHUNKS // LANES * LANES for at in range(CHUNKS)] + [inputs]
    copies = [
        pltpu.make_async_copy(labels_ref, row_ref, sems.at[0]),
        pltpu.make_async_copy(class_ref, weight_ref, sems.at[1]),
    ]
    for at in range(CHUNKS):
        rows = pl.ds(ends[at], ends[at + 1] - ends[at])
        for source, target in ((features_ref, left_ref), (fc_ref, right_ref)):
            copies.append(
                pltpu.make_async_copy(
                    source.at[rows, :], target.at[rows, :], sems.at[len(copies)]
                )
            )
    for copy in copies:
        copy.start()

    copies[0].wait()
    labels = spread_labels(row_ref[...])
    chosen = target_mask(first_of(place_ref, classes), labels, faces, classes)
    chosen = jnp.where(chosen, 1.0, 0.0).astype(jnp.bfloat16)
    copies[1].wait()
    class_f = weight_ref[...].astype(jnp.float32)
    unit_ref[...] = (class_f * (1.0 / row_norm(class_f))).astype(jnp.bfloat16)
    target_part = jnp.dot(chosen, unit_ref[...], preferred_element_type=jnp.float32)
    sent_ref[:, width:] = target_part.astype(jnp.bfloat16)

    for at in range(CHUNKS):
        copies[2 + 2 * at].wait()
        copies[3 + 2 * at].wait()
        here = slice(ends[at], ends[at + 1])
        part = across(left_ref[here, :], right_ref[here, :])
        if at > 0:
            part = part + total_ref[...]
        if at < CHUNKS - 1:
            total_ref[...] = part
        else:
            sent_ref[:, :width] = part.astype(jnp.bfloat16)


def embed(place, features, fc_weight, class_weight, labels):
    inputs, faces = features.shape
    classes, width = class_weight.shape
    arrays = [placed(array, pltpu.HBM) for array in (features, fc_weight, class_weight, labels)]
    return pl.pallas_call(
        embed_kernel,
        in_specs=[SMEM] + [pl.BlockSpec(memory_space=pltpu.HBM)] * len(arrays),
        out_specs=[VMEM, VMEM],
        out_shape=[
            pltpu.VMEM((faces, 2 * width), jnp.bfloat16),
            pltpu.VMEM((classes, width), jnp.bfloat16),
        ],
        scratch_shapes=[
            pltpu.VMEM((inputs, faces), jnp.bfloat16),
            pltpu.VMEM((inputs, width), jnp.bfloat16),
            pltpu.VMEM((faces, width), jnp.float32),
            pltpu.VMEM((classes, width), jnp.bfloat16),
            pltpu.VMEM((1, faces), jnp.int32),
            pltpu.SemaphoreType.DMA((2 + 2 * CHUNKS,)),
        ],
        compiler_params=pltpu.CompilerParams(vmem_limit_bytes=LIMIT),
        name="embed",
    )(place, *arrays)


def units_kernel(got_ref, raw_ref, target_ref, sent_ref):
    width = raw_ref.shape[1]
    got = got_ref[0].astype(jnp.float32)
    for peer in range(1, got_ref.shape[0]):
        got = got + got_ref[peer].astype(jnp.float32)
    raw_embed = got[:, :width]
    raw_ref[...] = raw_embed
    target_ref[...] = got[:, width:]
    unit = (raw_embed * (1.0 / row_norm(raw_embed))).astype(jnp.bfloat16)
    for copy in range(sent_ref.shape[0]):
        sent_ref[copy] = unit


def unit_rows(got):
    peers, owned, both = got.shape
    rows = (owned, both // 2)
    return call(
        units_kernel,
        "units",
        (got,),
        [(rows, jnp.float32), (rows, jnp.float32), ((peers,) + rows, jnp.bfloat16)],
    )


def target_terms(cosine):
    sine = jnp.sqrt(1.0 + SOFTEN - cosine * cosine)
    logit = SCALE * (cosine * math.cos(MARGIN) - sine * math.sin(MARGIN))
    slope = SCALE * (math.cos(MARGIN) + math.sin(MARGIN) * cosine / sine)
    return logit, slope


def cosine_kernel(place_ref, units_ref, class_ref, labels_ref, pull_ref, others_ref):
    faces, width = units_ref.shape
    classes = class_ref.shape[0]
    peers = pull_ref.shape[0]
    owned = faces // peers
    step = STEP
    first = first_of(place_ref, classes)
    labels = spread_labels(labels_ref[...])
    for at in range(0, faces, step):
        here = slice(at, at + step)
        cosine = lax.dot_general(
            units_ref[here, :],
            class_ref[...],
            (((1,), (1,)), ((), ())),
            preferred_element_type=jnp.float32,
        )
        label = labels[here, :]
        is_target = target_mask(first, label, step, classes)
        powers = jnp.exp(SCALE * cosine)
        others = jnp.where(is_target, 0.0, powers)
        pull = jnp.dot(
            others.astype(jnp.bfloat16), class_ref[...], preferred_element_type=jnp.float32
        )
        pull_ref[at // owned : (at + step) // owned, :owned, :] = pull.astype(
            jnp.bfloat16
        ).reshape(step // owned, owned, width)
        cos_t = jnp.sum(jnp.where(is_target, cosine, 0.0), axis=1, keepdims=True)
        logit, slope = target_terms(cos_t)
        others_ref[here, :] = jnp.where(is_target, -(slope + MARK), powers)
        mine = ((label >= first) & (label < first + classes))[:, :1]
        power_t = jnp.where(mine, jnp.exp(logit), 0.0)
        sums = packed_columns(jnp.sum(others, axis=1, keepdims=True), power_t)
        sums = jnp.transpose(sums)[:8].astype(jnp.bfloat16)
        for peer in range(peers):
            pull_ref[peer, owned:, here] = sums


def cosines(place, units, class_unit, labels, peers):
    faces, width = units.shape
    classes = class_unit.shape[0]
    return call(
        cosine_kernel,
        "cosines",
        (place, units, class_unit, labels),
        [
            ((peers, faces // peers + 8, width), jnp.bfloat16),
            ((faces, classes), jnp.float32),
        ],
    )


def raw_grad_kernel(
    loss_weight, place_ref, pulls_ref, raw_ref, target_ref, sent_ref, scales_ref
):
    owned, width = raw_ref.shape
    pulls = pulls_ref[0].astype(jnp.float32)
    for peer in range(1, pulls_ref.shape[0]):
        pulls = pulls + pulls_ref[peer].astype(jnp.float32)
    sums = jnp.concatenate([pulls[owned:], jnp.zeros((LANES - 8, width), jnp.float32)], axis=0)
    sums = jnp.transpose(sums)
    rest, power_t = unpacked_column(sums, 0), unpacked_column(sums, 1)
    inverse = loss_weight / (rest + power_t)
    lane = lax.broadcasted_iota(jnp.int32, sums.shape, 1)
    scales_ref[...] = jnp.where(lane == 0, SCALE * inverse, rest * inverse)
    own = pl.ds(pl.multiple_of(lax.div(place_ref[0], 4) * owned, owned), owned)
    scales = scales_ref[own, :]
    pull_scale, rest_scale = scales[:, 0:1], scales[:, 1:2]

    raw_embed, target = raw_ref[...], target_ref[...]
    inverse_norm = 1.0 / row_norm(raw_embed)
    unit_f = raw_embed * inverse_norm
    unit = unit_f.astype(jnp.bfloat16).astype(jnp.float32)
    _, slope = target_terms(jnp.sum(unit * target, axis=1, keepdims=True))
    unit_grad = pulls[:owned] * pull_scale - target * (rest_scale * slope)
    raw_grad = (
        unit_grad - unit_f * jnp.sum(unit_f * unit_grad, axis=1, keepdims=True)
    ) * inverse_norm
    raw_grad = raw_grad.astype(jnp.bfloat16)
    for copy in range(sent_ref.shape[0]):
        sent_ref[copy] = raw_grad


def raw_grads(loss_weight, place, pulls, raw_embed, target_unit):
    peers = pulls.shape[0]
    owned, width = raw_embed.shape
    return call(
        functools.partial(raw_grad_kernel, loss_weight),
        "raw_grads",
        (place, pulls, raw_embed, target_unit),
        [((peers, owned, width), jnp.bfloat16), ((peers * owned, LANES), jnp.float32)],
    )


def block_sizes(inputs, width, blocks):
    rows = inputs // (2 * blocks * 8) * 8
    return rows, width // LANES, 2 * blocks * rows


def parts_kernel(
    other_half, other_parity,
    place_ref, features_ref, grads_ref, scales_ref, units_ref, others_ref, class_ref, out_ref
):
    some = out_ref.shape[0]
    classes, width = class_ref.shape
    inputs = features_ref.shape[0]
    rows, groups, main = block_sizes(inputs, width, 2 * some)
    base = groups * rows
    half, parity = half_of(place_ref, other_half), parity_of(place_ref, other_parity)
    quarter = 2 * half + parity
    grads = grads_ref[...]

    first = pl.multiple_of(quarter * (some * rows), LANES)
    part = jnp.dot(
        features_ref[pl.ds(first, some * rows), :], grads, preferred_element_type=jnp.float32
    )
    part = part.astype(out_ref.dtype).reshape(some, rows, width)
    for group in range(groups):
        out_ref[:, group * rows : (group + 1) * rows, :] = part[
            :, :, group * LANES : (group + 1) * LANES
        ]

    scales = scales_ref[...]
    pull_scale, rest_scale = scales[:, 0:1], scales[:, 1:2]
    count = classes // 4
    first = pl.multiple_of(quarter * count, LANES)
    others = others_ref[:, pl.ds(first, count)]
    cos_grad = jnp.where(others < 0.0, (others + MARK) * rest_scale, others * pull_scale)
    part = across(cos_grad.astype(jnp.bfloat16), units_ref[...])
    class_f = class_ref[pl.ds(first, count), :].astype(jnp.float32)
    inverse = 1.0 / row_norm(class_f)
    along = jnp.sum(class_f * part, axis=1, keepdims=True) * (inverse * inverse)
    part = ((part - class_f * along) * inverse).astype(out_ref.dtype).reshape(some, 8, width)
    for group in range(groups):
        out_ref[:, base + group * 8 : base + (group + 1) * 8, :] = part[
            :, :, group * LANES : (group + 1) * LANES
        ]

    each = (inputs - main) // 2
    over = jnp.dot(
        features_ref[pl.ds(pl.multiple_of(main + half * each, each), each), :],
        grads,
        preferred_element_type=jnp.float32,
    ).astype(out_ref.dtype)
    strip = jnp.where(parity == 0, over[:8], over[8:])
    for group in range(groups):
        out_ref[group, base + groups * 8 :, :] = strip[:, group * LANES : (group + 1) * LANES]
    out_ref[groups:, base + groups * 8 :, :] = jnp.zeros((some - groups, 8, LANES), out_ref.dtype)


def parts(quarter, place, dtype, blocks, features, grads, scales, units, others, class_weight):
    width = class_weight.shape[1]
    rows, groups, _ = block_sizes(features.shape[0], width, blocks)
    return call(
        functools.partial(parts_kernel, *quarter),
        "parts",
        (place, features, grads, scales, units, others, class_weight),
        [((blocks // 2, groups * (rows + 8) + 8, LANES), dtype)],
    )[0]


def total_kernel(got_ref, sent_ref):
    total = got_ref[0].astype(jnp.float32)
    for peer in range(1, got_ref.shape[0]):
        total = total + got_ref[peer].astype(jnp.float32)
    total = total.astype(jnp.bfloat16)
    for copy in range(sent_ref.shape[0]):
        sent_ref[copy] = total


def totals(got):
    return call(total_kernel, "totals", (got,), [(got.shape, jnp.bfloat16)])[0]


def assemble_kernel(pieces, blocks, place_ref, *refs):
    sources = refs[: len(pieces)]
    fc_ref, class_ref, fc_rows, class_rows, over_rows, sems = refs[-6:]
    inputs, width = fc_ref.shape
    rows, groups, main = block_sizes(inputs, width, blocks)
    each = (inputs - main) // 2
    base = groups * rows
    some = blocks // 2
    copies = []
    done = 0

    def send(source, target, at, size):
        copies.append(
            pltpu.make_async_copy(
                source, target.at[pl.ds(pl.multiple_of(at, 8), size), :], sems.at[len(copies)]
            )
        )
        copies[-1].start()

    for number, (piece, source) in enumerate(zip(pieces, sources)):
        half, parity = half_of(place_ref, piece[0]), parity_of(place_ref, piece[1])
        count = source.shape[0]
        block = (2 * half + parity) * some
        for at in range(0, count, count // 2):
            fc_here = slice((done + at) * rows, (done + at + count // 2) * rows)
            for group in range(groups):
                values = source[
                    at : at + count // 2, group * rows : (group + 1) * rows, :
                ].astype(jnp.float32)
                fc_rows[fc_here, group * LANES : (group + 1) * LANES] = values.reshape(
                    count // 2 * rows, LANES
                ).astype(jnp.bfloat16)
            send(fc_rows.at[fc_here, :], fc_ref, (block + at) * rows, count // 2 * rows)
        class_here = slice(done * 8, (done + count) * 8)
        for group in range(groups):
            lanes = slice(group * LANES, (group + 1) * LANES)
            values = source[:, base + group * 8 : base + (group + 1) * 8, :].astype(jnp.float32)
            class_rows[class_here, lanes] = values.reshape(count * 8, LANES).astype(jnp.bfloat16)
            over_rows[number, :, lanes] = source[group, base + groups * 8 :, :]
        send(class_rows.at[class_here, :], class_ref, block * 8, count * 8)
        send(over_rows.at[number], fc_ref, main + half * each + parity * 8, 8)
        done += count
    for copy in copies:
        copy.wait()


def assemble(place, blocks, sizes, pieces, into):
    inputs, classes, width = sizes
    rows, _, _ = block_sizes(inputs, width, blocks)
    total = sum(source.shape[0] for source in pieces.values())
    anywhere = pl.BlockSpec(memory_space=pltpu.HBM)
    return pl.pallas_call(
        functools.partial(assemble_kernel, tuple(pieces), blocks),
        in_specs=[SMEM] + [VMEM] * len(pieces) + [anywhere] * len(into),
        out_specs=[anywhere, anywhere],
        out_shape=[
            jax.ShapeDtypeStruct((inputs, width), jnp.bfloat16),
            jax.ShapeDtypeStruct((classes, width), jnp.bfloat16),
        ],
        scratch_shapes=[
            pltpu.VMEM((total * rows, width), jnp.bfloat16),
            pltpu.VMEM((total * 8, width), jnp.bfloat16),
            pltpu.VMEM((len(pieces), 8, width), jnp.bfloat16),
            pltpu.SemaphoreType.DMA((4 * len(pieces),)),
        ],
        input_output_aliases={1 + len(pieces) + at: at for at in range(len(into))},
        cost_estimate=pl.CostEstimate(
            flops=0, transcendentals=0, bytes_accessed=total * (rows + 8) * width * 8
        ),
        compiler_params=pltpu.CompilerParams(vmem_limit_bytes=LIMIT),
        name="assemble",
    )(place, *[placed(source) for source in pieces.values()], *into)


def shards(features, fc_weight, class_weight, labels):
    faces, inputs = features.shape
    features = features.T
    classes, width = class_weight.shape
    n_cls = lax.axis_size(CLS)
    chips = lax.axis_size(CHIPS)
    blocks = 2 * chips
    loss_weight = 1.0 / math.sqrt(faces * blocks * lax.axis_size("core"))
    place = (lax.axis_index(CLS) * 2 + lax.axis_index("zl")) * 2 + lax.axis_index("core")
    place = place.reshape(1)
    labels = labels.reshape(1, faces)

    sent, class_unit = embed(place, features, fc_weight, class_weight, labels)
    got = exchange(sent, CLS).reshape(n_cls, faces // n_cls, 2 * width)
    raw_embed, target_unit, sent = unit_rows(got)
    units = exchange(sent, CLS)
    units = units.reshape(faces, width)

    pull, others = cosines(place, units, class_unit, labels, n_cls)
    got = exchange(pull, CLS)
    sent, scales = raw_grads(loss_weight, place, got, raw_embed, target_unit)
    grads = exchange(sent, CLS).reshape(faces, width)

    swap = [(0, 1), (1, 0)]
    neighbour = ("za", "zb", "zl", "core")
    length = lax.axis_size(neighbour) // 2
    pairs = []
    for z in range(length):
        pairs.append((2 * z, 2 * (z ^ 1)))
        pairs.append((2 * z + 1, 2 * ((z + 2 * (z % 2) - 1) % length) + 1))

    operands = (blocks, features, grads, scales, units, others, class_weight)
    theirs = parts((True, True), place, jnp.bfloat16, *operands)
    theirs = lax.ppermute(theirs, "core", swap)
    sent = parts((False, True), place, jnp.float32, *operands) + theirs.astype(jnp.float32)
    sent, later = lax.optimization_barrier((sent.astype(jnp.bfloat16), place))
    got = lax.ppermute(sent, neighbour, pairs)
    theirs = parts((True, False), later, jnp.bfloat16, *operands)
    theirs = lax.ppermute(theirs, "core", swap)
    mine = parts((False, False), later, jnp.float32, *operands) + got.astype(jnp.float32)
    mine = lax.optimization_barrier(mine)
    mine = (mine + theirs.astype(jnp.float32)).astype(jnp.bfloat16)
    sizes = (inputs, classes, width)
    mine = exchange(totals(exchange(mine, CHIPS)), CHIPS)
    next_mine = lax.ppermute(mine, neighbour, pairs)
    across_mine = lax.ppermute(mine, "core", swap)
    written = assemble(place, blocks, sizes, {(False, False): mine}, ())
    next_mine, written = lax.optimization_barrier((next_mine, written))
    across_next = lax.ppermute(next_mine, "core", swap)
    pieces = {(False, True): next_mine, (True, False): across_mine}
    written = assemble(place, blocks, sizes, pieces, written)
    return tuple(assemble(place, blocks, sizes, {(True, True): across_next}, written))


def solution(mesh):
    names = ("za", "zb", "zl", "ya", "yb", "core", "x", "yl")
    fine = Mesh(mesh.devices.reshape(2, 2, 2, 2, 2, 2, 4, 2), names)
    dp = names[:6]
    specs = (P(dp, CLS), P(CLS, None), P(CLS, None), P(dp))
    return jax.shard_map(
        shards,
        mesh=fine,
        in_specs=specs,
        out_specs=(P(CLS, None), P(CLS, None)),
        check_vma=False,
    )
```

```python
import functools
import math

import jax
import jax.numpy as jnp
from jax import lax
from jax.experimental import pallas as pl
from jax.experimental.pallas import tpu as pltpu
from jax.sharding import Mesh
from jax.sharding import PartitionSpec as P

SCALE = 64.0
MARGIN = 0.5
SOFTEN = 0.01
EPSILON = 1e-06

CLS = ("x", "yl")
CHIPS = ("zh", "yh")
LANES = 128
CHUNKS = 2
MARK = 1024.0
STEP = 512
LIMIT = 24 << 20
VMEM = pl.BlockSpec(memory_space=pltpu.VMEM)
SMEM = pl.BlockSpec(memory_space=pltpu.SMEM)


def exchange(blocks, axes):
    return lax.all_to_all(blocks, axes, 0, 0, tiled=True)


def across(left, right):
    return lax.dot_general(
        left, right, (((0,), (0,)), ((), ())), preferred_element_type=jnp.float32
    )


def row_norm(values):
    return jnp.sqrt(jnp.sum(values * values, axis=1, keepdims=True) + EPSILON)


def packed_columns(*columns):
    rows = columns[0].shape[0]
    lane = lax.broadcasted_iota(jnp.int32, (rows, LANES), 1)
    block = jnp.zeros((rows, LANES), jnp.float32)
    for at, column in enumerate(columns):
        rest = column
        for part in range(3):
            term = rest.astype(jnp.bfloat16).astype(jnp.float32)
            block = jnp.where(lane == 3 * at + part, term, block)
            rest = rest - term
    return block


def unpacked_column(block, at):
    lane = lax.broadcasted_iota(jnp.int32, block.shape, 1)
    inside = (lane >= 3 * at) & (lane < 3 * at + 3)
    return jnp.sum(jnp.where(inside, block, 0.0), axis=1, keepdims=True)


def placed(array, space=pltpu.VMEM):
    return pltpu.with_memory_space_constraint(array, space)


def half_of(place_ref, other):
    core = lax.rem(place_ref[0], 2)
    return 1 - core if other else core


def parity_of(place_ref, other):
    odd = lax.rem(lax.div(place_ref[0], 2), 2)
    return 1 - odd if other else odd


def first_of(place_ref, classes):
    return lax.div(place_ref[0], 4) * classes


def call(kernel, name, operands, results, **options):
    specs = [SMEM if operand.ndim == 1 else VMEM for operand in operands]
    operands = [operand if operand.ndim == 1 else placed(operand) for operand in operands]
    return pl.pallas_call(
        kernel,
        in_specs=specs,
        out_specs=[VMEM] * len(results),
        out_shape=[pltpu.VMEM(shape, dtype) for shape, dtype in results],
        compiler_params=pltpu.CompilerParams(vmem_limit_bytes=LIMIT),
        name=name,
        **options,
    )(*operands)


def target_mask(first, labels, rows, classes):
    lane = lax.broadcasted_iota(jnp.int32, (rows, LANES), 1)
    return jnp.concatenate(
        [labels == lane + (first + at) for at in range(0, classes, LANES)], axis=1
    )


def spread_labels(labels_row):
    faces = labels_row.shape[1]
    return jnp.transpose(jnp.broadcast_to(labels_row, (LANES, faces)))


def embed_kernel(
    place_ref, features_ref, fc_ref, class_ref, labels_ref, sent_ref, unit_ref,
    left_ref, right_ref, total_ref, weight_ref, row_ref, sems
):
    width = fc_ref.shape[1]
    inputs, faces = features_ref.shape
    classes = class_ref.shape[0]
    ends = [inputs * at // CHUNKS // LANES * LANES for at in range(CHUNKS)] + [inputs]
    copies = [
        pltpu.make_async_copy(labels_ref, row_ref, sems.at[0]),
        pltpu.make_async_copy(class_ref, weight_ref, sems.at[1]),
    ]
    for at in range(CHUNKS):
        rows = pl.ds(ends[at], ends[at + 1] - ends[at])
        for source, target in ((features_ref, left_ref), (fc_ref, right_ref)):
            copies.append(
                pltpu.make_async_copy(
                    source.at[rows, :], target.at[rows, :], sems.at[len(copies)]
                )
            )
    for copy in copies:
        copy.start()

    copies[0].wait()
    labels = spread_labels(row_ref[...])
    chosen = target_mask(first_of(place_ref, classes), labels, faces, classes)
    chosen = jnp.where(chosen, 1.0, 0.0).astype(jnp.bfloat16)
    copies[1].wait()
    class_f = weight_ref[...].astype(jnp.float32)
    unit_ref[...] = (class_f * (1.0 / row_norm(class_f))).astype(jnp.bfloat16)
    target_part = jnp.dot(chosen, unit_ref[...], preferred_element_type=jnp.float32)
    sent_ref[:, width:] = target_part.astype(jnp.bfloat16)

    for at in range(CHUNKS):
        copies[2 + 2 * at].wait()
        copies[3 + 2 * at].wait()
        here = slice(ends[at], ends[at + 1])
        part = across(left_ref[here, :], right_ref[here, :])
        if at > 0:
            part = part + total_ref[...]
        if at < CHUNKS - 1:
            total_ref[...] = part
        else:
            sent_ref[:, :width] = part.astype(jnp.bfloat16)


def embed(place, features, fc_weight, class_weight, labels):
    inputs, faces = features.shape
    classes, width = class_weight.shape
    arrays = [placed(array, pltpu.HBM) for array in (features, fc_weight, class_weight, labels)]
    return pl.pallas_call(
        embed_kernel,
        in_specs=[SMEM] + [pl.BlockSpec(memory_space=pltpu.HBM)] * len(arrays),
        out_specs=[VMEM, VMEM],
        out_shape=[
            pltpu.VMEM((faces, 2 * width), jnp.bfloat16),
            pltpu.VMEM((classes, width), jnp.bfloat16),
        ],
        scratch_shapes=[
            pltpu.VMEM((inputs, faces), jnp.bfloat16),
            pltpu.VMEM((inputs, width), jnp.bfloat16),
            pltpu.VMEM((faces, width), jnp.float32),
            pltpu.VMEM((classes, width), jnp.bfloat16),
            pltpu.VMEM((1, faces), jnp.int32),
            pltpu.SemaphoreType.DMA((2 + 2 * CHUNKS,)),
        ],
        compiler_params=pltpu.CompilerParams(vmem_limit_bytes=LIMIT),
        name="embed",
    )(place, *arrays)


def units_kernel(got_ref, raw_ref, target_ref, sent_ref):
    width = raw_ref.shape[1]
    got = got_ref[0].astype(jnp.float32)
    for peer in range(1, got_ref.shape[0]):
        got = got + got_ref[peer].astype(jnp.float32)
    raw_embed = got[:, :width]
    raw_ref[...] = raw_embed
    target_ref[...] = got[:, width:]
    unit = (raw_embed * (1.0 / row_norm(raw_embed))).astype(jnp.bfloat16)
    for copy in range(sent_ref.shape[0]):
        sent_ref[copy] = unit


def unit_rows(got):
    peers, owned, both = got.shape
    rows = (owned, both // 2)
    return call(
        units_kernel,
        "units",
        (got,),
        [(rows, jnp.float32), (rows, jnp.float32), ((peers,) + rows, jnp.bfloat16)],
    )


def target_terms(cosine):
    sine = jnp.sqrt(1.0 + SOFTEN - cosine * cosine)
    logit = SCALE * (cosine * math.cos(MARGIN) - sine * math.sin(MARGIN))
    slope = SCALE * (math.cos(MARGIN) + math.sin(MARGIN) * cosine / sine)
    return logit, slope


def cosine_kernel(place_ref, units_ref, class_ref, labels_ref, pull_ref, others_ref):
    faces, width = units_ref.shape
    classes = class_ref.shape[0]
    peers = pull_ref.shape[0]
    owned = faces // peers
    step = STEP
    first = first_of(place_ref, classes)
    labels = spread_labels(labels_ref[...])
    for at in range(0, faces, step):
        here = slice(at, at + step)
        cosine = lax.dot_general(
            units_ref[here, :],
            class_ref[...],
            (((1,), (1,)), ((), ())),
            preferred_element_type=jnp.float32,
        )
        label = labels[here, :]
        is_target = target_mask(first, label, step, classes)
        powers = jnp.exp(SCALE * cosine)
        others = jnp.where(is_target, 0.0, powers)
        pull = jnp.dot(
            others.astype(jnp.bfloat16), class_ref[...], preferred_element_type=jnp.float32
        )
        pull_ref[at // owned : (at + step) // owned, :owned, :] = pull.astype(
            jnp.bfloat16
        ).reshape(step // owned, owned, width)
        cos_t = jnp.sum(jnp.where(is_target, cosine, 0.0), axis=1, keepdims=True)
        logit, slope = target_terms(cos_t)
        others_ref[here, :] = jnp.where(is_target, -(slope + MARK), powers)
        mine = ((label >= first) & (label < first + classes))[:, :1]
        power_t = jnp.where(mine, jnp.exp(logit), 0.0)
        sums = packed_columns(jnp.sum(others, axis=1, keepdims=True), power_t)
        sums = jnp.transpose(sums)[:8].astype(jnp.bfloat16)
        for peer in range(peers):
            pull_ref[peer, owned:, here] = sums


def cosines(place, units, class_unit, labels, peers):
    faces, width = units.shape
    classes = class_unit.shape[0]
    return call(
        cosine_kernel,
        "cosines",
        (place, units, class_unit, labels),
        [
            ((peers, faces // peers + 8, width), jnp.bfloat16),
            ((faces, classes), jnp.float32),
        ],
    )


def raw_grad_kernel(
    loss_weight, place_ref, pulls_ref, raw_ref, target_ref, sent_ref, scales_ref
):
    owned, width = raw_ref.shape
    pulls = pulls_ref[0].astype(jnp.float32)
    for peer in range(1, pulls_ref.shape[0]):
        pulls = pulls + pulls_ref[peer].astype(jnp.float32)
    sums = jnp.concatenate([pulls[owned:], jnp.zeros((LANES - 8, width), jnp.float32)], axis=0)
    sums = jnp.transpose(sums)
    rest, power_t = unpacked_column(sums, 0), unpacked_column(sums, 1)
    inverse = loss_weight / (rest + power_t)
    lane = lax.broadcasted_iota(jnp.int32, sums.shape, 1)
    scales_ref[...] = jnp.where(lane == 0, SCALE * inverse, rest * inverse)
    own = pl.ds(pl.multiple_of(lax.div(place_ref[0], 4) * owned, owned), owned)
    scales = scales_ref[own, :]
    pull_scale, rest_scale = scales[:, 0:1], scales[:, 1:2]

    raw_embed, target = raw_ref[...], target_ref[...]
    inverse_norm = 1.0 / row_norm(raw_embed)
    unit_f = raw_embed * inverse_norm
    unit = unit_f.astype(jnp.bfloat16).astype(jnp.float32)
    _, slope = target_terms(jnp.sum(unit * target, axis=1, keepdims=True))
    unit_grad = pulls[:owned] * pull_scale - target * (rest_scale * slope)
    raw_grad = (
        unit_grad - unit_f * jnp.sum(unit_f * unit_grad, axis=1, keepdims=True)
    ) * inverse_norm
    raw_grad = raw_grad.astype(jnp.bfloat16)
    for copy in range(sent_ref.shape[0]):
        sent_ref[copy] = raw_grad


def raw_grads(loss_weight, place, pulls, raw_embed, target_unit):
    peers = pulls.shape[0]
    owned, width = raw_embed.shape
    return call(
        functools.partial(raw_grad_kernel, loss_weight),
        "raw_grads",
        (place, pulls, raw_embed, target_unit),
        [((peers, owned, width), jnp.bfloat16), ((peers * owned, LANES), jnp.float32)],
    )


def block_sizes(inputs, width, blocks):
    rows = inputs // (2 * blocks * 8) * 8
    return rows, width // LANES, 2 * blocks * rows


def parts_kernel(
    other_half, other_parity,
    place_ref, features_ref, grads_ref, scales_ref, units_ref, others_ref, class_ref, out_ref
):
    some = out_ref.shape[0]
    classes, width = class_ref.shape
    inputs = features_ref.shape[0]
    rows, groups, main = block_sizes(inputs, width, 2 * some)
    base = groups * rows
    half, parity = half_of(place_ref, other_half), parity_of(place_ref, other_parity)
    quarter = 2 * half + parity
    grads = grads_ref[...]

    each = (inputs - main) // 2
    first = pl.multiple_of(quarter * (some * rows), LANES)
    left = pl.multiple_of(main + half * each, each)
    faces = [features_ref[pl.ds(first, some * rows), :], features_ref[pl.ds(left, each), :]]
    both = jnp.dot(
        jnp.concatenate(faces, axis=0), grads, preferred_element_type=jnp.float32
    )
    part, over = both[: some * rows], both[some * rows :].astype(out_ref.dtype)
    part = part.astype(out_ref.dtype).reshape(some, rows, width)
    for group in range(groups):
        out_ref[:, group * rows : (group + 1) * rows, :] = part[
            :, :, group * LANES : (group + 1) * LANES
        ]

    scales = scales_ref[...]
    pull_scale, rest_scale = scales[:, 0:1], scales[:, 1:2]
    count = classes // 4
    first = pl.multiple_of(quarter * count, LANES)
    others = others_ref[:, pl.ds(first, count)]
    cos_grad = jnp.where(others < 0.0, (others + MARK) * rest_scale, others * pull_scale)
    part = across(cos_grad.astype(jnp.bfloat16), units_ref[...])
    class_f = class_ref[pl.ds(first, count), :].astype(jnp.float32)
    inverse = 1.0 / row_norm(class_f)
    along = jnp.sum(class_f * part, axis=1, keepdims=True) * (inverse * inverse)
    part = ((part - class_f * along) * inverse).astype(out_ref.dtype).reshape(some, 8, width)
    for group in range(groups):
        out_ref[:, base + group * 8 : base + (group + 1) * 8, :] = part[
            :, :, group * LANES : (group + 1) * LANES
        ]

    strip = jnp.where(parity == 0, over[:8], over[8:])
    for group in range(groups):
        out_ref[group, base + groups * 8 :, :] = strip[:, group * LANES : (group + 1) * LANES]
    out_ref[groups:, base + groups * 8 :, :] = jnp.zeros((some - groups, 8, LANES), out_ref.dtype)


def parts(quarter, place, dtype, blocks, features, grads, scales, units, others, class_weight):
    width = class_weight.shape[1]
    rows, groups, _ = block_sizes(features.shape[0], width, blocks)
    return call(
        functools.partial(parts_kernel, *quarter),
        "parts",
        (place, features, grads, scales, units, others, class_weight),
        [((blocks // 2, groups * (rows + 8) + 8, LANES), dtype)],
    )[0]


def total_kernel(got_ref, sent_ref):
    total = got_ref[0].astype(jnp.float32)
    for peer in range(1, got_ref.shape[0]):
        total = total + got_ref[peer].astype(jnp.float32)
    total = total.astype(jnp.bfloat16)
    for copy in range(sent_ref.shape[0]):
        sent_ref[copy] = total


def totals(got):
    return call(total_kernel, "totals", (got,), [(got.shape, jnp.bfloat16)])[0]


def assemble_kernel(pieces, blocks, place_ref, *refs):
    sources = refs[: len(pieces)]
    fc_ref, class_ref, fc_rows, class_rows, over_rows, sems = refs[-6:]
    inputs, width = fc_ref.shape
    rows, groups, main = block_sizes(inputs, width, blocks)
    each = (inputs - main) // 2
    base = groups * rows
    some = blocks // 2
    copies = []
    done = 0

    def send(source, target, at, size):
        copies.append(
            pltpu.make_async_copy(
                source, target.at[pl.ds(pl.multiple_of(at, 8), size), :], sems.at[len(copies)]
            )
        )
        copies[-1].start()

    for number, (piece, source) in enumerate(zip(pieces, sources)):
        half, parity = half_of(place_ref, piece[0]), parity_of(place_ref, piece[1])
        count = source.shape[0]
        block = (2 * half + parity) * some
        for at in range(0, count, count // 2):
            fc_here = slice((done + at) * rows, (done + at + count // 2) * rows)
            for group in range(groups):
                values = source[
                    at : at + count // 2, group * rows : (group + 1) * rows, :
                ].astype(jnp.float32)
                fc_rows[fc_here, group * LANES : (group + 1) * LANES] = values.reshape(
                    count // 2 * rows, LANES
                ).astype(jnp.bfloat16)
            send(fc_rows.at[fc_here, :], fc_ref, (block + at) * rows, count // 2 * rows)
        class_here = slice(done * 8, (done + count) * 8)
        for group in range(groups):
            lanes = slice(group * LANES, (group + 1) * LANES)
            values = source[:, base + group * 8 : base + (group + 1) * 8, :].astype(jnp.float32)
            class_rows[class_here, lanes] = values.reshape(count * 8, LANES).astype(jnp.bfloat16)
            over_rows[number, :, lanes] = source[group, base + groups * 8 :, :]
        send(class_rows.at[class_here, :], class_ref, block * 8, count * 8)
        send(over_rows.at[number], fc_ref, main + half * each + parity * 8, 8)
        done += count
    for copy in copies:
        copy.wait()


def assemble(place, blocks, sizes, pieces, into):
    inputs, classes, width = sizes
    rows, _, _ = block_sizes(inputs, width, blocks)
    total = sum(source.shape[0] for source in pieces.values())
    anywhere = pl.BlockSpec(memory_space=pltpu.HBM)
    return pl.pallas_call(
        functools.partial(assemble_kernel, tuple(pieces), blocks),
        in_specs=[SMEM] + [VMEM] * len(pieces) + [anywhere] * len(into),
        out_specs=[anywhere, anywhere],
        out_shape=[
            jax.ShapeDtypeStruct((inputs, width), jnp.bfloat16),
            jax.ShapeDtypeStruct((classes, width), jnp.bfloat16),
        ],
        scratch_shapes=[
            pltpu.VMEM((total * rows, width), jnp.bfloat16),
            pltpu.VMEM((total * 8, width), jnp.bfloat16),
            pltpu.VMEM((len(pieces), 8, width), jnp.bfloat16),
            pltpu.SemaphoreType.DMA((4 * len(pieces),)),
        ],
        input_output_aliases={1 + len(pieces) + at: at for at in range(len(into))},
        cost_estimate=pl.CostEstimate(
            flops=0, transcendentals=0, bytes_accessed=total * (rows + 8) * width * 8
        ),
        compiler_params=pltpu.CompilerParams(vmem_limit_bytes=LIMIT),
        name="assemble",
    )(place, *[placed(source) for source in pieces.values()], *into)


def shards(features, fc_weight, class_weight, labels):
    faces, inputs = features.shape
    features = features.T
    classes, width = class_weight.shape
    n_cls = lax.axis_size(CLS)
    chips = lax.axis_size(CHIPS)
    blocks = 2 * chips
    loss_weight = 1.0 / math.sqrt(faces * blocks * lax.axis_size("core"))
    place = (lax.axis_index(CLS) * 2 + lax.axis_index("zl")) * 2 + lax.axis_index("core")
    place = place.reshape(1)
    labels = labels.reshape(1, faces)

    sent, class_unit = embed(place, features, fc_weight, class_weight, labels)
    got = exchange(sent, CLS).reshape(n_cls, faces // n_cls, 2 * width)
    raw_embed, target_unit, sent = unit_rows(got)
    units = exchange(sent, CLS)
    units = units.reshape(faces, width)

    pull, others = cosines(place, units, class_unit, labels, n_cls)
    got = exchange(pull, CLS)
    sent, scales = raw_grads(loss_weight, place, got, raw_embed, target_unit)
    grads = exchange(sent, CLS).reshape(faces, width)

    swap = [(0, 1), (1, 0)]
    length = 2 * lax.axis_size("zh")
    pairs = []
    for z in range(length):
        pairs.append((2 * z, 2 * (z ^ 1)))
        pairs.append((2 * z + 1, 2 * ((z + 2 * (z % 2) - 1) % length) + 1))
    neighbour = ("zh", "zl", "core")

    operands = (blocks, features, grads, scales, units, others, class_weight)
    theirs = parts((True, True), place, jnp.bfloat16, *operands)
    theirs = lax.ppermute(theirs, "core", swap)
    sent = parts((False, True), place, jnp.float32, *operands) + theirs.astype(jnp.float32)
    sent, later = lax.optimization_barrier((sent.astype(jnp.bfloat16), place))
    got = lax.ppermute(sent, neighbour, pairs)
    theirs = parts((True, False), later, jnp.bfloat16, *operands)
    theirs = lax.ppermute(theirs, "core", swap)
    mine = parts((False, False), later, jnp.float32, *operands) + got.astype(jnp.float32)
    mine = lax.optimization_barrier(mine)
    mine = (mine + theirs.astype(jnp.float32)).astype(jnp.bfloat16)
    sizes = (inputs, classes, width)
    mine = exchange(totals(exchange(mine, CHIPS)), CHIPS)
    next_mine = lax.ppermute(mine, neighbour, pairs)
    across_mine = lax.ppermute(mine, "core", swap)
    written = assemble(place, blocks, sizes, {(False, False): mine}, ())
    next_mine, written = lax.optimization_barrier((next_mine, written))
    across_next = lax.ppermute(next_mine, "core", swap)
    pieces = {(False, True): next_mine, (True, False): across_mine}
    written = assemble(place, blocks, sizes, pieces, written)
    return tuple(assemble(place, blocks, sizes, {(True, True): across_next}, written))


def solution(mesh):
    fine = Mesh(mesh.devices.reshape(4, 2, 4, 2, 4, 2), ("zh", "zl", "yh", "core", "x", "yl"))
    dp = ("zh", "zl", "yh", "core")
    specs = (P(dp, CLS), P(CLS, None), P(CLS, None), P(dp))
    return jax.shard_map(
        shards,
        mesh=fine,
        in_specs=specs,
        out_specs=(P(CLS, None), P(CLS, None)),
        check_vma=False,
    )
```
